256 devices in a mesh: node: 16 (over z, core), dev: 16 (over x, y).
Axes of the slice: x: 4, y: 4, z: 8, core: 2. Of those that a mesh axis runs over, the one named last changes fastest.
Arguments:
- density: float32 [1536, 64, 4096], P(('node', 'dev')), may hold values from -18 to 18
- owner_counts: int32 [256], P(('node', 'dev')), may hold values from 1 to 6, as said below
Outputs:
- coefficients: float32 [1536, 64, 4096], P(('node', 'dev'))
The draws below stay inside these ranges and needn't reach their ends.
Inputs may be any that keep to these rules, and one draw needn't show every extreme that they name: `owner_counts`: every device holds at least one block, the counts sum to 768, and some device holds exactly 6.
All inputs are finite; a program needn't handle non-finite values.
Results may differ from the reference program's by a relative error of at most 0.00002.
Values sent between devices are 32-bit elements; how exact they have to be, the bound alone decides.
A program may use at most 128 MiB of HBM per device.

```python
import jax
import jax.numpy as jnp
from jax import lax

B = 64
BLK_DEV = 3
SLOTS = 6
NBLK = 768
Q = 16
M = 32
DEVICES = 256


def draw_density(key, part):
    rows_total = DEVICES * SLOTS
    shape_full = (rows_total, B, B, B)
    keys_all = jax.random.split(key, 8)
    summed = jax.random.truncated_normal(keys_all[0], -3.0, 3.0, shape_full, jnp.float32)
    for exponent in range(1, 6):
        cell_span = 2 ** exponent
        if cell_span <= B // 2:
            coarse_edge = B // cell_span
            coarse_shape = (rows_total, coarse_edge, 1, coarse_edge, 1, coarse_edge, 1)
            component = jax.random.truncated_normal(keys_all[exponent], -3.0, 3.0, coarse_shape, jnp.float32)
            wide_shape = (rows_total, coarse_edge, cell_span, coarse_edge, cell_span, coarse_edge, cell_span)
            summed = summed + jnp.broadcast_to(component, wide_shape).reshape(shape_full)
    return summed.reshape(rows_total, B, B * B)


def spread_even(total_sum, width):
    base_value = total_sum // width
    remainder = total_sum % width
    return (base_value + (jnp.arange(width, dtype=jnp.int32) < remainder).astype(jnp.int32)).astype(jnp.int32)


def draw_owner_counts(key, part):
    quad_total = DEVICES // 4
    per_device = BLK_DEV
    keys_all = jax.random.split(key, 8)
    pattern_kind = jax.random.randint(keys_all[0], (quad_total,), 0, 2)
    first_pick = jax.random.randint(keys_all[1], (quad_total,), 1, 2 * per_device - 1)
    room_left = 2 * per_device - 1 - first_pick
    second_pick = 1 + jax.random.randint(keys_all[2], (quad_total,), 0, 1 << 20) % room_left
    heavy_pattern = jnp.stack([jnp.full((quad_total,), 2 * per_device, jnp.int32), first_pick, second_pick, 2 * per_device - first_pick - second_pick], 1)
    spread_one = jax.random.randint(keys_all[3], (quad_total,), 1 - per_device, per_device)
    spread_two = jax.random.randint(keys_all[4], (quad_total,), 1 - per_device, per_device)
    even_pattern = jnp.stack([per_device + spread_one, per_device - spread_one, per_device + spread_two, per_device - spread_two], 1)
    chosen = jnp.where(pattern_kind[:, None] == 0, heavy_pattern, even_pattern)
    rotate_by = jax.random.randint(keys_all[5], (quad_total,), 0, 4)
    positions = (jnp.arange(4)[None, :] + rotate_by[:, None]) % 4
    counts = jnp.take_along_axis(chosen, positions, axis=1).reshape(DEVICES).astype(jnp.int32)
    window_start = DEVICES // 2 - 16
    prefix_sum = jnp.sum(counts[:window_start]).astype(jnp.int32)
    fill_total = 32 * per_device - 8
    extra_room = fill_total - 2 * per_device - 19 - 11
    base_head = 2 * per_device + 19 + extra_room * 12 // 23
    head_total = (base_head - (base_head + prefix_sum) % 8).astype(jnp.int32)
    head_rest = jnp.roll(spread_even(head_total - 2 * per_device, 12), jax.random.randint(keys_all[6], (), 0, 12))
    tail_fill = jnp.roll(spread_even(fill_total - head_total, 11), jax.random.randint(keys_all[7], (), 0, 11))
    singles = jnp.ones((8,), jnp.int32)
    window = jnp.concatenate([jnp.full((1,), 2 * per_device, jnp.int32), head_rest, singles, tail_fill]).astype(jnp.int32)
    counts = lax.dynamic_update_slice(counts, window, (window_start,))
    return counts.astype(jnp.int32)


def setup_inputs(seed: int = 0) -> dict:
    key_list = jax.random.split(jax.random.key(seed), 3)
    return {
        "density": draw_density(jax.random.fold_in(key_list[2], 71), 0),
        "owner_counts": draw_owner_counts(jax.random.fold_in(key_list[2], 71), 0),
    }


ALPHA_LIFT = -1.586134342059924
BETA_LIFT = -0.052980118572961
GAMMA_LIFT = 0.882911075530934
DELTA_LIFT = 0.443506852043971
SCALE_LIFT = 1.230174104914001
INVERSE_SCALE = 1.0 / SCALE_LIFT


def lift_front(values):
    length = values.shape[0]
    paired = values.reshape((length // 2, 2) + values.shape[1:])
    low_part = paired[:, 0]
    high_part = paired[:, 1]
    high_part = high_part + ALPHA_LIFT * (low_part + jnp.concatenate([low_part[1:], low_part[-1:]], 0))
    low_part = low_part + BETA_LIFT * (jnp.concatenate([high_part[:1], high_part[:-1]], 0) + high_part)
    high_part = high_part + GAMMA_LIFT * (low_part + jnp.concatenate([low_part[1:], low_part[-1:]], 0))
    low_part = low_part + DELTA_LIFT * (jnp.concatenate([high_part[:1], high_part[:-1]], 0) + high_part)
    return jnp.concatenate([low_part * INVERSE_SCALE, high_part * SCALE_LIFT], 0)


def one_level(volume):
    for axis_number in range(3):
        volume = jnp.moveaxis(lift_front(jnp.moveaxis(volume, axis_number, 0)), 0, axis_number)
    return volume


def corner_level(volume, corner_edge):
    inner = one_level(volume[:corner_edge, :corner_edge, :corner_edge])
    return volume.at[:corner_edge, :corner_edge, :corner_edge].set(inner)


def fine_levels(block_cube):
    return corner_level(one_level(block_cube), B // 2)


def coarse_levels(merged):
    return corner_level(corner_level(one_level(merged), M // 2), M // 4)


def assemble(pieces):
    return jnp.transpose(pieces.reshape(2, 2, 2, Q, Q, Q), (2, 3, 1, 4, 0, 5)).reshape(M, M, M)


def split_octet(merged):
    return jnp.transpose(merged.reshape(2, Q, 2, Q, 2, Q), (4, 2, 0, 1, 3, 5)).reshape(8, Q, Q, Q)


def reference(density, owner_counts):
    counts = owner_counts.astype(jnp.int32)
    starts = (jnp.cumsum(counts) - counts).astype(jnp.int32)
    blocks = density.reshape(DEVICES * SLOTS, B, B, B)
    lowpass = lax.map(lambda block_cube: fine_levels(block_cube)[:Q, :Q, :Q], blocks)
    block_ids = jnp.arange(NBLK, dtype=jnp.int32)
    owners = (jnp.sum((starts[None, :] <= block_ids[:, None]).astype(jnp.int32), axis=1) - 1).astype(jnp.int32)
    row_index = (owners * SLOTS + block_ids - starts[owners]).astype(jnp.int32)
    octets = jax.vmap(assemble)(lowpass[row_index].reshape(NBLK // 8, 8, Q, Q, Q))
    coarse = lax.map(coarse_levels, octets)
    corners = jax.vmap(split_octet)(coarse).reshape(NBLK, Q, Q, Q)
    slot_corner = jnp.zeros((DEVICES * SLOTS, Q, Q, Q), jnp.float32).at[row_index].set(corners)
    slot_ids = jnp.arange(DEVICES * SLOTS, dtype=jnp.int32)
    live_slots = (slot_ids % SLOTS) < counts[slot_ids // SLOTS]

    def finish_block(inputs):
        block_cube, corner_cube, is_live = inputs
        finished = fine_levels(block_cube).at[:Q, :Q, :Q].set(corner_cube)
        return jnp.where(is_live, finished, jnp.zeros_like(finished))

    result = lax.map(finish_block, (blocks, slot_corner, live_slots))
    return result.reshape(DEVICES * SLOTS, B, B * B)
```

```python
import functools

import jax
import jax.numpy as jnp
import ml_dtypes
import numpy as np
from jax import lax
from jax.experimental import pallas as pl
from jax.experimental.pallas import tpu as pltpu
from jax.sharding import PartitionSpec as P

MESH = pl.DeviceIdType.MESH
F32 = jnp.float32
BF16 = jnp.bfloat16

A_LIFT = -1.586134342059924
B_LIFT = -0.052980118572961
C_LIFT = 0.882911075530934
D_LIFT = 0.443506852043971
K_LIFT = 1.230174104914001
A_SC = A_LIFT * K_LIFT * K_LIFT
B_SC = B_LIFT / (K_LIFT * K_LIFT)
C_SC = C_LIFT * K_LIFT * K_LIFT
D_SC = D_LIFT / (K_LIFT * K_LIFT)

SLOTS = 6
HALO = (6, 6, 5, 4, 3, 2, 1)
HBASE = (0, 6, 12, 17, 21, 24, 26)
HTOTAL = 27


def lift_matrix(n):
    x = np.eye(n)
    s, e = x[0::2].copy(), x[1::2].copy()

    def up(v):
        return np.concatenate([v[1:], v[-1:]], 0)

    def down(v):
        return np.concatenate([v[:1], v[:-1]], 0)

    e = e + A_LIFT * (s + up(s))
    s = s + B_LIFT * (down(e) + e)
    e = e + C_LIFT * (s + up(s))
    s = s + D_LIFT * (down(e) + e)
    return np.concatenate([s / K_LIFT, e * K_LIFT], 0)


def split_const(m):
    hi = m.astype(ml_dtypes.bfloat16)
    lo = (m - hi.astype(np.float64)).astype(ml_dtypes.bfloat16)
    return hi, lo


def left_const(m):
    hi, lo = split_const(m)
    return np.concatenate([hi, lo, hi, lo], 1)


def right_const(m):
    hi, lo = split_const(m)
    return np.concatenate([hi, lo, hi], 0)


def fine_right(n):
    t = lift_matrix(n)
    w = np.zeros((256, 256))
    for q in range(2):
        for par in range(2):
            r = 128 * q + 64 * par
            c = 128 * par + 64 * q
            w[r : r + n, c : c + n] = t.T * (K_LIFT if par else 1.0 / K_LIFT)
    return right_const(w)


def coarse_right():
    t = lift_matrix(32)
    w = np.zeros((256, 256))
    for j in range(8):
        for k2 in range(2):
            for kb in range(2):
                r = 128 * k2 + 16 * j
                c = 128 * (j % 2) + 64 * kb + 16 * (j // 2)
                scale = K_LIFT if j % 2 else 1.0 / K_LIFT
                w[r : r + 16, c : c + 16] = t[16 * kb : 16 * kb + 16, 16 * k2 : 16 * k2 + 16].T * scale
    return right_const(w)


def corner_left():
    t16, t8 = lift_matrix(16), lift_matrix(8)
    return left_const(np.concatenate([t16, t8 @ t16[:8]], 0))


def corner_right():
    t16, t8 = lift_matrix(16), lift_matrix(8)
    second = np.kron(t16, t16).T
    low = t8 @ t16[:8]
    both = np.zeros((256, 128))
    for j in range(8):
        for k in range(8):
            both[:, 16 * j + k] = np.kron(low[j], low[k])
    return right_const(np.concatenate([second, both], 1))


def split(x):
    hi = x.astype(BF16)
    lo = (x - hi.astype(F32)).astype(BF16)
    return hi, lo


def left_dot(t, x):
    hi, lo = split(x)
    return jnp.dot(t, jnp.concatenate([hi, hi, lo, lo], 0), preferred_element_type=F32)


def right_dot(hi, lo, w):
    return jnp.dot(jnp.concatenate([hi, hi, lo], 1), w, preferred_element_type=F32)


def lift_lanes(s, e, mask, up, down):
    n = len(s)
    sp = up(s)
    e = [e[g] + A_SC * (s[g] + sp[g]) for g in range(n)]
    em = down(e)
    s = [s[g] + B_SC * (em[g] + e[g]) for g in range(n)]
    sp = up(s)
    e = [e[g] + C_SC * (s[g] + sp[g]) for g in range(n)]
    em = down(e)
    s = [s[g] + D_SC * (em[g] + e[g]) for g in range(n)]
    return s, e


def lift_halves(s, e, low):
    n = len(s)

    def up(v):
        r = [pltpu.roll(x, 64, 1) for x in v]
        return [jnp.where(low, r[g], r[g + 1] if g + 1 < n else v[g]) for g in range(n)]

    def down(v):
        r = [pltpu.roll(x, 64, 1) for x in v]
        return [jnp.where(low, r[g - 1] if g else v[g], r[g]) for g in range(n)]

    return lift_lanes(s, e, low, up, down)


def lift_quarters(s, e, last, first):
    n = len(s)

    def up(v):
        out = []
        for g in range(n):
            near = pltpu.roll(v[g], 112, 1)
            far = pltpu.roll(v[g + 1], 48, 1) if g + 1 < n else v[g]
            out.append(jnp.where(last, far, near))
        return out

    def down(v):
        out = []
        for g in range(n):
            near = pltpu.roll(v[g], 16, 1)
            far = pltpu.roll(v[g - 1], 80, 1) if g else v[g]
            out.append(jnp.where(first, far, near))
        return out

    return lift_lanes(s, e, last, up, down)


def fine_kernel(count_ref, x_ref, t1_ref, w1_ref, t2_ref, w2_ref, o_ref, lpf_ref, lpb_ref, cv_ref, a_ref, se_ref):
    slot = pl.program_id(0)
    count = count_ref[0]
    lane = lax.broadcasted_iota(jnp.int32, (8, 128), 1)
    low = lane < 64

    @pl.when(slot == 0)
    def _():
        lpf_ref[...] = jnp.zeros_like(lpf_ref)
        lpb_ref[...] = jnp.zeros_like(lpb_ref)
        cv_ref[...] = jnp.full_like(cv_ref, count)

    @pl.when(slot >= count)
    def _():
        o_ref[...] = jnp.zeros_like(o_ref)

    @pl.when(slot < count)
    def _():
        for g in range(16):
            y = left_dot(t1_ref[...], x_ref[0, :, 256 * g : 256 * g + 256])
            hi, lo = split(y)
            a_ref[64 * g : 64 * g + 64, :256] = hi
            a_ref[64 * g : 64 * g + 64, 256:] = lo
        se_ref[...] = right_dot(a_ref[:, :256], a_ref[:, 256:], w1_ref[...])
        for r in range(8):
            s = [se_ref[64 * g + 8 * r : 64 * g + 8 * r + 8, :128] for g in range(16)]
            e = [se_ref[64 * g + 8 * r : 64 * g + 8 * r + 8, 128:] for g in range(16)]
            s, e = lift_halves(s, e, low)
            for g in range(16):
                o_ref[0, 8 * r : 8 * r + 8, 128 * g : 128 * g + 128] = s[g]
                o_ref[0, 8 * r : 8 * r + 8, 2048 + 128 * g : 2048 + 128 * g + 128] = e[g]
        for h in range(8):
            y = left_dot(t2_ref[...], o_ref[0, :32, 256 * h : 256 * h + 256])
            hi, lo = split(y)
            a_ref[32 * h : 32 * h + 32, :256] = hi
            a_ref[32 * h : 32 * h + 32, 256:] = lo
        se_ref[:256] = right_dot(a_ref[:256, :256], a_ref[:256, 256:], w2_ref[...])
        corner = (lane & 63) < 32
        for r in range(4):
            s = [se_ref[32 * h + 8 * r : 32 * h + 8 * r + 8, :128] for h in range(8)]
            e = [se_ref[32 * h + 8 * r : 32 * h + 8 * r + 8, 128:] for h in range(8)]
            s, e = lift_halves(s, e, low)
            rows = slice(8 * r, 8 * r + 8)
            for h in range(8):
                cols = slice(128 * h, 128 * h + 128)
                o_ref[0, rows, cols] = jnp.where(corner, s[h], o_ref[0, rows, cols])
                cols = slice(1024 + 128 * h, 1024 + 128 * h + 128)
                o_ref[0, rows, cols] = jnp.where(corner, e[h], o_ref[0, rows, cols])
            if r < 2:
                for half in range(2):
                    packed = s[4 * half]
                    for hh in range(4):
                        v = s[4 * half + hh]
                        if hh:
                            packed = jnp.where(lane // 16 == 2 * hh, pltpu.roll(v, 32 * hh, 1), packed)
                        packed = jnp.where(lane // 16 == 2 * hh + 1, pltpu.roll(v, (32 * hh + 80) % 128, 1), packed)
                    at = 16 * half + 8 * r
                    lpf_ref[slot, at : at + 8] = packed
                    lpb_ref[slot + SLOTS - count, at : at + 8] = packed


def fine_call(density, counts):
    t1 = left_const(lift_matrix(64))
    w1 = fine_right(64)
    t2 = left_const(lift_matrix(32))
    w2 = fine_right(32)
    whole = lambda s, c: (0, 0)
    grid_spec = pltpu.PrefetchScalarGridSpec(
        num_scalar_prefetch=1,
        grid=(SLOTS,),
        in_specs=[
            pl.BlockSpec((1, 64, 4096), lambda s, c: (jnp.minimum(s, c[0] - 1), 0, 0)),
            pl.BlockSpec(t1.shape, whole),
            pl.BlockSpec(w1.shape, whole),
            pl.BlockSpec(t2.shape, whole),
            pl.BlockSpec(w2.shape, whole),
        ],
        out_specs=[
            pl.BlockSpec((1, 64, 4096), lambda s, c: (s, 0, 0)),
            pl.BlockSpec((SLOTS, 32, 128), lambda s, c: (0, 0, 0)),
            pl.BlockSpec((SLOTS, 32, 128), lambda s, c: (0, 0, 0)),
            pl.BlockSpec((8, 128), whole),
        ],
        scratch_shapes=[pltpu.VMEM((1024, 512), BF16), pltpu.VMEM((1024, 256), F32)],
    )
    return pl.pallas_call(
        fine_kernel,
        grid_spec=grid_spec,
        out_shape=[
            jax.ShapeDtypeStruct(density.shape, F32),
            jax.ShapeDtypeStruct((SLOTS, 32, 128), F32),
            jax.ShapeDtypeStruct((SLOTS, 32, 128), F32),
            jax.ShapeDtypeStruct((8, 128), jnp.int32),
        ],
        compiler_params=pltpu.CompilerParams(vmem_limit_bytes=32 << 20, dimension_semantics=("arbitrary",)),
        name="fine",
    )(counts, density, jnp.asarray(t1), jnp.asarray(w1), jnp.asarray(t2), jnp.asarray(w2))


def exchange_kernel(lpf_ref, lpb_ref, cv_ref, fw_ref, bw_ref, tab_ref, a_ref, row_ref, b_ref, dsend, drecv, asend, arecv, bsend, brecv):
    node, dev = lax.axis_index("node"), lax.axis_index("dev")
    me = node * 16 + dev
    barrier = pltpu.get_barrier_semaphore()

    def by_offset(step):
        t = lax.rem(me + step + 256, 256)
        return {"node": t // 16, "dev": lax.rem(t, 16)}

    def by_dev(k):
        return {"node": node, "dev": lax.rem(dev + k, 16)}

    def by_node(k):
        return {"node": lax.rem(node + k, 16), "dev": dev}

    partners = [by_offset(o) for o in range(1, 8)] + [by_offset(-o) for o in range(1, 8)]
    partners += [by_dev(k) for k in range(1, 16)] + [by_node(k) for k in range(1, 16)]
    for p in partners:
        pl.semaphore_signal(barrier, inc=1, device_id=p, device_id_type=MESH)
    pl.semaphore_wait(barrier, len(partners))

    stage_a, stage_b, data = [], [], []
    a_ref[0] = cv_ref[...]
    for k in range(1, 16):
        c = pltpu.make_async_remote_copy(
            src_ref=cv_ref, dst_ref=a_ref.at[k], send_sem=asend.at[k], recv_sem=arecv.at[k], device_id=by_dev(k), device_id_type=MESH
        )
        c.start()
        stage_a.append(c)
    for o in range(1, 8):
        n, b = HALO[o - 1], HBASE[o - 1]
        for way in range(2):
            c = pltpu.make_async_remote_copy(
                src_ref=lpb_ref.at[pl.ds(SLOTS - n, n)] if way else lpf_ref.at[pl.ds(0, n)],
                dst_ref=(bw_ref if way else fw_ref).at[pl.ds(b, n)],
                send_sem=dsend.at[way, o],
                recv_sem=drecv.at[way, o],
                device_id=by_offset(o if way else -o),
                device_id_type=MESH,
            )
            c.start()
            data.append(c)
    for c in stage_a:
        c.wait()
    lane = lax.broadcasted_iota(jnp.int32, (8, 128), 1)
    row = jnp.zeros((8, 128), jnp.int32)
    for k in range(16):
        row = jnp.where(lane == lax.rem(dev - k + 16, 16), a_ref[k], row)
    row_ref[...] = row
    for k in range(1, 16):
        c = pltpu.make_async_remote_copy(
            src_ref=row_ref, dst_ref=b_ref.at[k], send_sem=bsend.at[k], recv_sem=brecv.at[k], device_id=by_node(k), device_id_type=MESH
        )
        c.start()
        stage_b.append(c)
    for c in stage_b:
        c.wait()
    tab_ref[0:1] = row[0:1]
    for k in range(1, 16):
        tab_ref[k : k + 1] = b_ref[k][0:1]
    for c in data:
        c.wait()


def exchange_call(lpf, lpb, cv):
    vmem = pl.BlockSpec(memory_space=pltpu.VMEM)
    dma = pltpu.SemaphoreType.DMA
    return pl.pallas_call(
        exchange_kernel,
        in_specs=[vmem] * 3,
        out_specs=[vmem] * 3,
        out_shape=[
            jax.ShapeDtypeStruct((HTOTAL, 32, 128), F32),
            jax.ShapeDtypeStruct((HTOTAL, 32, 128), F32),
            jax.ShapeDtypeStruct((16, 128), jnp.int32),
        ],
        scratch_shapes=[
            pltpu.VMEM((16, 8, 128), jnp.int32),
            pltpu.VMEM((8, 128), jnp.int32),
            pltpu.VMEM((16, 8, 128), jnp.int32),
            dma((2, 8)),
            dma((2, 8)),
            dma((16,)),
            dma((16,)),
            dma((16,)),
            dma((16,)),
        ],
        compiler_params=pltpu.CompilerParams(collective_id=0, has_side_effects=True, vmem_limit_bytes=16 << 20),
        name="exchange",
    )(lpf, lpb, cv)


def coarse_kernel(tabs_ref, lpf_ref, fw_ref, bw_ref, tab_ref, t1_ref, w1_ref, t2_ref, w2_ref, fine_ref, o_ref, h_ref, ctx_ref, res_ref, rsem, wsem):
    del fine_ref
    node, dev = lax.axis_index("node"), lax.axis_index("dev")
    me = node * 16 + dev
    for s in range(SLOTS):
        pltpu.make_async_copy(o_ref.at[s, pl.ds(0, 16), pl.ds(0, 1024)], ctx_ref.at[s], rsem.at[s]).start()
    krow = lax.broadcasted_iota(jnp.int32, (16, 128), 0)
    klane = lax.broadcasted_iota(jnp.int32, (16, 128), 1)
    owner = lax.rem(node - krow + 16, 16) * 16 + klane
    start = jnp.sum(jnp.where((klane < 16) & (owner < me), tab_ref[...], 0))
    first = start // 8

    def count_of(t):
        return tabs_ref[lax.rem(node - t // 16 + 16, 16), lax.rem(t, 16)]

    count = count_of(me)
    for s in range(SLOTS):
        h_ref[7 + s] = lpf_ref[s]
    after = 7 + count
    before = 7
    for o in range(1, 8):
        n, b = HALO[o - 1], HBASE[o - 1]
        for s in range(n):
            h_ref[jnp.minimum(after + s, 24)] = fw_ref[b + s]
        for s in range(n):
            p = before - n + s
            h_ref[jnp.where(p < 0, 25, p)] = bw_ref[b + s]
        after = after + count_of(lax.rem(me + o, 256))
        before = before - count_of(lax.rem(me - o + 256, 256))

    lane = lax.broadcasted_iota(jnp.int32, (8, 128), 1)
    base = 7 + first * 8 - start
    hs, ls = [], []
    for q in range(2):
        groups = []
        for c1 in range(2):
            for jh in range(2):
                for c2 in range(2):
                    c = 2 * c1 + 4 * c2
                    at = base + 8 * q + c
                    groups.append(jnp.concatenate([h_ref[at, 16 * jh : 16 * jh + 16], h_ref[at + 1, 16 * jh : 16 * jh + 16]], 0))
        y = left_dot(t1_ref[...], jnp.concatenate(groups, 1))
        hi, lo = split(y)
        for g in range(4):
            hs.append(hi[:, 256 * g : 256 * g + 256])
            ls.append(lo[:, 256 * g : 256 * g + 256])
    y = right_dot(jnp.concatenate(hs, 0), jnp.concatenate(ls, 0), w1_ref[...])
    last, firstm = (lane // 16) % 4 == 3, (lane // 16) % 4 == 0
    low = lane < 64
    corners = []
    for q in range(2):
        halves = []
        for r in range(4):
            at = [128 * q + 32 * g + 8 * r for g in range(4)]
            s = [y[a : a + 8, :128] for a in at]
            e = [y[a : a + 8, 128:] for a in at]
            s, e = lift_quarters(s, e, last, firstm)
            for g in range(4):
                res_ref[q, r // 2, 0, g, 8 * (r % 2) : 8 * (r % 2) + 8] = s[g]
                res_ref[q, r // 2, 1, g, 8 * (r % 2) : 8 * (r % 2) + 8] = e[g]
            if r < 2:
                halves.append(
                    jnp.concatenate([jnp.where(low, s[0], pltpu.roll(s[1], 64, 1)), jnp.where(low, s[2], pltpu.roll(s[3], 64, 1))], 1)
                )
        corners.append(jnp.concatenate(halves, 0))
    y = left_dot(t2_ref[...], jnp.concatenate(corners, 1))
    hi, lo = split(y)
    y = right_dot(
        jnp.concatenate([hi[:, :256], hi[:, 256:]], 0), jnp.concatenate([lo[:, :256], lo[:, 256:]], 0), w2_ref[...]
    )
    deep = (lane & 15) < 8
    for q in range(2):
        for r in range(2):
            a = 24 * q + 8 * r
            v0, v1 = y[a : a + 8, :128], y[a : a + 8, 128:256]
            if r == 0:
                v0 = jnp.where(deep, y[24 * q + 16 : 24 * q + 24, 256:], v0)
            rows = slice(8 * r, 8 * r + 8)
            for g, v in enumerate([v0, pltpu.roll(v0, 64, 1), v1, pltpu.roll(v1, 64, 1)]):
                res_ref[q, 0, 0, g, rows] = jnp.where(low, v, res_ref[q, 0, 0, g, rows])
    for s in range(SLOTS):
        pltpu.make_async_copy(o_ref.at[s, pl.ds(0, 16), pl.ds(0, 1024)], ctx_ref.at[s], rsem.at[s]).wait()

        @pl.when(s < count)
        def _(s=s):
            block = start + s
            q = block // 8 - first
            c0, c1, c2 = lax.rem(block, 2), lax.rem(block // 2, 2), lax.rem(block // 4, 2)
            for r in range(2):
                rows = slice(8 * r, 8 * r + 8)
                for g in range(4):
                    v = res_ref[q, c0, c1, g, rows]
                    v = jnp.where(c2 == 1, pltpu.roll(v, 64, 1), v)
                    for mh in range(2):
                        cols = slice(256 * g + 128 * mh, 256 * g + 128 * mh + 128)
                        left = pltpu.roll(v, 96, 1) if mh else v
                        right = pltpu.roll(v, 16 if mh else 48, 1)
                        old = ctx_ref[s, rows, cols]
                        new = jnp.where(lane < 16, left, jnp.where((lane >= 64) & (lane < 80), right, old))
                        ctx_ref[s, rows, cols] = new
            pltpu.make_async_copy(ctx_ref.at[s], o_ref.at[s, pl.ds(0, 16), pl.ds(0, 1024)], wsem.at[s]).start()

    for s in range(SLOTS):

        @pl.when(s < count)
        def _(s=s):
            pltpu.make_async_copy(ctx_ref.at[s], o_ref.at[s, pl.ds(0, 16), pl.ds(0, 1024)], wsem.at[s]).wait()


def coarse_call(fine, lpf, fw, bw, tab):
    t1, w1, t2, w2 = left_const(lift_matrix(32)), coarse_right(), corner_left(), corner_right()
    vmem = pl.BlockSpec(memory_space=pltpu.VMEM)
    dma = pltpu.SemaphoreType.DMA
    return pl.pallas_call(
        coarse_kernel,
        in_specs=[pl.BlockSpec(memory_space=pltpu.SMEM)] + [vmem] * 8 + [pl.BlockSpec(memory_space=pl.ANY)],
        out_specs=pl.BlockSpec(memory_space=pl.ANY),
        out_shape=jax.ShapeDtypeStruct(fine.shape, F32),
        scratch_shapes=[
            pltpu.VMEM((32, 32, 128), F32),
            pltpu.VMEM((SLOTS, 16, 1024), F32),
            pltpu.VMEM((2, 2, 2, 4, 16, 128), F32),
            dma((SLOTS,)),
            dma((SLOTS,)),
        ],
        input_output_aliases={9: 0},
        compiler_params=pltpu.CompilerParams(vmem_limit_bytes=16 << 20),
        name="coarse",
    )(tab, lpf, fw, bw, tab, jnp.asarray(t1), jnp.asarray(w1), jnp.asarray(t2), jnp.asarray(w2), fine)


def per_device(density, counts):
    fine, lpf, lpb, cv = fine_call(density, counts)
    fw, bw, tab = exchange_call(lpf, lpb, cv)
    return coarse_call(fine, lpf, fw, bw, tab)


def solution(mesh):
    in_specs = (P(("node", "dev"), None, None), P(("node", "dev")))
    out_specs = P(("node", "dev"), None, None)
    return jax.shard_map(per_device, mesh=mesh, in_specs=in_specs, out_specs=out_specs, check_vma=False)
```

```python
import functools

import jax
import jax.numpy as jnp
import ml_dtypes
import numpy as np
from jax import lax
from jax.experimental import pallas as pl
from jax.experimental.pallas import tpu as pltpu
from jax.sharding import PartitionSpec as P

MESH = pl.DeviceIdType.MESH
F32 = jnp.float32
BF16 = jnp.bfloat16

A_LIFT = -1.586134342059924
B_LIFT = -0.052980118572961
C_LIFT = 0.882911075530934
D_LIFT = 0.443506852043971
K_LIFT = 1.230174104914001
A_SC = A_LIFT * K_LIFT * K_LIFT
B_SC = B_LIFT / (K_LIFT * K_LIFT)
C_SC = C_LIFT * K_LIFT * K_LIFT
D_SC = D_LIFT / (K_LIFT * K_LIFT)

SLOTS = 6
HALO = (6, 6, 5, 4, 3, 2, 1)
HBASE = (0, 6, 12, 17, 21, 24, 26)
HTOTAL = 27


def lift_matrix(n):
    x = np.eye(n)
    s, e = x[0::2].copy(), x[1::2].copy()

    def up(v):
        return np.concatenate([v[1:], v[-1:]], 0)

    def down(v):
        return np.concatenate([v[:1], v[:-1]], 0)

    e = e + A_LIFT * (s + up(s))
    s = s + B_LIFT * (down(e) + e)
    e = e + C_LIFT * (s + up(s))
    s = s + D_LIFT * (down(e) + e)
    return np.concatenate([s / K_LIFT, e * K_LIFT], 0)


def split_const(m):
    hi = m.astype(ml_dtypes.bfloat16)
    lo = (m - hi.astype(np.float64)).astype(ml_dtypes.bfloat16)
    return hi, lo


def left_const(m):
    hi, lo = split_const(m)
    return np.concatenate([hi, lo, hi], 1)


def right_const(m):
    hi, lo = split_const(m)
    return np.concatenate([hi, lo, hi], 0)


def fine_right(n):
    t = lift_matrix(n)
    w = np.zeros((256, 256))
    for q in range(2):
        for par in range(2):
            r = 128 * q + 64 * par
            c = 128 * par + 64 * q
            w[r : r + n, c : c + n] = t.T * (K_LIFT if par else 1.0 / K_LIFT)
    return right_const(w)


def coarse_right():
    t = lift_matrix(32)
    w = np.zeros((256, 256))
    for j in range(8):
        for k2 in range(2):
            for kb in range(2):
                r = 128 * k2 + 16 * j
                c = 128 * (j % 2) + 64 * kb + 16 * (j // 2)
                scale = K_LIFT if j % 2 else 1.0 / K_LIFT
                w[r : r + 16, c : c + 16] = t[16 * kb : 16 * kb + 16, 16 * k2 : 16 * k2 + 16].T * scale
    return right_const(w)


def corner_left():
    t16, t8 = lift_matrix(16), lift_matrix(8)
    return left_const(np.concatenate([t16, t8 @ t16[:8]], 0))


def corner_right():
    t16, t8 = lift_matrix(16), lift_matrix(8)
    second = np.kron(t16, t16).T
    low = t8 @ t16[:8]
    both = np.zeros((256, 128))
    for j in range(8):
        for k in range(8):
            both[:, 16 * j + k] = np.kron(low[j], low[k])
    return right_const(np.concatenate([second, both], 1))


def split(x):
    hi = x.astype(BF16)
    lo = (x - hi.astype(F32)).astype(BF16)
    return hi, lo


def left_dot(t, x):
    hi, lo = split(x)
    return jnp.dot(t, jnp.concatenate([hi, hi, lo], 0), preferred_element_type=F32)


def right_dot(hi, lo, w):
    return jnp.dot(jnp.concatenate([hi, hi, lo], 1), w, preferred_element_type=F32)


def lift_lanes(s, e, mask, up, down):
    n = len(s)
    sp = up(s)
    e = [e[g] + A_SC * (s[g] + sp[g]) for g in range(n)]
    em = down(e)
    s = [s[g] + B_SC * (em[g] + e[g]) for g in range(n)]
    sp = up(s)
    e = [e[g] + C_SC * (s[g] + sp[g]) for g in range(n)]
    em = down(e)
    s = [s[g] + D_SC * (em[g] + e[g]) for g in range(n)]
    return s, e


def lift_halves(s, e, low):
    n = len(s)

    def up(v):
        r = [pltpu.roll(x, 64, 1) for x in v]
        return [jnp.where(low, r[g], r[g + 1] if g + 1 < n else v[g]) for g in range(n)]

    def down(v):
        r = [pltpu.roll(x, 64, 1) for x in v]
        return [jnp.where(low, r[g - 1] if g else v[g], r[g]) for g in range(n)]

    return lift_lanes(s, e, low, up, down)


def lift_quarters(s, e, last, first):
    n = len(s)

    def up(v):
        out = []
        for g in range(n):
            near = pltpu.roll(v[g], 112, 1)
            far = pltpu.roll(v[g + 1], 48, 1) if g + 1 < n else v[g]
            out.append(jnp.where(last, far, near))
        return out

    def down(v):
        out = []
        for g in range(n):
            near = pltpu.roll(v[g], 16, 1)
            far = pltpu.roll(v[g - 1], 80, 1) if g else v[g]
            out.append(jnp.where(first, far, near))
        return out

    return lift_lanes(s, e, last, up, down)


def lift_stream(load_s, load_e, n, emit):
    s0, e1, s1, e2 = load_s(0), None, None, None
    for i in range(n):
        s_next = load_s(i + 1) if i + 1 < n else s0
        e1_new = load_e(i) + A_SC * (s0 + s_next)
        s1_new = s0 + B_SC * ((e1 if i else e1_new) + e1_new)
        if i:
            e2_new = e1 + C_SC * (s1 + s1_new)
            emit(i - 1, s1 + D_SC * ((e2 if i > 1 else e2_new) + e2_new), e2_new)
            e2 = e2_new
        s0, e1, s1 = s_next, e1_new, s1_new
    e2_new = e1 + C_SC * (s1 + s1)
    emit(n - 1, s1 + D_SC * (e2 + e2_new), e2_new)


def fine_kernel(
    count_ref, x_ref, wc_ref, t1c_ref, t2c_ref, o_ref, lpf_ref, fw_ref, bw_ref, tab_ref,
    lpb_ref, w_ref, t1_ref, t2_ref, xh_ref, xl_ref, ah_ref, al_ref, se_ref, cv_ref, a_ref, row_ref, b_ref,
    xsem, wsem, dsend, drecv, csend, crecv,
):
    node, dev = lax.axis_index("node"), lax.axis_index("dev")
    me = node * 16 + dev
    count = count_ref[0]
    lane = lax.broadcasted_iota(jnp.int32, (16, 128), 1)
    low = lane < 64
    corner = (lane & 63) < 32

    def load_x(s):
        return pltpu.make_async_copy(x_ref.at[s], o_ref.at[s], xsem.at[s])

    constants = [(wc_ref, w_ref), (t1c_ref, t1_ref), (t2c_ref, t2_ref)]
    load_c = [pltpu.make_async_copy(a, b, wsem.at[i]) for i, (a, b) in enumerate(constants)]
    load_x(0).start()
    for c in load_c:
        c.start()
    for s in range(1, SLOTS):
        load_x(s).start()

    barrier = pltpu.get_barrier_semaphore()

    def by_offset(step):
        t = lax.rem(me + step + 256, 256)
        return {"node": t // 16, "dev": lax.rem(t, 16)}

    def by_dev(k):
        return {"node": node, "dev": lax.rem(dev + k, 16)}

    def by_node(k):
        return {"node": lax.rem(node + k, 16), "dev": dev}

    partners = [by_offset(o) for o in range(1, 8)] + [by_offset(-o) for o in range(1, 8)]
    partners += [by_dev(k) for k in range(1, 16)] + [by_node(k) for k in range(1, 16)]
    for p in partners:
        pl.semaphore_signal(barrier, inc=1, device_id=p, device_id_type=MESH)
    cv_ref[...] = jnp.zeros_like(cv_ref) + count

    def remote(src, dst, send, recv, to):
        return pltpu.make_async_remote_copy(
            src_ref=src, dst_ref=dst, send_sem=send, recv_sem=recv, device_id=to, device_id_type=MESH
        )

    def stage(src, dst, i, to):
        for k in range(1, 16):
            remote(src, dst.at[k], csend.at[i], crecv.at[i], to(k)).start()

    def stage_wait(dst, i):
        c = remote(dst.at[pl.ds(1, 15)], dst.at[pl.ds(1, 15)], csend.at[i], crecv.at[i], by_dev(1))
        c.wait_send()
        c.wait_recv()

    def forward(o, part):
        first, last = (0, min(3, HALO[o - 1])) if part == 0 else (3, HALO[o - 1])
        at = pl.ds(HBASE[o - 1] + first, last - first)
        return remote(lpf_ref.at[pl.ds(first, last - first)], fw_ref.at[at], dsend.at[part, o], drecv.at[part, o], by_offset(-o))

    def backward(o):
        n, b = HALO[o - 1], HBASE[o - 1]
        return remote(lpb_ref.at[pl.ds(SLOTS - n, n)], bw_ref.at[pl.ds(b, n)], dsend.at[2, o], drecv.at[2, o], by_offset(o))

    def rows_dot(t, hi, lo, g):
        y = jnp.dot(t, jnp.concatenate([hi, hi, lo], 0), preferred_element_type=F32)
        hi, lo = split(y)
        for nn in range(2):
            to = slice((2 * g + nn) * 16, (2 * g + nn) * 16 + 16)
            cols = slice(128 * nn, 128 * nn + 128)
            for q in range(2):
                ah_ref[to, 128 * q : 128 * q + 128] = hi[16 * q : 16 * q + 16, cols]
                al_ref[to, 128 * q : 128 * q + 128] = lo[16 * q : 16 * q + 16, cols]

    def columns(n, w, store, keep):
        rows = slice(0, 16 * n)
        se_ref[rows] = right_dot(ah_ref[rows], al_ref[rows], w_ref[w])
        held = {}

        def emit(i, s, e):
            keep(s)
            if i % 2 == 0:
                held[0] = (s, e)
                return
            for band, (x0, x1) in enumerate(zip(held[0], (s, e))):
                r0, r1 = pltpu.roll(x0, 64, 1), pltpu.roll(x1, 64, 1)
                store(0, band, i // 2, jnp.where(low, x0, r1))
                store(16, band, i // 2, jnp.where(low, r0, x1))

        lift_stream(lambda i: se_ref[16 * i : 16 * i + 16, :128], lambda i: se_ref[16 * i : 16 * i + 16, 128:], n, emit)

    def first_pass(slot, carry):
        load_x(slot).wait()

        @pl.when(slot == 0)
        def _():
            for c in load_c:
                c.wait()

        for g in range(16):
            cols = slice(256 * g, 256 * g + 256)
            hi, lo = split(o_ref[slot, :, cols])
            xh_ref[slot, :, cols] = hi
            xl_ref[slot, :, cols] = lo
            rows_dot(t1_ref[:32], hi, lo, g)

        def store1(row, band, u, v):
            o_ref[slot, row : row + 16, 2048 * band + 128 * u : 2048 * band + 128 * u + 128] = v

        columns(32, 0, store1, lambda s: None)
        for h in range(8):
            hi, lo = split(o_ref[slot, :32, 256 * h : 256 * h + 256])
            rows_dot(t2_ref[...], hi, lo, h)
        kept = []

        def store2(row, band, u, v):
            at = (slot, slice(row, row + 16), slice(1024 * band + 128 * u, 1024 * band + 128 * u + 128))
            o_ref[at] = jnp.where(corner, v, o_ref[at])

        columns(16, 1, store2, kept.append)
        for half in range(2):
            packed = kept[8 * half]
            for jl in range(1, 8):
                packed = jnp.where((lane >> 4) == jl, pltpu.roll(kept[8 * half + jl], 16 * jl, 1), packed)
            lpf_ref[slot, 16 * half : 16 * half + 16] = packed

        @pl.when(slot == 0)
        def _():
            pl.semaphore_wait(barrier, len(partners))
            stage(cv_ref, a_ref, 0, by_dev)

        @pl.when(slot == 1)
        def _():
            stage_wait(a_ref, 0)
            row = jnp.where(lane[:8] == dev, cv_ref[...], 0)
            for k in range(1, 16):
                row = jnp.where(lane[:8] == lax.rem(dev - k + 16, 16), a_ref[k], row)
            row_ref[...] = row
            stage(row_ref, b_ref, 1, by_node)

        @pl.when(slot == 2)
        def _():
            for o in range(1, 8):
                forward(o, 0).start()

        return carry

    lax.fori_loop(0, SLOTS, first_pass, 0)
    for s in range(SLOTS):
        lpb_ref[s] = lpf_ref[jnp.maximum(count - SLOTS + s, 0)]
    for o in range(1, 8):
        backward(o).start()
        if HALO[o - 1] > 3:
            forward(o, 1).start()

    def second_pass(slot, carry):
        for g in range(16):
            cols = slice(256 * g, 256 * g + 256)
            rows_dot(t1_ref[32:], xh_ref[slot, :, cols], xl_ref[slot, :, cols], g)

        def store1(row, band, u, v):
            o_ref[slot, 32 + row : 48 + row, 2048 * band + 128 * u : 2048 * band + 128 * u + 128] = v

        columns(32, 0, store1, lambda s: None)
        return carry

    lax.fori_loop(0, SLOTS, second_pass, 0)
    stage_wait(b_ref, 1)
    tab_ref[0:1] = row_ref[0:1]
    for k in range(1, 16):
        tab_ref[k : k + 1] = b_ref[k][0:1]
    for o in range(1, 8):
        forward(o, 0).wait()
        if HALO[o - 1] > 3:
            forward(o, 1).wait()
        backward(o).wait()


def fine_call(density, counts):
    t1, t2 = left_const(lift_matrix(64)), left_const(lift_matrix(32))
    w = np.stack([fine_right(64), fine_right(32)])
    vmem = pl.BlockSpec(memory_space=pltpu.VMEM)
    hbm = pl.BlockSpec(memory_space=pltpu.HBM)
    dma = pltpu.SemaphoreType.DMA
    return pl.pallas_call(
        fine_kernel,
        in_specs=[pl.BlockSpec(memory_space=pltpu.SMEM)] + [hbm] * 4,
        out_specs=[vmem] * 5,
        out_shape=[
            jax.ShapeDtypeStruct(density.shape, F32),
            jax.ShapeDtypeStruct((SLOTS, 32, 128), F32),
            jax.ShapeDtypeStruct((HTOTAL, 32, 128), F32),
            jax.ShapeDtypeStruct((HTOTAL, 32, 128), F32),
            jax.ShapeDtypeStruct((16, 128), jnp.int32),
        ],
        scratch_shapes=[
            pltpu.VMEM((SLOTS, 32, 128), F32),
            pltpu.VMEM(w.shape, BF16),
            pltpu.VMEM(t1.shape, BF16),
            pltpu.VMEM(t2.shape, BF16),
            pltpu.VMEM((SLOTS, 64, 4096), BF16),
            pltpu.VMEM((SLOTS, 64, 4096), BF16),
            pltpu.VMEM((512, 256), BF16),
            pltpu.VMEM((512, 256), BF16),
            pltpu.VMEM((512, 256), F32),
            pltpu.VMEM((8, 128), jnp.int32),
            pltpu.VMEM((16, 8, 128), jnp.int32),
            pltpu.VMEM((8, 128), jnp.int32),
            pltpu.VMEM((16, 8, 128), jnp.int32),
            dma((SLOTS,)),
            dma((3,)),
            dma((3, 8)),
            dma((3, 8)),
            dma((2,)),
            dma((2,)),
        ],
        compiler_params=pltpu.CompilerParams(collective_id=0, has_side_effects=True, vmem_limit_bytes=30 << 20),
        name="fine",
    )(counts, *[pltpu.with_memory_space_constraint(jnp.asarray(a), pltpu.HBM) for a in (density, w, t1, t2)])


def coarse_kernel(tabs_ref, lpf_ref, fw_ref, bw_ref, tab_ref, t1_ref, w1_ref, t2_ref, w2_ref, fine_ref, o_ref, h_ref, ctx_ref, res_ref, zero_ref, wsem):
    node, dev = lax.axis_index("node"), lax.axis_index("dev")
    me = node * 16 + dev
    count = tabs_ref[0, dev]

    def body(s):
        return pltpu.make_async_copy(fine_ref.at[s, pl.ds(16, 48)], o_ref.at[s, pl.ds(16, 48)], wsem.at[s, 0])

    def side(s):
        rows, cols = pl.ds(0, 16), pl.ds(1024, 3072)
        return pltpu.make_async_copy(fine_ref.at[s, rows, cols], o_ref.at[s, rows, cols], wsem.at[s, 1])

    def corner_out(s):
        return pltpu.make_async_copy(ctx_ref.at[s], o_ref.at[s, pl.ds(0, 16), pl.ds(0, 1024)], wsem.at[s, 2])

    def zeros(s):
        return pltpu.make_async_copy(zero_ref, o_ref.at[s], wsem.at[s, 0])

    for s in range(SLOTS):

        @pl.when(s < count)
        def _(s=s):
            body(s).start()
            side(s).start()

    krow = lax.broadcasted_iota(jnp.int32, (16, 128), 0)
    klane = lax.broadcasted_iota(jnp.int32, (16, 128), 1)
    owner = lax.rem(node - krow + 16, 16) * 16 + klane
    start = jnp.sum(jnp.where((klane < 16) & (owner < me), tab_ref[...], 0))
    first = start // 8

    def count_of(t):
        return tabs_ref[lax.rem(node - t // 16 + 16, 16), lax.rem(t, 16)]

    for s in range(SLOTS):
        h_ref[7 + s] = lpf_ref[s]
    after = 7 + count
    before = 7
    for o in range(1, 8):
        n, b = HALO[o - 1], HBASE[o - 1]
        for s in range(n):
            h_ref[jnp.minimum(after + s, 24)] = fw_ref[b + s]
        for s in range(n):
            p = before - n + s
            h_ref[jnp.where(p < 0, 25, p)] = bw_ref[b + s]
        after = after + count_of(lax.rem(me + o, 256))
        before = before - count_of(lax.rem(me - o + 256, 256))

    lane = lax.broadcasted_iota(jnp.int32, (8, 128), 1)
    base = 7 + first * 8 - start
    hs, ls = [], []
    for q in range(2):
        groups = []
        for c1 in range(2):
            for jh in range(2):
                for c2 in range(2):
                    c = 2 * c1 + 4 * c2
                    at = base + 8 * q + c
                    groups.append(jnp.concatenate([h_ref[at, 16 * jh : 16 * jh + 16], h_ref[at + 1, 16 * jh : 16 * jh + 16]], 0))
        y = left_dot(t1_ref[...], jnp.concatenate(groups, 1))
        hi, lo = split(y)
        for g in range(4):
            hs.append(hi[:, 256 * g : 256 * g + 256])
            ls.append(lo[:, 256 * g : 256 * g + 256])
    y = right_dot(jnp.concatenate(hs, 0), jnp.concatenate(ls, 0), w1_ref[...])
    last, firstm = (lane // 16) % 4 == 3, (lane // 16) % 4 == 0
    low = lane < 64
    corners = []
    for q in range(2):
        halves = []
        for r in range(4):
            at = [128 * q + 32 * g + 8 * r for g in range(4)]
            s = [y[a : a + 8, :128] for a in at]
            e = [y[a : a + 8, 128:] for a in at]
            s, e = lift_quarters(s, e, last, firstm)
            for g in range(4):
                res_ref[q, r // 2, 0, g, 8 * (r % 2) : 8 * (r % 2) + 8] = s[g]
                res_ref[q, r // 2, 1, g, 8 * (r % 2) : 8 * (r % 2) + 8] = e[g]
            if r < 2:
                halves.append(
                    jnp.concatenate([jnp.where(low, s[0], pltpu.roll(s[1], 64, 1)), jnp.where(low, s[2], pltpu.roll(s[3], 64, 1))], 1)
                )
        corners.append(jnp.concatenate(halves, 0))
    y = left_dot(t2_ref[...], jnp.concatenate(corners, 1))
    hi, lo = split(y)
    y = right_dot(
        jnp.concatenate([hi[:, :256], hi[:, 256:]], 0), jnp.concatenate([lo[:, :256], lo[:, 256:]], 0), w2_ref[...]
    )
    deep = (lane & 15) < 8
    for q in range(2):
        for r in range(2):
            a = 24 * q + 8 * r
            v0, v1 = y[a : a + 8, :128], y[a : a + 8, 128:256]
            if r == 0:
                v0 = jnp.where(deep, y[24 * q + 16 : 24 * q + 24, 256:], v0)
            rows = slice(8 * r, 8 * r + 8)
            for g, v in enumerate([v0, pltpu.roll(v0, 64, 1), v1, pltpu.roll(v1, 64, 1)]):
                res_ref[q, 0, 0, g, rows] = jnp.where(low, v, res_ref[q, 0, 0, g, rows])
    for s in range(SLOTS):

        @pl.when(s < count)
        def _(s=s):
            block = start + s
            q = block // 8 - first
            c0, c1, c2 = lax.rem(block, 2), lax.rem(block // 2, 2), lax.rem(block // 4, 2)
            for r in range(2):
                rows = slice(8 * r, 8 * r + 8)
                for g in range(4):
                    v = res_ref[q, c0, c1, g, rows]
                    v = jnp.where(c2 == 1, pltpu.roll(v, 64, 1), v)
                    for mh in range(2):
                        cols = slice(256 * g + 128 * mh, 256 * g + 128 * mh + 128)
                        left = pltpu.roll(v, 96, 1) if mh else v
                        right = pltpu.roll(v, 16 if mh else 48, 1)
                        old = fine_ref[s, rows, cols]
                        new = jnp.where(lane < 16, left, jnp.where((lane >= 64) & (lane < 80), right, old))
                        ctx_ref[s, rows, cols] = new
            corner_out(s).start()

    @pl.when(count < SLOTS)
    def _():
        zero_ref[...] = jnp.zeros_like(zero_ref)

    for s in range(1, SLOTS):

        @pl.when(s >= count)
        def _(s=s):
            zeros(s).start()

    for s in range(SLOTS):

        @pl.when(s < count)
        def _(s=s):
            body(s).wait()
            side(s).wait()
            corner_out(s).wait()

        @pl.when(s >= count)
        def _(s=s):
            zeros(s).wait()


def coarse_call(fine, lpf, fw, bw, tab):
    t1, w1, t2, w2 = left_const(lift_matrix(32)), coarse_right(), corner_left(), corner_right()
    vmem = pl.BlockSpec(memory_space=pltpu.VMEM)
    dma = pltpu.SemaphoreType.DMA
    return pl.pallas_call(
        coarse_kernel,
        in_specs=[pl.BlockSpec(memory_space=pltpu.SMEM)] + [vmem] * 9,
        out_specs=pl.BlockSpec(memory_space=pl.ANY),
        out_shape=jax.ShapeDtypeStruct(fine.shape, F32),
        scratch_shapes=[
            pltpu.VMEM((32, 32, 128), F32),
            pltpu.VMEM((SLOTS, 16, 1024), F32),
            pltpu.VMEM((2, 2, 2, 4, 16, 128), F32),
            pltpu.VMEM((64, 4096), F32),
            dma((SLOTS, 3)),
        ],
        compiler_params=pltpu.CompilerParams(vmem_limit_bytes=16 << 20),
        name="coarse",
    )(tab, lpf, fw, bw, tab, jnp.asarray(t1), jnp.asarray(w1), jnp.asarray(t2), jnp.asarray(w2), fine)


def per_device(density, counts):
    fine, lpf, fw, bw, tab = fine_call(density, counts)
    return coarse_call(fine, lpf, fw, bw, tab)


def solution(mesh):
    in_specs = (P(("node", "dev"), None, None), P(("node", "dev")))
    out_specs = P(("node", "dev"), None, None)
    return jax.shard_map(per_device, mesh=mesh, in_specs=in_specs, out_specs=out_specs, check_vma=False)
```

```python
import functools

import jax
import jax.numpy as jnp
import ml_dtypes
import numpy as np
from jax import lax
from jax.experimental import pallas as pl
from jax.experimental.pallas import tpu as pltpu
from jax.sharding import PartitionSpec as P

MESH = pl.DeviceIdType.MESH
F32 = jnp.float32
BF16 = jnp.bfloat16

A_LIFT = -1.586134342059924
B_LIFT = -0.052980118572961
C_LIFT = 0.882911075530934
D_LIFT = 0.443506852043971
K_LIFT = 1.230174104914001
A_SC = A_LIFT * K_LIFT * K_LIFT
B_SC = B_LIFT / (K_LIFT * K_LIFT)
C_SC = C_LIFT * K_LIFT * K_LIFT
D_SC = D_LIFT / (K_LIFT * K_LIFT)

SLOTS = 6
HALO = (6, 6, 5, 4, 3, 2, 1)
HBASE = (0, 6, 12, 17, 21, 24, 26)
HTOTAL = 27


def lift_matrix(n):
    x = np.eye(n)
    s, e = x[0::2].copy(), x[1::2].copy()

    def up(v):
        return np.concatenate([v[1:], v[-1:]], 0)

    def down(v):
        return np.concatenate([v[:1], v[:-1]], 0)

    e = e + A_LIFT * (s + up(s))
    s = s + B_LIFT * (down(e) + e)
    e = e + C_LIFT * (s + up(s))
    s = s + D_LIFT * (down(e) + e)
    return np.concatenate([s / K_LIFT, e * K_LIFT], 0)


def split_const(m):
    hi = m.astype(ml_dtypes.bfloat16)
    lo = (m - hi.astype(np.float64)).astype(ml_dtypes.bfloat16)
    return hi, lo


def left_const(m):
    hi, lo = split_const(m)
    return np.concatenate([hi, lo, hi], 1)


def right_const(m):
    hi, lo = split_const(m)
    return np.concatenate([hi, lo, hi], 0)


def fine_right(n):
    t = lift_matrix(n)
    w = np.zeros((256, 256))
    for q in range(2):
        for par in range(2):
            r = 128 * q + 64 * par
            c = 128 * par + 64 * q
            w[r : r + n, c : c + n] = t.T * (K_LIFT if par else 1.0 / K_LIFT)
    return right_const(w)


def coarse_right():
    t = lift_matrix(32)
    w = np.zeros((256, 256))
    for j in range(8):
        for k2 in range(2):
            for kb in range(2):
                r = 128 * k2 + 16 * j
                c = 128 * (j % 2) + 64 * kb + 16 * (j // 2)
                scale = K_LIFT if j % 2 else 1.0 / K_LIFT
                w[r : r + 16, c : c + 16] = t[16 * kb : 16 * kb + 16, 16 * k2 : 16 * k2 + 16].T * scale
    return right_const(w)


def corner_left():
    t16, t8 = lift_matrix(16), lift_matrix(8)
    return left_const(np.concatenate([t16, t8 @ t16[:8]], 0))


def corner_right():
    t16, t8 = lift_matrix(16), lift_matrix(8)
    second = np.kron(t16, t16).T
    low = t8 @ t16[:8]
    both = np.zeros((256, 128))
    for j in range(8):
        for k in range(8):
            both[:, 16 * j + k] = np.kron(low[j], low[k])
    return right_const(np.concatenate([second, both], 1))


def split(x):
    hi = x.astype(BF16)
    lo = (x - hi.astype(F32)).astype(BF16)
    return hi, lo


def left_dot(t, x):
    hi, lo = split(x)
    return jnp.dot(t, jnp.concatenate([hi, hi, lo], 0), preferred_element_type=F32)


def right_dot(hi, lo, w):
    return jnp.dot(jnp.concatenate([hi, hi, lo], 1), w, preferred_element_type=F32)


def lift_lanes(s, e, mask, up, down):
    n = len(s)
    sp = up(s)
    e = [e[g] + A_SC * (s[g] + sp[g]) for g in range(n)]
    em = down(e)
    s = [s[g] + B_SC * (em[g] + e[g]) for g in range(n)]
    sp = up(s)
    e = [e[g] + C_SC * (s[g] + sp[g]) for g in range(n)]
    em = down(e)
    s = [s[g] + D_SC * (em[g] + e[g]) for g in range(n)]
    return s, e


def lift_halves(s, e, low):
    n = len(s)

    def up(v):
        r = [pltpu.roll(x, 64, 1) for x in v]
        return [jnp.where(low, r[g], r[g + 1] if g + 1 < n else v[g]) for g in range(n)]

    def down(v):
        r = [pltpu.roll(x, 64, 1) for x in v]
        return [jnp.where(low, r[g - 1] if g else v[g], r[g]) for g in range(n)]

    return lift_lanes(s, e, low, up, down)


def lift_quarters(s, e, last, first):
    n = len(s)

    def up(v):
        out = []
        for g in range(n):
            near = pltpu.roll(v[g], 112, 1)
            far = pltpu.roll(v[g + 1], 48, 1) if g + 1 < n else v[g]
            out.append(jnp.where(last, far, near))
        return out

    def down(v):
        out = []
        for g in range(n):
            near = pltpu.roll(v[g], 16, 1)
            far = pltpu.roll(v[g - 1], 80, 1) if g else v[g]
            out.append(jnp.where(first, far, near))
        return out

    return lift_lanes(s, e, last, up, down)


def lift_stream(load_s, load_e, n, emit):
    s0, e1, s1, e2 = load_s(0), None, None, None
    for i in range(n):
        s_next = load_s(i + 1) if i + 1 < n else s0
        e1_new = load_e(i) + A_SC * (s0 + s_next)
        s1_new = s0 + B_SC * ((e1 if i else e1_new) + e1_new)
        if i:
            e2_new = e1 + C_SC * (s1 + s1_new)
            emit(i - 1, s1 + D_SC * ((e2 if i > 1 else e2_new) + e2_new), e2_new)
            e2 = e2_new
        s0, e1, s1 = s_next, e1_new, s1_new
    e2_new = e1 + C_SC * (s1 + s1)
    emit(n - 1, s1 + D_SC * (e2 + e2_new), e2_new)


def fine_kernel(
    count_ref, x_ref, wc_ref, t1c_ref, t2c_ref, o_ref, lpf_ref, fw_ref, bw_ref, tab_ref,
    lpb_ref, w_ref, t1_ref, t2_ref, xv_ref, ah_ref, al_ref, se_ref, cv_ref, a_ref, row_ref, b_ref,
    xsem, wsem, dsend, drecv, csend, crecv,
):
    node, dev = lax.axis_index("node"), lax.axis_index("dev")
    me = node * 16 + dev
    count = count_ref[0]
    lane = lax.broadcasted_iota(jnp.int32, (16, 128), 1)
    low = lane < 64
    corner = (lane & 63) < 32

    def load_x(s):
        return pltpu.make_async_copy(x_ref.at[s], xv_ref.at[s], xsem.at[s])

    constants = [(wc_ref, w_ref), (t1c_ref, t1_ref), (t2c_ref, t2_ref)]
    load_c = [pltpu.make_async_copy(a, b, wsem.at[i]) for i, (a, b) in enumerate(constants)]
    load_x(0).start()
    for c in load_c:
        c.start()
    load_x(1).start()

    barrier = pltpu.get_barrier_semaphore()

    def by_offset(step):
        t = lax.rem(me + step + 256, 256)
        return {"node": t // 16, "dev": lax.rem(t, 16)}

    def by_dev(k):
        return {"node": node, "dev": lax.rem(dev + k, 16)}

    def by_node(k):
        return {"node": lax.rem(node + k, 16), "dev": dev}

    partners = [by_offset(o) for o in range(1, 8)] + [by_offset(-o) for o in range(1, 8)]
    partners += [by_dev(k) for k in range(1, 16)] + [by_node(k) for k in range(1, 16)]
    for p in partners:
        pl.semaphore_signal(barrier, inc=1, device_id=p, device_id_type=MESH)
    cv_ref[...] = jnp.zeros_like(cv_ref) + count

    def remote(src, dst, send, recv, to):
        return pltpu.make_async_remote_copy(
            src_ref=src, dst_ref=dst, send_sem=send, recv_sem=recv, device_id=to, device_id_type=MESH
        )

    def stage(src, dst, i, to):
        for k in range(1, 16):
            remote(src, dst.at[k], csend.at[i], crecv.at[i], to(k)).start()

    def stage_wait(dst, i):
        c = remote(dst.at[pl.ds(1, 15)], dst.at[pl.ds(1, 15)], csend.at[i], crecv.at[i], by_dev(1))
        c.wait_send()
        c.wait_recv()

    def forward(o):
        n, b = HALO[o - 1], HBASE[o - 1]
        return remote(lpf_ref.at[pl.ds(0, n)], fw_ref.at[pl.ds(b, n)], dsend.at[0, o], drecv.at[0, o], by_offset(-o))

    def backward(o):
        n, b = HALO[o - 1], HBASE[o - 1]
        return remote(lpb_ref.at[pl.ds(SLOTS - n, n)], bw_ref.at[pl.ds(b, n)], dsend.at[1, o], drecv.at[1, o], by_offset(o))

    def rows_dot(t, hi, lo, g):
        y = jnp.dot(t, jnp.concatenate([hi, hi, lo], 0), preferred_element_type=F32)
        hi, lo = split(y)
        for nn in range(2):
            to = slice((2 * g + nn) * 16, (2 * g + nn) * 16 + 16)
            cols = slice(128 * nn, 128 * nn + 128)
            for q in range(2):
                ah_ref[to, 128 * q : 128 * q + 128] = hi[16 * q : 16 * q + 16, cols]
                al_ref[to, 128 * q : 128 * q + 128] = lo[16 * q : 16 * q + 16, cols]

    def columns(n, w, store, keep):
        rows = slice(0, 16 * n)
        se_ref[rows] = right_dot(ah_ref[rows], al_ref[rows], w_ref[w])
        held = {}

        def emit(i, s, e):
            keep(s)
            if i % 2 == 0:
                held[0] = (s, e)
                return
            for band, (x0, x1) in enumerate(zip(held[0], (s, e))):
                r0, r1 = pltpu.roll(x0, 64, 1), pltpu.roll(x1, 64, 1)
                store(0, band, i // 2, jnp.where(low, x0, r1))
                store(16, band, i // 2, jnp.where(low, r0, x1))

        lift_stream(lambda i: se_ref[16 * i : 16 * i + 16, :128], lambda i: se_ref[16 * i : 16 * i + 16, 128:], n, emit)

    def first_pass(slot, carry):
        load_x(slot).wait()

        @pl.when(slot < SLOTS - 2)
        def _():
            load_x(slot + 2).start()

        @pl.when(slot == 0)
        def _():
            for c in load_c:
                c.wait()

        for g in range(16):
            cols = slice(256 * g, 256 * g + 256)
            rows_dot(t1_ref[:32], *split(xv_ref[slot, :, cols]), g)

        def store1(row, band, u, v):
            o_ref[slot, row : row + 16, 2048 * band + 128 * u : 2048 * band + 128 * u + 128] = v

        columns(32, 0, store1, lambda s: None)
        for h in range(8):
            hi, lo = split(o_ref[slot, :32, 256 * h : 256 * h + 256])
            rows_dot(t2_ref[...], hi, lo, h)
        kept = []

        def store2(row, band, u, v):
            at = (slot, slice(row, row + 16), slice(1024 * band + 128 * u, 1024 * band + 128 * u + 128))
            o_ref[at] = jnp.where(corner, v, o_ref[at])

        columns(16, 1, store2, kept.append)
        for half in range(2):
            packed = kept[8 * half]
            for jl in range(1, 8):
                packed = jnp.where((lane >> 4) == jl, pltpu.roll(kept[8 * half + jl], 16 * jl, 1), packed)
            lpf_ref[slot, 16 * half : 16 * half + 16] = packed

        @pl.when(slot == 3)
        def _():
            pl.semaphore_wait(barrier, len(partners))
            stage(cv_ref, a_ref, 0, by_dev)

        @pl.when(slot == 5)
        def _():
            stage_wait(a_ref, 0)
            row = jnp.where(lane[:8] == dev, cv_ref[...], 0)
            for k in range(1, 16):
                row = jnp.where(lane[:8] == lax.rem(dev - k + 16, 16), a_ref[k], row)
            row_ref[...] = row
            stage(row_ref, b_ref, 1, by_node)

        return carry

    lax.fori_loop(0, SLOTS, first_pass, 0)
    for s in range(SLOTS):
        lpb_ref[s] = lpf_ref[jnp.maximum(count - SLOTS + s, 0)]
    for o in range(1, 8):
        backward(o).start()
        forward(o).start()

    def second_pass(slot, carry):
        for g in range(16):
            cols = slice(256 * g, 256 * g + 256)
            rows_dot(t1_ref[32:], *split(xv_ref[slot, :, cols]), g)

        def store1(row, band, u, v):
            o_ref[slot, 32 + row : 48 + row, 2048 * band + 128 * u : 2048 * band + 128 * u + 128] = v

        columns(32, 0, store1, lambda s: None)
        return carry

    lax.fori_loop(0, SLOTS, second_pass, 0)
    stage_wait(b_ref, 1)
    tab_ref[0:1] = row_ref[0:1]
    for k in range(1, 16):
        tab_ref[k : k + 1] = b_ref[k][0:1]
    for o in range(1, 8):
        forward(o).wait()
        backward(o).wait()


def fine_call(density, counts):
    t1, t2 = left_const(lift_matrix(64)), left_const(lift_matrix(32))
    w = np.stack([fine_right(64), fine_right(32)])
    vmem = pl.BlockSpec(memory_space=pltpu.VMEM)
    hbm = pl.BlockSpec(memory_space=pltpu.HBM)
    dma = pltpu.SemaphoreType.DMA
    return pl.pallas_call(
        fine_kernel,
        in_specs=[pl.BlockSpec(memory_space=pltpu.SMEM)] + [hbm] * 4,
        out_specs=[vmem] * 5,
        out_shape=[
            jax.ShapeDtypeStruct(density.shape, F32),
            jax.ShapeDtypeStruct((SLOTS, 32, 128), F32),
            jax.ShapeDtypeStruct((HTOTAL, 32, 128), F32),
            jax.ShapeDtypeStruct((HTOTAL, 32, 128), F32),
            jax.ShapeDtypeStruct((16, 128), jnp.int32),
        ],
        scratch_shapes=[
            pltpu.VMEM((SLOTS, 32, 128), F32),
            pltpu.VMEM(w.shape, BF16),
            pltpu.VMEM(t1.shape, BF16),
            pltpu.VMEM(t2.shape, BF16),
            pltpu.VMEM((SLOTS, 64, 4096), F32),
            pltpu.VMEM((512, 256), BF16),
            pltpu.VMEM((512, 256), BF16),
            pltpu.VMEM((512, 256), F32),
            pltpu.VMEM((8, 128), jnp.int32),
            pltpu.VMEM((16, 8, 128), jnp.int32),
            pltpu.VMEM((8, 128), jnp.int32),
            pltpu.VMEM((16, 8, 128), jnp.int32),
            dma((SLOTS,)),
            dma((3,)),
            dma((2, 8)),
            dma((2, 8)),
            dma((2,)),
            dma((2,)),
        ],
        compiler_params=pltpu.CompilerParams(collective_id=0, has_side_effects=True, vmem_limit_bytes=30 << 20),
        name="fine",
    )(counts, *[pltpu.with_memory_space_constraint(jnp.asarray(a), pltpu.HBM) for a in (density, w, t1, t2)])


def coarse_kernel(tabs_ref, lpf_ref, fw_ref, bw_ref, tab_ref, t1_ref, w1_ref, t2_ref, w2_ref, fine_ref, o_ref, h_ref, ctx_ref, res_ref, zero_ref, wsem):
    node, dev = lax.axis_index("node"), lax.axis_index("dev")
    me = node * 16 + dev
    count = tabs_ref[0, dev]

    def body(s):
        return pltpu.make_async_copy(fine_ref.at[s, pl.ds(16, 48)], o_ref.at[s, pl.ds(16, 48)], wsem.at[s, 0])

    def side(s):
        rows, cols = pl.ds(0, 16), pl.ds(1024, 3072)
        return pltpu.make_async_copy(fine_ref.at[s, rows, cols], o_ref.at[s, rows, cols], wsem.at[s, 1])

    def corner_out(s):
        return pltpu.make_async_copy(ctx_ref.at[s], o_ref.at[s, pl.ds(0, 16), pl.ds(0, 1024)], wsem.at[s, 2])

    def zeros(s):
        return pltpu.make_async_copy(zero_ref, o_ref.at[s], wsem.at[s, 0])

    for s in range(SLOTS):

        @pl.when(s < count)
        def _(s=s):
            body(s).start()
            side(s).start()

    krow = lax.broadcasted_iota(jnp.int32, (16, 128), 0)
    klane = lax.broadcasted_iota(jnp.int32, (16, 128), 1)
    owner = lax.rem(node - krow + 16, 16) * 16 + klane
    start = jnp.sum(jnp.where((klane < 16) & (owner < me), tab_ref[...], 0))
    first = start // 8

    def count_of(t):
        return tabs_ref[lax.rem(node - t // 16 + 16, 16), lax.rem(t, 16)]

    for s in range(SLOTS):
        h_ref[7 + s] = lpf_ref[s]
    after = 7 + count
    before = 7
    for o in range(1, 8):
        n, b = HALO[o - 1], HBASE[o - 1]
        for s in range(n):
            h_ref[jnp.minimum(after + s, 24)] = fw_ref[b + s]
        for s in range(n):
            p = before - n + s
            h_ref[jnp.where(p < 0, 25, p)] = bw_ref[b + s]
        after = after + count_of(lax.rem(me + o, 256))
        before = before - count_of(lax.rem(me - o + 256, 256))

    lane = lax.broadcasted_iota(jnp.int32, (8, 128), 1)
    base = 7 + first * 8 - start
    hs, ls = [], []
    for q in range(2):
        groups = []
        for c1 in range(2):
            for jh in range(2):
                for c2 in range(2):
                    c = 2 * c1 + 4 * c2
                    at = base + 8 * q + c
                    groups.append(jnp.concatenate([h_ref[at, 16 * jh : 16 * jh + 16], h_ref[at + 1, 16 * jh : 16 * jh + 16]], 0))
        y = left_dot(t1_ref[...], jnp.concatenate(groups, 1))
        hi, lo = split(y)
        for g in range(4):
            hs.append(hi[:, 256 * g : 256 * g + 256])
            ls.append(lo[:, 256 * g : 256 * g + 256])
    y = right_dot(jnp.concatenate(hs, 0), jnp.concatenate(ls, 0), w1_ref[...])
    last, firstm = (lane // 16) % 4 == 3, (lane // 16) % 4 == 0
    low = lane < 64
    corners = []
    for q in range(2):
        halves = []
        for r in range(4):
            at = [128 * q + 32 * g + 8 * r for g in range(4)]
            s = [y[a : a + 8, :128] for a in at]
            e = [y[a : a + 8, 128:] for a in at]
            s, e = lift_quarters(s, e, last, firstm)
            for g in range(4):
                res_ref[q, r // 2, 0, g, 8 * (r % 2) : 8 * (r % 2) + 8] = s[g]
                res_ref[q, r // 2, 1, g, 8 * (r % 2) : 8 * (r % 2) + 8] = e[g]
            if r < 2:
                halves.append(
                    jnp.concatenate([jnp.where(low, s[0], pltpu.roll(s[1], 64, 1)), jnp.where(low, s[2], pltpu.roll(s[3], 64, 1))], 1)
                )
        corners.append(jnp.concatenate(halves, 0))
    y = left_dot(t2_ref[...], jnp.concatenate(corners, 1))
    hi, lo = split(y)
    y = right_dot(
        jnp.concatenate([hi[:, :256], hi[:, 256:]], 0), jnp.concatenate([lo[:, :256], lo[:, 256:]], 0), w2_ref[...]
    )
    deep = (lane & 15) < 8
    for q in range(2):
        for r in range(2):
            a = 24 * q + 8 * r
            v0, v1 = y[a : a + 8, :128], y[a : a + 8, 128:256]
            if r == 0:
                v0 = jnp.where(deep, y[24 * q + 16 : 24 * q + 24, 256:], v0)
            rows = slice(8 * r, 8 * r + 8)
            for g, v in enumerate([v0, pltpu.roll(v0, 64, 1), v1, pltpu.roll(v1, 64, 1)]):
                res_ref[q, 0, 0, g, rows] = jnp.where(low, v, res_ref[q, 0, 0, g, rows])
    for s in range(SLOTS):

        @pl.when(s < count)
        def _(s=s):
            block = start + s
            q = block // 8 - first
            c0, c1, c2 = lax.rem(block, 2), lax.rem(block // 2, 2), lax.rem(block // 4, 2)
            for r in range(2):
                rows = slice(8 * r, 8 * r + 8)
                for g in range(4):
                    v = res_ref[q, c0, c1, g, rows]
                    v = jnp.where(c2 == 1, pltpu.roll(v, 64, 1), v)
                    for mh in range(2):
                        cols = slice(256 * g + 128 * mh, 256 * g + 128 * mh + 128)
                        left = pltpu.roll(v, 96, 1) if mh else v
                        right = pltpu.roll(v, 16 if mh else 48, 1)
                        old = fine_ref[s, rows, cols]
                        new = jnp.where(lane < 16, left, jnp.where((lane >= 64) & (lane < 80), right, old))
                        ctx_ref[s, rows, cols] = new
            corner_out(s).start()

    @pl.when(count < SLOTS)
    def _():
        zero_ref[...] = jnp.zeros_like(zero_ref)

    for s in range(1, SLOTS):

        @pl.when(s >= count)
        def _(s=s):
            zeros(s).start()

    for s in range(SLOTS):

        @pl.when(s < count)
        def _(s=s):
            body(s).wait()
            side(s).wait()
            corner_out(s).wait()

        @pl.when(s >= count)
        def _(s=s):
            zeros(s).wait()


def coarse_call(fine, lpf, fw, bw, tab):
    t1, w1, t2, w2 = left_const(lift_matrix(32)), coarse_right(), corner_left(), corner_right()
    vmem = pl.BlockSpec(memory_space=pltpu.VMEM)
    dma = pltpu.SemaphoreType.DMA
    return pl.pallas_call(
        coarse_kernel,
        in_specs=[pl.BlockSpec(memory_space=pltpu.SMEM)] + [vmem] * 9,
        out_specs=pl.BlockSpec(memory_space=pl.ANY),
        out_shape=jax.ShapeDtypeStruct(fine.shape, F32),
        scratch_shapes=[
            pltpu.VMEM((32, 32, 128), F32),
            pltpu.VMEM((SLOTS, 16, 1024), F32),
            pltpu.VMEM((2, 2, 2, 4, 16, 128), F32),
            pltpu.VMEM((64, 4096), F32),
            dma((SLOTS, 3)),
        ],
        compiler_params=pltpu.CompilerParams(vmem_limit_bytes=16 << 20),
        name="coarse",
    )(tab, lpf, fw, bw, tab, jnp.asarray(t1), jnp.asarray(w1), jnp.asarray(t2), jnp.asarray(w2), fine)


def per_device(density, counts):
    fine, lpf, fw, bw, tab = fine_call(density, counts)
    return coarse_call(fine, lpf, fw, bw, tab)


def solution(mesh):
    in_specs = (P(("node", "dev"), None, None), P(("node", "dev")))
    out_specs = P(("node", "dev"), None, None)
    return jax.shard_map(per_device, mesh=mesh, in_specs=in_specs, out_specs=out_specs, check_vma=False)
```

```python
import functools

import jax
import jax.numpy as jnp
import ml_dtypes
import numpy as np
from jax import lax
from jax.experimental import pallas as pl
from jax.experimental.pallas import tpu as pltpu
from jax.sharding import PartitionSpec as P

MESH = pl.DeviceIdType.MESH
F32 = jnp.float32
BF16 = jnp.bfloat16

A_LIFT = -1.586134342059924
B_LIFT = -0.052980118572961
C_LIFT = 0.882911075530934
D_LIFT = 0.443506852043971
K_LIFT = 1.230174104914001
A_SC = A_LIFT * K_LIFT * K_LIFT
B_SC = B_LIFT / (K_LIFT * K_LIFT)
C_SC = C_LIFT * K_LIFT * K_LIFT
D_SC = D_LIFT / (K_LIFT * K_LIFT)

SLOTS = 6
HALO = (6, 6, 5, 4, 3, 2, 1)
HBASE = (0, 6, 12, 17, 21, 24, 26)
HTOTAL = 27


def lift_matrix(n):
    x = np.eye(n)
    s, e = x[0::2].copy(), x[1::2].copy()

    def up(v):
        return np.concatenate([v[1:], v[-1:]], 0)

    def down(v):
        return np.concatenate([v[:1], v[:-1]], 0)

    e = e + A_LIFT * (s + up(s))
    s = s + B_LIFT * (down(e) + e)
    e = e + C_LIFT * (s + up(s))
    s = s + D_LIFT * (down(e) + e)
    return np.concatenate([s / K_LIFT, e * K_LIFT], 0)


def split_const(m):
    hi = m.astype(ml_dtypes.bfloat16)
    lo = (m - hi.astype(np.float64)).astype(ml_dtypes.bfloat16)
    return hi, lo


def left_const(m):
    hi, lo = split_const(m)
    return np.concatenate([hi, lo, hi], 1)


def right_const(m):
    hi, lo = split_const(m)
    return np.concatenate([hi, lo, hi], 0)


def fine_right(n):
    t = lift_matrix(n)
    w = np.zeros((256, 256))
    for q in range(2):
        for par in range(2):
            r = 128 * q + 64 * par
            c = 128 * par + 64 * q
            w[r : r + n, c : c + n] = t.T * (K_LIFT if par else 1.0 / K_LIFT)
    return right_const(w)


def low_rows():
    return lift_matrix(32)[:16] @ lift_matrix(64)[:32]


def low_right():
    return right_const(np.kron(np.eye(4), low_rows().T) @ np.kron(np.ones((1, 2)), np.eye(64)))


def low_mid():
    return np.stack(split_const(np.kron(low_rows().T, np.eye(16))))


def coarse_right():
    t = lift_matrix(32)
    w = np.zeros((256, 256))
    for j in range(8):
        for k2 in range(2):
            for kb in range(2):
                r = 128 * k2 + 16 * j
                c = 128 * (j % 2) + 64 * kb + 16 * (j // 2)
                scale = K_LIFT if j % 2 else 1.0 / K_LIFT
                w[r : r + 16, c : c + 16] = t[16 * kb : 16 * kb + 16, 16 * k2 : 16 * k2 + 16].T * scale
    return right_const(w)


def corner_left():
    t16, t8 = lift_matrix(16), lift_matrix(8)
    return left_const(np.concatenate([t16, t8 @ t16[:8]], 0))


def corner_right():
    t16, t8 = lift_matrix(16), lift_matrix(8)
    second = np.kron(t16, t16).T
    low = t8 @ t16[:8]
    both = np.zeros((256, 128))
    for j in range(8):
        for k in range(8):
            both[:, 16 * j + k] = np.kron(low[j], low[k])
    return right_const(np.concatenate([second, both], 1))


def split(x):
    hi = x.astype(BF16)
    lo = (x - hi.astype(F32)).astype(BF16)
    return hi, lo


def left_dot(t, x):
    hi, lo = split(x)
    return jnp.dot(t, jnp.concatenate([hi, hi, lo], 0), preferred_element_type=F32)


def right_dot(hi, lo, w):
    return jnp.dot(jnp.concatenate([hi, hi, lo], 1), w, preferred_element_type=F32)


def lift_lanes(s, e, mask, up, down):
    n = len(s)
    sp = up(s)
    e = [e[g] + A_SC * (s[g] + sp[g]) for g in range(n)]
    em = down(e)
    s = [s[g] + B_SC * (em[g] + e[g]) for g in range(n)]
    sp = up(s)
    e = [e[g] + C_SC * (s[g] + sp[g]) for g in range(n)]
    em = down(e)
    s = [s[g] + D_SC * (em[g] + e[g]) for g in range(n)]
    return s, e


def lift_halves(s, e, low):
    n = len(s)

    def up(v):
        r = [pltpu.roll(x, 64, 1) for x in v]
        return [jnp.where(low, r[g], r[g + 1] if g + 1 < n else v[g]) for g in range(n)]

    def down(v):
        r = [pltpu.roll(x, 64, 1) for x in v]
        return [jnp.where(low, r[g - 1] if g else v[g], r[g]) for g in range(n)]

    return lift_lanes(s, e, low, up, down)


def lift_quarters(s, e, last, first):
    n = len(s)

    def up(v):
        out = []
        for g in range(n):
            near = pltpu.roll(v[g], 112, 1)
            far = pltpu.roll(v[g + 1], 48, 1) if g + 1 < n else v[g]
            out.append(jnp.where(last, far, near))
        return out

    def down(v):
        out = []
        for g in range(n):
            near = pltpu.roll(v[g], 16, 1)
            far = pltpu.roll(v[g - 1], 80, 1) if g else v[g]
            out.append(jnp.where(first, far, near))
        return out

    return lift_lanes(s, e, last, up, down)


def lift_stream(load_s, load_e, n, emit):
    s0, e1, s1, e2 = load_s(0), None, None, None
    for i in range(n):
        s_next = load_s(i + 1) if i + 1 < n else s0
        e1_new = load_e(i) + A_SC * (s0 + s_next)
        s1_new = s0 + B_SC * ((e1 if i else e1_new) + e1_new)
        if i:
            e2_new = e1 + C_SC * (s1 + s1_new)
            emit(i - 1, s1 + D_SC * ((e2 if i > 1 else e2_new) + e2_new), e2_new)
            e2 = e2_new
        s0, e1, s1 = s_next, e1_new, s1_new
    e2_new = e1 + C_SC * (s1 + s1)
    emit(n - 1, s1 + D_SC * (e2 + e2_new), e2_new)


def fine_kernel(
    count_ref, x_ref, wc_ref, t1c_ref, t2c_ref, tlc_ref, wlc_ref, wmc_ref, o_ref, lpf_ref, fw_ref, bw_ref, tab_ref,
    lpb_ref, w_ref, t1_ref, t2_ref, tl_ref, wl_ref, wm_ref, xv_ref, ah_ref, al_ref, se_ref, zh_ref, zl_ref, cv_ref, a_ref, row_ref, b_ref,
    xsem, wsem, dsend, drecv, csend, crecv,
):
    node, dev = lax.axis_index("node"), lax.axis_index("dev")
    me = node * 16 + dev
    count = count_ref[0]
    lane = lax.broadcasted_iota(jnp.int32, (32, 128), 1)
    low = lane < 64
    corner = (lane[:16] & 63) < 32

    def load_x(s):
        return pltpu.make_async_copy(x_ref.at[s], xv_ref.at[s], xsem.at[s])

    constants = [(tlc_ref, tl_ref), (wlc_ref, wl_ref), (wmc_ref, wm_ref), (wc_ref, w_ref), (t1c_ref, t1_ref), (t2c_ref, t2_ref)]
    load_c = [pltpu.make_async_copy(a, b, wsem.at[i]) for i, (a, b) in enumerate(constants)]
    for c in load_c[:2]:
        c.start()
    load_x(0).start()
    load_x(1).start()

    barrier = pltpu.get_barrier_semaphore()

    def by_offset(step):
        t = lax.rem(me + step + 256, 256)
        return {"node": t // 16, "dev": lax.rem(t, 16)}

    def by_dev(k):
        return {"node": node, "dev": lax.rem(dev + k, 16)}

    def by_node(k):
        return {"node": lax.rem(node + k, 16), "dev": dev}

    partners = [by_offset(o) for o in range(1, 8)] + [by_offset(-o) for o in range(1, 8)]
    partners += [by_dev(k) for k in range(1, 16)] + [by_node(k) for k in range(1, 16)]
    for p in partners:
        pl.semaphore_signal(barrier, inc=1, device_id=p, device_id_type=MESH)
    cv_ref[...] = jnp.zeros_like(cv_ref) + count

    def remote(src, dst, send, recv, to):
        return pltpu.make_async_remote_copy(
            src_ref=src, dst_ref=dst, send_sem=send, recv_sem=recv, device_id=to, device_id_type=MESH
        )

    def stage(src, dst, i, to):
        for k in range(1, 16):
            remote(src, dst.at[k], csend.at[i], crecv.at[i], to(k)).start()

    def stage_wait(dst, i):
        c = remote(dst.at[pl.ds(1, 15)], dst.at[pl.ds(1, 15)], csend.at[i], crecv.at[i], by_dev(1))
        c.wait_send()
        c.wait_recv()

    def forward(o):
        n, b = HALO[o - 1], HBASE[o - 1]
        return remote(lpf_ref.at[pl.ds(0, n)], fw_ref.at[pl.ds(b, n)], dsend.at[0, o], drecv.at[0, o], by_offset(-o))

    def backward(o):
        n, b = HALO[o - 1], HBASE[o - 1]
        return remote(lpb_ref.at[pl.ds(SLOTS - n, n)], bw_ref.at[pl.ds(b, n)], dsend.at[1, o], drecv.at[1, o], by_offset(o))

    def low_pass(slot, carry):
        load_x(slot).wait()

        @pl.when(slot < SLOTS - 2)
        def _():
            load_x(slot + 2).start()

        @pl.when(slot == 0)
        def _():
            for c in load_c[:2]:
                c.wait()

        @pl.when(slot == 2)
        def _():
            for c in load_c[2:]:
                c.start()

        for g in range(16):
            y = left_dot(tl_ref[...], xv_ref[slot, :, 256 * g : 256 * g + 256])
            ah_ref[16 * g : 16 * g + 16], al_ref[16 * g : 16 * g + 16] = split(y)
        z = right_dot(ah_ref[:256], al_ref[:256], wl_ref[...])
        rows = pl.ds(slot * 16, 16)
        for g in range(8):
            pair = jnp.where(low[:16], z[32 * g : 32 * g + 16], z[32 * g + 16 : 32 * g + 32])
            cols = slice(128 * g, 128 * g + 128)
            zh_ref[rows, cols], zl_ref[rows, cols] = split(pair)
        return carry

    lax.fori_loop(0, SLOTS, low_pass, 0)
    for c in load_c[2:]:
        c.wait()
    z = right_dot(zh_ref[...], zl_ref[...], jnp.concatenate([wm_ref[0], wm_ref[1], wm_ref[0]], 0))
    for s in range(SLOTS):
        for half in range(2):
            lpf_ref[s, 16 * half : 16 * half + 16] = z[16 * s : 16 * s + 16, 128 * half : 128 * half + 128]
    for s in range(SLOTS):
        lpb_ref[s] = lpf_ref[jnp.maximum(count - SLOTS + s, 0)]
    pl.semaphore_wait(barrier, len(partners))
    stage(cv_ref, a_ref, 0, by_dev)
    for o in (2, 1, 3, 6, 5, 4, 7):
        forward(o).start()
        backward(o).start()

    def rows_dot(t, x, g):
        hi, lo = split(left_dot(t, x))
        parts = t.shape[0] // 32
        for nn in range(2):
            cols = slice(128 * nn, 128 * nn + 128)
            for p in range(parts):
                at = 16 * ((2 * g + nn) * parts + p)
                for q in range(2):
                    rows = slice(32 * p + 16 * q, 32 * p + 16 * q + 16)
                    ah_ref[at : at + 16, 128 * q : 128 * q + 128] = hi[rows, cols]
                    al_ref[at : at + 16, 128 * q : 128 * q + 128] = lo[rows, cols]

    def columns(n, parts, w, store):
        size = 16 * parts
        se_ref[: n * size] = right_dot(ah_ref[: n * size], al_ref[: n * size], w_ref[w])
        held = {}

        def emit(i, s, e):
            if i % 2 == 0:
                held[0] = (s, e)
                return
            for band, (x0, x1) in enumerate(zip(held[0], (s, e))):
                r0, r1 = pltpu.roll(x0, 64, 1), pltpu.roll(x1, 64, 1)
                for q, v in enumerate((jnp.where(low[:size], x0, r1), jnp.where(low[:size], r0, x1))):
                    for p in range(parts):
                        store(32 * p + 16 * q, band, i // 2, v[16 * p : 16 * p + 16])

        lift_stream(
            lambda i: se_ref[size * i : size * i + size, :128], lambda i: se_ref[size * i : size * i + size, 128:], n, emit
        )

    def full_pass(slot, carry):
        for g in range(16):
            rows_dot(t1_ref[...], xv_ref[slot, :, 256 * g : 256 * g + 256], g)

        def store1(row, band, u, v):
            o_ref[slot, row : row + 16, 2048 * band + 128 * u : 2048 * band + 128 * u + 128] = v

        columns(32, 2, 0, store1)
        for h in range(8):
            rows_dot(t2_ref[...], o_ref[slot, :32, 256 * h : 256 * h + 256], h)

        def store2(row, band, u, v):
            at = (slot, slice(row, row + 16), slice(1024 * band + 128 * u, 1024 * band + 128 * u + 128))
            o_ref[at] = jnp.where(corner, v, o_ref[at])

        columns(16, 1, 1, store2)

        @pl.when(slot == 1)
        def _():
            stage_wait(a_ref, 0)
            row = jnp.where(lane[:8] == dev, cv_ref[...], 0)
            for k in range(1, 16):
                row = jnp.where(lane[:8] == lax.rem(dev - k + 16, 16), a_ref[k], row)
            row_ref[...] = row
            stage(row_ref, b_ref, 1, by_node)

        return carry

    lax.fori_loop(0, SLOTS, full_pass, 0)
    stage_wait(b_ref, 1)
    tab_ref[0:1] = row_ref[0:1]
    for k in range(1, 16):
        tab_ref[k : k + 1] = b_ref[k][0:1]
    for o in range(1, 8):
        forward(o).wait()
        backward(o).wait()


def fine_call(density, counts):
    t1, t2 = left_const(lift_matrix(64)), left_const(lift_matrix(32))
    w = np.stack([fine_right(64), fine_right(32)])
    tl, wl, wm = left_const(low_rows()), low_right(), low_mid()
    vmem = pl.BlockSpec(memory_space=pltpu.VMEM)
    hbm = pl.BlockSpec(memory_space=pltpu.HBM)
    dma = pltpu.SemaphoreType.DMA
    return pl.pallas_call(
        fine_kernel,
        in_specs=[pl.BlockSpec(memory_space=pltpu.SMEM)] + [hbm] * 7,
        out_specs=[vmem] * 5,
        out_shape=[
            jax.ShapeDtypeStruct(density.shape, F32),
            jax.ShapeDtypeStruct((SLOTS, 32, 128), F32),
            jax.ShapeDtypeStruct((HTOTAL, 32, 128), F32),
            jax.ShapeDtypeStruct((HTOTAL, 32, 128), F32),
            jax.ShapeDtypeStruct((16, 128), jnp.int32),
        ],
        scratch_shapes=[
            pltpu.VMEM((SLOTS, 32, 128), F32),
            pltpu.VMEM(w.shape, BF16),
            pltpu.VMEM(t1.shape, BF16),
            pltpu.VMEM(t2.shape, BF16),
            pltpu.VMEM(tl.shape, BF16),
            pltpu.VMEM(wl.shape, BF16),
            pltpu.VMEM(wm.shape, BF16),
            pltpu.VMEM((SLOTS, 64, 4096), F32),
            pltpu.VMEM((1024, 256), BF16),
            pltpu.VMEM((1024, 256), BF16),
            pltpu.VMEM((1024, 256), F32),
            pltpu.VMEM((16 * SLOTS, 1024), BF16),
            pltpu.VMEM((16 * SLOTS, 1024), BF16),
            pltpu.VMEM((8, 128), jnp.int32),
            pltpu.VMEM((16, 8, 128), jnp.int32),
            pltpu.VMEM((8, 128), jnp.int32),
            pltpu.VMEM((16, 8, 128), jnp.int32),
            dma((SLOTS,)),
            dma((6,)),
            dma((2, 8)),
            dma((2, 8)),
            dma((2,)),
            dma((2,)),
        ],
        compiler_params=pltpu.CompilerParams(collective_id=0, has_side_effects=True, vmem_limit_bytes=30 << 20),
        name="fine",
    )(counts, *[pltpu.with_memory_space_constraint(jnp.asarray(a), pltpu.HBM) for a in (density, w, t1, t2, tl, wl, wm)])


def coarse_kernel(tabs_ref, lpf_ref, fw_ref, bw_ref, tab_ref, t1_ref, w1_ref, t2_ref, w2_ref, fine_ref, o_ref, h_ref, ctx_ref, res_ref, zero_ref, wsem):
    node, dev = lax.axis_index("node"), lax.axis_index("dev")
    me = node * 16 + dev
    count = tabs_ref[0, dev]

    def body(s):
        return pltpu.make_async_copy(fine_ref.at[s, pl.ds(16, 48)], o_ref.at[s, pl.ds(16, 48)], wsem.at[s, 0])

    def side(s):
        rows, cols = pl.ds(0, 16), pl.ds(1024, 3072)
        return pltpu.make_async_copy(fine_ref.at[s, rows, cols], o_ref.at[s, rows, cols], wsem.at[s, 1])

    def corner_out(s):
        return pltpu.make_async_copy(ctx_ref.at[s], o_ref.at[s, pl.ds(0, 16), pl.ds(0, 1024)], wsem.at[s, 2])

    def zeros(s):
        return pltpu.make_async_copy(zero_ref, o_ref.at[s], wsem.at[s, 0])

    for s in range(SLOTS):

        @pl.when(s < count)
        def _(s=s):
            body(s).start()
            side(s).start()

    krow = lax.broadcasted_iota(jnp.int32, (16, 128), 0)
    klane = lax.broadcasted_iota(jnp.int32, (16, 128), 1)
    owner = lax.rem(node - krow + 16, 16) * 16 + klane
    start = jnp.sum(jnp.where((klane < 16) & (owner < me), tab_ref[...], 0))
    first = start // 8

    def count_of(t):
        return tabs_ref[lax.rem(node - t // 16 + 16, 16), lax.rem(t, 16)]

    for s in range(SLOTS):
        h_ref[7 + s] = lpf_ref[s]
    after = 7 + count
    before = 7
    for o in range(1, 8):
        n, b = HALO[o - 1], HBASE[o - 1]
        for s in range(n):
            h_ref[jnp.minimum(after + s, 24)] = fw_ref[b + s]
        for s in range(n):
            p = before - n + s
            h_ref[jnp.where(p < 0, 25, p)] = bw_ref[b + s]
        after = after + count_of(lax.rem(me + o, 256))
        before = before - count_of(lax.rem(me - o + 256, 256))

    lane = lax.broadcasted_iota(jnp.int32, (8, 128), 1)
    base = 7 + first * 8 - start
    hs, ls = [], []
    for q in range(2):
        groups = []
        for c1 in range(2):
            for jh in range(2):
                for c2 in range(2):
                    c = 2 * c1 + 4 * c2
                    at = base + 8 * q + c
                    groups.append(jnp.concatenate([h_ref[at, 16 * jh : 16 * jh + 16], h_ref[at + 1, 16 * jh : 16 * jh + 16]], 0))
        y = left_dot(t1_ref[...], jnp.concatenate(groups, 1))
        hi, lo = split(y)
        for g in range(4):
            hs.append(hi[:, 256 * g : 256 * g + 256])
            ls.append(lo[:, 256 * g : 256 * g + 256])
    y = right_dot(jnp.concatenate(hs, 0), jnp.concatenate(ls, 0), w1_ref[...])
    last, firstm = (lane // 16) % 4 == 3, (lane // 16) % 4 == 0
    low = lane < 64
    corners = []
    for q in range(2):
        halves = []
        for r in range(4):
            at = [128 * q + 32 * g + 8 * r for g in range(4)]
            s = [y[a : a + 8, :128] for a in at]
            e = [y[a : a + 8, 128:] for a in at]
            s, e = lift_quarters(s, e, last, firstm)
            for g in range(4):
                res_ref[q, r // 2, 0, g, 8 * (r % 2) : 8 * (r % 2) + 8] = s[g]
                res_ref[q, r // 2, 1, g, 8 * (r % 2) : 8 * (r % 2) + 8] = e[g]
            if r < 2:
                halves.append(
                    jnp.concatenate([jnp.where(low, s[0], pltpu.roll(s[1], 64, 1)), jnp.where(low, s[2], pltpu.roll(s[3], 64, 1))], 1)
                )
        corners.append(jnp.concatenate(halves, 0))
    y = left_dot(t2_ref[...], jnp.concatenate(corners, 1))
    hi, lo = split(y)
    y = right_dot(
        jnp.concatenate([hi[:, :256], hi[:, 256:]], 0), jnp.concatenate([lo[:, :256], lo[:, 256:]], 0), w2_ref[...]
    )
    deep = (lane & 15) < 8
    for q in range(2):
        for r in range(2):
            a = 24 * q + 8 * r
            v0, v1 = y[a : a + 8, :128], y[a : a + 8, 128:256]
            if r == 0:
                v0 = jnp.where(deep, y[24 * q + 16 : 24 * q + 24, 256:], v0)
            rows = slice(8 * r, 8 * r + 8)
            for g, v in enumerate([v0, pltpu.roll(v0, 64, 1), v1, pltpu.roll(v1, 64, 1)]):
                res_ref[q, 0, 0, g, rows] = jnp.where(low, v, res_ref[q, 0, 0, g, rows])
    for s in range(SLOTS):

        @pl.when(s < count)
        def _(s=s):
            block = start + s
            q = block // 8 - first
            c0, c1, c2 = lax.rem(block, 2), lax.rem(block // 2, 2), lax.rem(block // 4, 2)
            for r in range(2):
                rows = slice(8 * r, 8 * r + 8)
                for g in range(4):
                    v = res_ref[q, c0, c1, g, rows]
                    v = jnp.where(c2 == 1, pltpu.roll(v, 64, 1), v)
                    for mh in range(2):
                        cols = slice(256 * g + 128 * mh, 256 * g + 128 * mh + 128)
                        left = pltpu.roll(v, 96, 1) if mh else v
                        right = pltpu.roll(v, 16 if mh else 48, 1)
                        old = fine_ref[s, rows, cols]
                        new = jnp.where(lane < 16, left, jnp.where((lane >= 64) & (lane < 80), right, old))
                        ctx_ref[s, rows, cols] = new
            corner_out(s).start()

    @pl.when(count < SLOTS)
    def _():
        zero_ref[...] = jnp.zeros_like(zero_ref)

    for s in range(1, SLOTS):

        @pl.when(s >= count)
        def _(s=s):
            zeros(s).start()

    for s in range(SLOTS):

        @pl.when(s < count)
        def _(s=s):
            body(s).wait()
            side(s).wait()
            corner_out(s).wait()

        @pl.when(s >= count)
        def _(s=s):
            zeros(s).wait()


def coarse_call(fine, lpf, fw, bw, tab):
    t1, w1, t2, w2 = left_const(lift_matrix(32)), coarse_right(), corner_left(), corner_right()
    vmem = pl.BlockSpec(memory_space=pltpu.VMEM)
    dma = pltpu.SemaphoreType.DMA
    return pl.pallas_call(
        coarse_kernel,
        in_specs=[pl.BlockSpec(memory_space=pltpu.SMEM)] + [vmem] * 9,
        out_specs=pl.BlockSpec(memory_space=pl.ANY),
        out_shape=jax.ShapeDtypeStruct(fine.shape, F32),
        scratch_shapes=[
            pltpu.VMEM((32, 32, 128), F32),
            pltpu.VMEM((SLOTS, 16, 1024), F32),
            pltpu.VMEM((2, 2, 2, 4, 16, 128), F32),
            pltpu.VMEM((64, 4096), F32),
            dma((SLOTS, 3)),
        ],
        compiler_params=pltpu.CompilerParams(vmem_limit_bytes=16 << 20),
        name="coarse",
    )(tab, lpf, fw, bw, tab, jnp.asarray(t1), jnp.asarray(w1), jnp.asarray(t2), jnp.asarray(w2), fine)


def per_device(density, counts):
    fine, lpf, fw, bw, tab = fine_call(density, counts)
    return coarse_call(fine, lpf, fw, bw, tab)


def solution(mesh):
    in_specs = (P(("node", "dev"), None, None), P(("node", "dev")))
    out_specs = P(("node", "dev"), None, None)
    return jax.shard_map(per_device, mesh=mesh, in_specs=in_specs, out_specs=out_specs, check_vma=False)
```

```python
import functools

import jax
import jax.numpy as jnp
import ml_dtypes
import numpy as np
from jax import lax
from jax.experimental import pallas as pl
from jax.experimental.pallas import tpu as pltpu
from jax.sharding import PartitionSpec as P

MESH = pl.DeviceIdType.MESH
F32 = jnp.float32
BF16 = jnp.bfloat16

A_LIFT = -1.586134342059924
B_LIFT = -0.052980118572961
C_LIFT = 0.882911075530934
D_LIFT = 0.443506852043971
K_LIFT = 1.230174104914001
A_SC = A_LIFT * K_LIFT * K_LIFT
B_SC = B_LIFT / (K_LIFT * K_LIFT)
C_SC = C_LIFT * K_LIFT * K_LIFT
D_SC = D_LIFT / (K_LIFT * K_LIFT)

SLOTS = 6
HALO = (6, 6, 5, 4, 3, 2, 1)
HBASE = (0, 6, 12, 17, 21, 24, 26)
HTOTAL = 27


def lift_matrix(n):
    x = np.eye(n)
    s, e = x[0::2].copy(), x[1::2].copy()

    def up(v):
        return np.concatenate([v[1:], v[-1:]], 0)

    def down(v):
        return np.concatenate([v[:1], v[:-1]], 0)

    e = e + A_LIFT * (s + up(s))
    s = s + B_LIFT * (down(e) + e)
    e = e + C_LIFT * (s + up(s))
    s = s + D_LIFT * (down(e) + e)
    return np.concatenate([s / K_LIFT, e * K_LIFT], 0)


def split_const(m):
    hi = m.astype(ml_dtypes.bfloat16)
    lo = (m - hi.astype(np.float64)).astype(ml_dtypes.bfloat16)
    return hi, lo


def left_const(m):
    hi, lo = split_const(m)
    return np.concatenate([hi, lo, hi], 1)


def right_const(m):
    hi, lo = split_const(m)
    return np.concatenate([hi, lo, hi], 0)


def fine_right(n):
    t = lift_matrix(n)
    w = np.zeros((256, 256))
    for q in range(2):
        for par in range(2):
            r = 128 * q + 64 * par
            c = 128 * par + 64 * q
            w[r : r + n, c : c + n] = t.T * (K_LIFT if par else 1.0 / K_LIFT)
    return right_const(w)


def low_rows():
    return lift_matrix(32)[:16] @ lift_matrix(64)[:32]


def low_right():
    return right_const(np.kron(np.eye(4), low_rows().T) @ np.kron(np.ones((1, 2)), np.eye(64)))


def low_mid():
    return np.stack([m.astype(np.float32) for m in split_const(np.kron(low_rows().T, np.ones((1, 16))))])


def coarse_right():
    t = lift_matrix(32)
    w = np.zeros((256, 256))
    for j in range(8):
        for k2 in range(2):
            for kb in range(2):
                r = 128 * k2 + 16 * j
                c = 128 * (j % 2) + 64 * kb + 16 * (j // 2)
                scale = K_LIFT if j % 2 else 1.0 / K_LIFT
                w[r : r + 16, c : c + 16] = t[16 * kb : 16 * kb + 16, 16 * k2 : 16 * k2 + 16].T * scale
    return right_const(w)


def corner_left():
    t16, t8 = lift_matrix(16), lift_matrix(8)
    return left_const(np.concatenate([t16, t8 @ t16[:8]], 0))


def corner_right():
    t16, t8 = lift_matrix(16), lift_matrix(8)
    second = np.kron(t16, t16).T
    low = t8 @ t16[:8]
    both = np.zeros((256, 128))
    for j in range(8):
        for k in range(8):
            both[:, 16 * j + k] = np.kron(low[j], low[k])
    return right_const(np.concatenate([second, both], 1))


def split(x):
    hi = x.astype(BF16)
    lo = (x - hi.astype(F32)).astype(BF16)
    return hi, lo


def left_dot(t, x):
    hi, lo = split(x)
    return jnp.dot(t, jnp.concatenate([hi, hi, lo], 0), preferred_element_type=F32)


def right_dot(hi, lo, w):
    return jnp.dot(jnp.concatenate([hi, hi, lo], 1), w, preferred_element_type=F32)


def lift_lanes(s, e, mask, up, down):
    n = len(s)
    sp = up(s)
    e = [e[g] + A_SC * (s[g] + sp[g]) for g in range(n)]
    em = down(e)
    s = [s[g] + B_SC * (em[g] + e[g]) for g in range(n)]
    sp = up(s)
    e = [e[g] + C_SC * (s[g] + sp[g]) for g in range(n)]
    em = down(e)
    s = [s[g] + D_SC * (em[g] + e[g]) for g in range(n)]
    return s, e


def lift_halves(s, e, low):
    n = len(s)

    def up(v):
        r = [pltpu.roll(x, 64, 1) for x in v]
        return [jnp.where(low, r[g], r[g + 1] if g + 1 < n else v[g]) for g in range(n)]

    def down(v):
        r = [pltpu.roll(x, 64, 1) for x in v]
        return [jnp.where(low, r[g - 1] if g else v[g], r[g]) for g in range(n)]

    return lift_lanes(s, e, low, up, down)


def lift_quarters(s, e, last, first):
    n = len(s)

    def up(v):
        out = []
        for g in range(n):
            near = pltpu.roll(v[g], 112, 1)
            far = pltpu.roll(v[g + 1], 48, 1) if g + 1 < n else v[g]
            out.append(jnp.where(last, far, near))
        return out

    def down(v):
        out = []
        for g in range(n):
            near = pltpu.roll(v[g], 16, 1)
            far = pltpu.roll(v[g - 1], 80, 1) if g else v[g]
            out.append(jnp.where(first, far, near))
        return out

    return lift_lanes(s, e, last, up, down)


def lift_stream(load_s, load_e, n, emit):
    s0, e1, s1, e2 = load_s(0), None, None, None
    for i in range(n):
        s_next = load_s(i + 1) if i + 1 < n else s0
        e1_new = load_e(i) + A_SC * (s0 + s_next)
        s1_new = s0 + B_SC * ((e1 if i else e1_new) + e1_new)
        if i:
            e2_new = e1 + C_SC * (s1 + s1_new)
            emit(i - 1, s1 + D_SC * ((e2 if i > 1 else e2_new) + e2_new), e2_new)
            e2 = e2_new
        s0, e1, s1 = s_next, e1_new, s1_new
    e2_new = e1 + C_SC * (s1 + s1)
    emit(n - 1, s1 + D_SC * (e2 + e2_new), e2_new)


def fine_kernel(
    count_ref, x_ref, wc_ref, t1c_ref, t2c_ref, tlc_ref, wlc_ref, wmc_ref, o_ref, lpf_ref, fw_ref, bw_ref, tab_ref,
    lpb_ref, w_ref, t1_ref, t2_ref, tl_ref, wl_ref, wr_ref, wm_ref, xv_ref, ah_ref, al_ref, se_ref, zh_ref, zl_ref, cv_ref, a_ref, row_ref, b_ref,
    xsem, wsem, dsend, drecv, csend, crecv,
):
    node, dev = lax.axis_index("node"), lax.axis_index("dev")
    me = node * 16 + dev
    count = count_ref[0]
    lane = lax.broadcasted_iota(jnp.int32, (32, 128), 1)
    low = lane < 64
    corner = (lane[:16] & 63) < 32

    def load_x(s):
        return pltpu.make_async_copy(x_ref.at[s], xv_ref.at[s], xsem.at[s])

    constants = [(tlc_ref, tl_ref), (wlc_ref, wl_ref), (wmc_ref, wr_ref), (wc_ref, w_ref), (t1c_ref, t1_ref), (t2c_ref, t2_ref)]
    load_c = [pltpu.make_async_copy(a, b, wsem.at[i]) for i, (a, b) in enumerate(constants)]
    for c in load_c[:3]:
        c.start()
    load_x(0).start()
    load_x(1).start()

    barrier = pltpu.get_barrier_semaphore()

    def by_offset(step):
        t = lax.rem(me + step + 256, 256)
        return {"node": t // 16, "dev": lax.rem(t, 16)}

    def by_dev(k):
        return {"node": node, "dev": lax.rem(dev + k, 16)}

    def by_node(k):
        return {"node": lax.rem(node + k, 16), "dev": dev}

    partners = [by_offset(o) for o in range(1, 8)] + [by_offset(-o) for o in range(1, 8)]
    partners += [by_dev(k) for k in range(1, 16)] + [by_node(k) for k in range(1, 16)]
    for p in partners:
        pl.semaphore_signal(barrier, inc=1, device_id=p, device_id_type=MESH)
    cv_ref[...] = jnp.zeros_like(cv_ref) + count

    def remote(src, dst, send, recv, to):
        return pltpu.make_async_remote_copy(
            src_ref=src, dst_ref=dst, send_sem=send, recv_sem=recv, device_id=to, device_id_type=MESH
        )

    def stage(src, dst, i, to):
        for k in range(1, 16):
            remote(src, dst.at[k], csend.at[i], crecv.at[i], to(k)).start()

    def stage_wait(dst, i):
        c = remote(dst.at[pl.ds(1, 15)], dst.at[pl.ds(1, 15)], csend.at[i], crecv.at[i], by_dev(1))
        c.wait_send()
        c.wait_recv()

    def forward(o):
        n, b = HALO[o - 1], HBASE[o - 1]
        return remote(lpf_ref.at[pl.ds(0, n)], fw_ref.at[pl.ds(b, n)], dsend.at[0, o], drecv.at[0, o], by_offset(-o))

    def backward(o):
        n, b = HALO[o - 1], HBASE[o - 1]
        return remote(lpb_ref.at[pl.ds(SLOTS - n, n)], bw_ref.at[pl.ds(b, n)], dsend.at[1, o], drecv.at[1, o], by_offset(o))

    def low_pass(slot, carry):
        load_x(slot).wait()

        @pl.when(slot < SLOTS - 2)
        def _():
            load_x(slot + 2).start()

        @pl.when(slot == 0)
        def _():
            for c in load_c[:3]:
                c.wait()

        @pl.when(slot == 1)
        def _():
            wide = lax.broadcasted_iota(jnp.int32, (16, 256), 1) & 15
            same = wide == lax.broadcasted_iota(jnp.int32, (16, 256), 0)
            for part in range(2):
                for j in range(64):
                    row = jnp.broadcast_to(wr_ref[part, j : j + 1], (16, 256))
                    wm_ref[part, 16 * j : 16 * j + 16] = jnp.where(same, row, 0.0).astype(BF16)

        @pl.when(slot == SLOTS - 1)
        def _():
            for c in load_c[3:]:
                c.start()

        for g in range(16):
            y = left_dot(tl_ref[...], xv_ref[slot, :, 256 * g : 256 * g + 256])
            ah_ref[16 * g : 16 * g + 16], al_ref[16 * g : 16 * g + 16] = split(y)
        z = right_dot(ah_ref[:256], al_ref[:256], wl_ref[...])
        rows = pl.ds(slot * 16, 16)
        for g in range(8):
            pair = jnp.where(low[:16], z[32 * g : 32 * g + 16], z[32 * g + 16 : 32 * g + 32])
            cols = slice(128 * g, 128 * g + 128)
            zh_ref[rows, cols], zl_ref[rows, cols] = split(pair)
        return carry

    lax.fori_loop(0, SLOTS, low_pass, 0)
    z = right_dot(zh_ref[...], zl_ref[...], jnp.concatenate([wm_ref[0], wm_ref[1], wm_ref[0]], 0))
    for s in range(SLOTS):
        for half in range(2):
            lpf_ref[s, 16 * half : 16 * half + 16] = z[16 * s : 16 * s + 16, 128 * half : 128 * half + 128]
    for s in range(SLOTS):
        lpb_ref[s] = lpf_ref[jnp.maximum(count - SLOTS + s, 0)]
    pl.semaphore_wait(barrier, len(partners))
    for o in (2, 1, 6, 3, 5, 7, 4):
        forward(o).start()
        backward(o).start()
    stage(cv_ref, a_ref, 0, by_dev)

    def rows_dot(t, x, g):
        hi, lo = split(left_dot(t, x))
        parts = t.shape[0] // 32
        for nn in range(2):
            cols = slice(128 * nn, 128 * nn + 128)
            for p in range(parts):
                at = 16 * ((2 * g + nn) * parts + p)
                for q in range(2):
                    rows = slice(32 * p + 16 * q, 32 * p + 16 * q + 16)
                    ah_ref[at : at + 16, 128 * q : 128 * q + 128] = hi[rows, cols]
                    al_ref[at : at + 16, 128 * q : 128 * q + 128] = lo[rows, cols]

    def columns(n, parts, w, store):
        size = 16 * parts
        se_ref[: n * size] = right_dot(ah_ref[: n * size], al_ref[: n * size], w_ref[w])
        held = {}

        def emit(i, s, e):
            if i % 2 == 0:
                held[0] = (s, e)
                return
            for band, (x0, x1) in enumerate(zip(held[0], (s, e))):
                r0, r1 = pltpu.roll(x0, 64, 1), pltpu.roll(x1, 64, 1)
                for q, v in enumerate((jnp.where(low[:size], x0, r1), jnp.where(low[:size], r0, x1))):
                    for p in range(parts):
                        store(32 * p + 16 * q, band, i // 2, v[16 * p : 16 * p + 16])

        lift_stream(
            lambda i: se_ref[size * i : size * i + size, :128], lambda i: se_ref[size * i : size * i + size, 128:], n, emit
        )

    def full_pass(slot, carry):
        for g in range(16):
            rows_dot(t1_ref[...], xv_ref[slot, :, 256 * g : 256 * g + 256], g)

        def store1(row, band, u, v):
            o_ref[slot, row : row + 16, 2048 * band + 128 * u : 2048 * band + 128 * u + 128] = v

        columns(32, 2, 0, store1)
        for h in range(8):
            rows_dot(t2_ref[...], o_ref[slot, :32, 256 * h : 256 * h + 256], h)

        def store2(row, band, u, v):
            at = (slot, slice(row, row + 16), slice(1024 * band + 128 * u, 1024 * band + 128 * u + 128))
            o_ref[at] = jnp.where(corner, v, o_ref[at])

        columns(16, 1, 1, store2)

        @pl.when(slot == 1)
        def _():
            stage_wait(a_ref, 0)
            row = jnp.where(lane[:8] == dev, cv_ref[...], 0)
            for k in range(1, 16):
                row = jnp.where(lane[:8] == lax.rem(dev - k + 16, 16), a_ref[k], row)
            row_ref[...] = row
            stage(row_ref, b_ref, 1, by_node)

        return carry

    for c in load_c[3:]:
        c.wait()
    lax.fori_loop(0, SLOTS, full_pass, 0)
    stage_wait(b_ref, 1)
    tab_ref[0:1] = row_ref[0:1]
    for k in range(1, 16):
        tab_ref[k : k + 1] = b_ref[k][0:1]
    for o in range(1, 8):
        forward(o).wait()
        backward(o).wait()


def fine_call(density, counts):
    t1, t2 = left_const(lift_matrix(64)), left_const(lift_matrix(32))
    w = np.stack([fine_right(64), fine_right(32)])
    tl, wl, wm = left_const(low_rows()), low_right(), low_mid()
    vmem = pl.BlockSpec(memory_space=pltpu.VMEM)
    hbm = pl.BlockSpec(memory_space=pltpu.HBM)
    dma = pltpu.SemaphoreType.DMA
    return pl.pallas_call(
        fine_kernel,
        in_specs=[pl.BlockSpec(memory_space=pltpu.SMEM)] + [hbm] * 7,
        out_specs=[vmem] * 5,
        out_shape=[
            jax.ShapeDtypeStruct(density.shape, F32),
            jax.ShapeDtypeStruct((SLOTS, 32, 128), F32),
            jax.ShapeDtypeStruct((HTOTAL, 32, 128), F32),
            jax.ShapeDtypeStruct((HTOTAL, 32, 128), F32),
            jax.ShapeDtypeStruct((16, 128), jnp.int32),
        ],
        scratch_shapes=[
            pltpu.VMEM((SLOTS, 32, 128), F32),
            pltpu.VMEM(w.shape, BF16),
            pltpu.VMEM(t1.shape, BF16),
            pltpu.VMEM(t2.shape, BF16),
            pltpu.VMEM(tl.shape, BF16),
            pltpu.VMEM(wl.shape, BF16),
            pltpu.VMEM(wm.shape, F32),
            pltpu.VMEM((2, 1024, 256), BF16),
            pltpu.VMEM((SLOTS, 64, 4096), F32),
            pltpu.VMEM((1024, 256), BF16),
            pltpu.VMEM((1024, 256), BF16),
            pltpu.VMEM((1024, 256), F32),
            pltpu.VMEM((16 * SLOTS, 1024), BF16),
            pltpu.VMEM((16 * SLOTS, 1024), BF16),
            pltpu.VMEM((8, 128), jnp.int32),
            pltpu.VMEM((16, 8, 128), jnp.int32),
            pltpu.VMEM((8, 128), jnp.int32),
            pltpu.VMEM((16, 8, 128), jnp.int32),
            dma((SLOTS,)),
            dma((6,)),
            dma((2, 8)),
            dma((2, 8)),
            dma((2,)),
            dma((2,)),
        ],
        compiler_params=pltpu.CompilerParams(collective_id=0, has_side_effects=True, vmem_limit_bytes=30 << 20),
        name="fine",
    )(counts, *[pltpu.with_memory_space_constraint(jnp.asarray(a), pltpu.HBM) for a in (density, w, t1, t2, tl, wl, wm)])


def coarse_kernel(tabs_ref, lpf_ref, fw_ref, bw_ref, tab_ref, t1_ref, w1_ref, t2_ref, w2_ref, fine_ref, o_ref, h_ref, ctx_ref, res_ref, zero_ref, wsem):
    node, dev = lax.axis_index("node"), lax.axis_index("dev")
    me = node * 16 + dev
    count = tabs_ref[0, dev]

    def body(s):
        return pltpu.make_async_copy(fine_ref.at[s, pl.ds(16, 48)], o_ref.at[s, pl.ds(16, 48)], wsem.at[s, 0])

    def side(s):
        rows, cols = pl.ds(0, 16), pl.ds(1024, 3072)
        return pltpu.make_async_copy(fine_ref.at[s, rows, cols], o_ref.at[s, rows, cols], wsem.at[s, 1])

    def corner_out(s):
        return pltpu.make_async_copy(ctx_ref.at[s], o_ref.at[s, pl.ds(0, 16), pl.ds(0, 1024)], wsem.at[s, 2])

    def zeros(s):
        return pltpu.make_async_copy(zero_ref, o_ref.at[s], wsem.at[s, 0])

    for s in range(SLOTS):

        @pl.when(s < count)
        def _(s=s):
            body(s).start()
            side(s).start()

    krow = lax.broadcasted_iota(jnp.int32, (16, 128), 0)
    klane = lax.broadcasted_iota(jnp.int32, (16, 128), 1)
    owner = lax.rem(node - krow + 16, 16) * 16 + klane
    start = jnp.sum(jnp.where((klane < 16) & (owner < me), tab_ref[...], 0))
    first = start // 8

    def count_of(t):
        return tabs_ref[lax.rem(node - t // 16 + 16, 16), lax.rem(t, 16)]

    for s in range(SLOTS):
        h_ref[7 + s] = lpf_ref[s]
    after = 7 + count
    before = 7
    for o in range(1, 8):
        n, b = HALO[o - 1], HBASE[o - 1]
        for s in range(n):
            h_ref[jnp.minimum(after + s, 24)] = fw_ref[b + s]
        for s in range(n):
            p = before - n + s
            h_ref[jnp.where(p < 0, 25, p)] = bw_ref[b + s]
        after = after + count_of(lax.rem(me + o, 256))
        before = before - count_of(lax.rem(me - o + 256, 256))

    lane = lax.broadcasted_iota(jnp.int32, (8, 128), 1)
    base = 7 + first * 8 - start
    hs, ls = [], []
    for q in range(2):
        groups = []
        for c1 in range(2):
            for jh in range(2):
                for c2 in range(2):
                    c = 2 * c1 + 4 * c2
                    at = base + 8 * q + c
                    groups.append(jnp.concatenate([h_ref[at, 16 * jh : 16 * jh + 16], h_ref[at + 1, 16 * jh : 16 * jh + 16]], 0))
        y = left_dot(t1_ref[...], jnp.concatenate(groups, 1))
        hi, lo = split(y)
        for g in range(4):
            hs.append(hi[:, 256 * g : 256 * g + 256])
            ls.append(lo[:, 256 * g : 256 * g + 256])
    y = right_dot(jnp.concatenate(hs, 0), jnp.concatenate(ls, 0), w1_ref[...])
    last, firstm = (lane // 16) % 4 == 3, (lane // 16) % 4 == 0
    low = lane < 64
    corners = []
    for q in range(2):
        halves = []
        for r in range(4):
            at = [128 * q + 32 * g + 8 * r for g in range(4)]
            s = [y[a : a + 8, :128] for a in at]
            e = [y[a : a + 8, 128:] for a in at]
            s, e = lift_quarters(s, e, last, firstm)
            for g in range(4):
                res_ref[q, r // 2, 0, g, 8 * (r % 2) : 8 * (r % 2) + 8] = s[g]
                res_ref[q, r // 2, 1, g, 8 * (r % 2) : 8 * (r % 2) + 8] = e[g]
            if r < 2:
                halves.append(
                    jnp.concatenate([jnp.where(low, s[0], pltpu.roll(s[1], 64, 1)), jnp.where(low, s[2], pltpu.roll(s[3], 64, 1))], 1)
                )
        corners.append(jnp.concatenate(halves, 0))
    y = left_dot(t2_ref[...], jnp.concatenate(corners, 1))
    hi, lo = split(y)
    y = right_dot(
        jnp.concatenate([hi[:, :256], hi[:, 256:]], 0), jnp.concatenate([lo[:, :256], lo[:, 256:]], 0), w2_ref[...]
    )
    deep = (lane & 15) < 8
    for q in range(2):
        for r in range(2):
            a = 24 * q + 8 * r
            v0, v1 = y[a : a + 8, :128], y[a : a + 8, 128:256]
            if r == 0:
                v0 = jnp.where(deep, y[24 * q + 16 : 24 * q + 24, 256:], v0)
            rows = slice(8 * r, 8 * r + 8)
            for g, v in enumerate([v0, pltpu.roll(v0, 64, 1), v1, pltpu.roll(v1, 64, 1)]):
                res_ref[q, 0, 0, g, rows] = jnp.where(low, v, res_ref[q, 0, 0, g, rows])
    for s in range(SLOTS):

        @pl.when(s < count)
        def _(s=s):
            block = start + s
            q = block // 8 - first
            c0, c1, c2 = lax.rem(block, 2), lax.rem(block // 2, 2), lax.rem(block // 4, 2)
            for r in range(2):
                rows = slice(8 * r, 8 * r + 8)
                for g in range(4):
                    v = res_ref[q, c0, c1, g, rows]
                    v = jnp.where(c2 == 1, pltpu.roll(v, 64, 1), v)
                    for mh in range(2):
                        cols = slice(256 * g + 128 * mh, 256 * g + 128 * mh + 128)
                        left = pltpu.roll(v, 96, 1) if mh else v
                        right = pltpu.roll(v, 16 if mh else 48, 1)
                        old = fine_ref[s, rows, cols]
                        new = jnp.where(lane < 16, left, jnp.where((lane >= 64) & (lane < 80), right, old))
                        ctx_ref[s, rows, cols] = new
            corner_out(s).start()

    @pl.when(count < SLOTS)
    def _():
        zero_ref[...] = jnp.zeros_like(zero_ref)

    for s in range(1, SLOTS):

        @pl.when(s >= count)
        def _(s=s):
            zeros(s).start()

    for s in range(SLOTS):

        @pl.when(s < count)
        def _(s=s):
            body(s).wait()
            side(s).wait()
            corner_out(s).wait()

        @pl.when(s >= count)
        def _(s=s):
            zeros(s).wait()


def coarse_call(fine, lpf, fw, bw, tab):
    t1, w1, t2, w2 = left_const(lift_matrix(32)), coarse_right(), corner_left(), corner_right()
    vmem = pl.BlockSpec(memory_space=pltpu.VMEM)
    dma = pltpu.SemaphoreType.DMA
    return pl.pallas_call(
        coarse_kernel,
        in_specs=[pl.BlockSpec(memory_space=pltpu.SMEM)] + [vmem] * 9,
        out_specs=pl.BlockSpec(memory_space=pl.ANY),
        out_shape=jax.ShapeDtypeStruct(fine.shape, F32),
        scratch_shapes=[
            pltpu.VMEM((32, 32, 128), F32),
            pltpu.VMEM((SLOTS, 16, 1024), F32),
            pltpu.VMEM((2, 2, 2, 4, 16, 128), F32),
            pltpu.VMEM((64, 4096), F32),
            dma((SLOTS, 3)),
        ],
        compiler_params=pltpu.CompilerParams(vmem_limit_bytes=16 << 20),
        name="coarse",
    )(tab, lpf, fw, bw, tab, jnp.asarray(t1), jnp.asarray(w1), jnp.asarray(t2), jnp.asarray(w2), fine)


def per_device(density, counts):
    fine, lpf, fw, bw, tab = fine_call(density, counts)
    return coarse_call(fine, lpf, fw, bw, tab)


def solution(mesh):
    in_specs = (P(("node", "dev"), None, None), P(("node", "dev")))
    out_specs = P(("node", "dev"), None, None)
    return jax.shard_map(per_device, mesh=mesh, in_specs=in_specs, out_specs=out_specs, check_vma=False)
```

```python
import functools

import jax
import jax.numpy as jnp
import ml_dtypes
import numpy as np
from jax import lax
from jax.experimental import pallas as pl
from jax.experimental.pallas import tpu as pltpu
from jax.sharding import PartitionSpec as P

MESH = pl.DeviceIdType.MESH
F32 = jnp.float32
BF16 = jnp.bfloat16

A_LIFT = -1.586134342059924
B_LIFT = -0.052980118572961
C_LIFT = 0.882911075530934
D_LIFT = 0.443506852043971
K_LIFT = 1.230174104914001
A_SC = A_LIFT * K_LIFT * K_LIFT
B_SC = B_LIFT / (K_LIFT * K_LIFT)
C_SC = C_LIFT * K_LIFT * K_LIFT
D_SC = D_LIFT / (K_LIFT * K_LIFT)

SLOTS = 6
HALO = (6, 6, 5, 4, 3, 2, 1)
HBASE = (0, 6, 12, 17, 21, 24, 26)
HTOTAL = 27


def lift_matrix(n):
    x = np.eye(n)
    s, e = x[0::2].copy(), x[1::2].copy()

    def up(v):
        return np.concatenate([v[1:], v[-1:]], 0)

    def down(v):
        return np.concatenate([v[:1], v[:-1]], 0)

    e = e + A_LIFT * (s + up(s))
    s = s + B_LIFT * (down(e) + e)
    e = e + C_LIFT * (s + up(s))
    s = s + D_LIFT * (down(e) + e)
    return np.concatenate([s / K_LIFT, e * K_LIFT], 0)


def split_const(m):
    hi = m.astype(ml_dtypes.bfloat16)
    lo = (m - hi.astype(np.float64)).astype(ml_dtypes.bfloat16)
    return hi, lo


def left_const(m):
    hi, lo = split_const(m)
    return np.concatenate([hi, lo, hi], 1)


def right_const(m):
    hi, lo = split_const(m)
    return np.concatenate([hi, lo, hi], 0)


def fine_right(n):
    t = lift_matrix(n)
    w = np.zeros((256, 256))
    for q in range(2):
        for par in range(2):
            r = 128 * q + 64 * par
            c = 128 * par + 64 * q
            w[r : r + n, c : c + n] = t.T * (K_LIFT if par else 1.0 / K_LIFT)
    return right_const(w)


def low_rows():
    return lift_matrix(32)[:16] @ lift_matrix(64)[:32]


def low_right():
    return right_const(np.kron(np.eye(4), low_rows().T) @ np.kron(np.ones((1, 2)), np.eye(64)))


def low_mid():
    return np.stack([m.astype(np.float32) for m in split_const(np.kron(low_rows().T, np.ones((1, 16))))])


def coarse_right():
    t = lift_matrix(32)
    w = np.zeros((256, 256))
    for j in range(8):
        for k2 in range(2):
            for kb in range(2):
                r = 128 * k2 + 16 * j
                c = 128 * (j % 2) + 64 * kb + 16 * (j // 2)
                scale = K_LIFT if j % 2 else 1.0 / K_LIFT
                w[r : r + 16, c : c + 16] = t[16 * kb : 16 * kb + 16, 16 * k2 : 16 * k2 + 16].T * scale
    return right_const(w)


def corner_left():
    t16, t8 = lift_matrix(16), lift_matrix(8)
    return left_const(np.concatenate([t16, t8 @ t16[:8]], 0))


def corner_right():
    t16, t8 = lift_matrix(16), lift_matrix(8)
    second = np.kron(t16, t16).T
    low = t8 @ t16[:8]
    both = np.zeros((256, 128))
    for j in range(8):
        for k in range(8):
            both[:, 16 * j + k] = np.kron(low[j], low[k])
    return right_const(np.concatenate([second, both], 1))


def split(x):
    hi = x.astype(BF16)
    lo = (x - hi.astype(F32)).astype(BF16)
    return hi, lo


def left_dot(t, x):
    hi, lo = split(x)
    return jnp.dot(t, jnp.concatenate([hi, hi, lo], 0), preferred_element_type=F32)


def right_dot(hi, lo, w):
    return jnp.dot(jnp.concatenate([hi, hi, lo], 1), w, preferred_element_type=F32)


def lift_lanes(s, e, mask, up, down):
    n = len(s)
    sp = up(s)
    e = [e[g] + A_SC * (s[g] + sp[g]) for g in range(n)]
    em = down(e)
    s = [s[g] + B_SC * (em[g] + e[g]) for g in range(n)]
    sp = up(s)
    e = [e[g] + C_SC * (s[g] + sp[g]) for g in range(n)]
    em = down(e)
    s = [s[g] + D_SC * (em[g] + e[g]) for g in range(n)]
    return s, e


def lift_halves(s, e, low):
    n = len(s)

    def up(v):
        r = [pltpu.roll(x, 64, 1) for x in v]
        return [jnp.where(low, r[g], r[g + 1] if g + 1 < n else v[g]) for g in range(n)]

    def down(v):
        r = [pltpu.roll(x, 64, 1) for x in v]
        return [jnp.where(low, r[g - 1] if g else v[g], r[g]) for g in range(n)]

    return lift_lanes(s, e, low, up, down)


def lift_quarters(s, e, last, first):
    n = len(s)

    def up(v):
        out = []
        for g in range(n):
            near = pltpu.roll(v[g], 112, 1)
            far = pltpu.roll(v[g + 1], 48, 1) if g + 1 < n else v[g]
            out.append(jnp.where(last, far, near))
        return out

    def down(v):
        out = []
        for g in range(n):
            near = pltpu.roll(v[g], 16, 1)
            far = pltpu.roll(v[g - 1], 80, 1) if g else v[g]
            out.append(jnp.where(first, far, near))
        return out

    return lift_lanes(s, e, last, up, down)


def lift_stream(load_s, load_e, n, emit):
    s0, e1, s1, e2 = load_s(0), None, None, None
    for i in range(n):
        s_next = load_s(i + 1) if i + 1 < n else s0
        e1_new = load_e(i) + A_SC * (s0 + s_next)
        s1_new = s0 + B_SC * ((e1 if i else e1_new) + e1_new)
        if i:
            e2_new = e1 + C_SC * (s1 + s1_new)
            emit(i - 1, s1 + D_SC * ((e2 if i > 1 else e2_new) + e2_new), e2_new)
            e2 = e2_new
        s0, e1, s1 = s_next, e1_new, s1_new
    e2_new = e1 + C_SC * (s1 + s1)
    emit(n - 1, s1 + D_SC * (e2 + e2_new), e2_new)


def fine_kernel(
    count_ref, x_ref, wc_ref, t1c_ref, t2c_ref, tlc_ref, wlc_ref, wmc_ref, o_ref, lpf_ref, fw_ref, bw_ref, tab_ref,
    lpb_ref, w_ref, t1_ref, t2_ref, tl_ref, wl_ref, wr_ref, wm_ref, xv_ref, ah_ref, al_ref, se_ref, zh_ref, zl_ref, cv_ref, a_ref, row_ref, b_ref,
    xsem, wsem, dsend, drecv, csend, crecv,
):
    node, dev = lax.axis_index("node"), lax.axis_index("dev")
    me = node * 16 + dev
    count = count_ref[0]
    lane = lax.broadcasted_iota(jnp.int32, (32, 128), 1)
    low = lane < 64
    corner = (lane[:16] & 63) < 32

    def load_x(s):
        return pltpu.make_async_copy(x_ref.at[s], xv_ref.at[s], xsem.at[s])

    constants = [(tlc_ref, tl_ref), (wlc_ref, wl_ref), (wmc_ref, wr_ref), (wc_ref, w_ref), (t1c_ref, t1_ref), (t2c_ref, t2_ref)]
    load_c = [pltpu.make_async_copy(a, b, wsem.at[i]) for i, (a, b) in enumerate(constants)]
    for c in load_c[:3]:
        c.start()
    load_x(0).start()
    load_x(1).start()

    barrier = pltpu.get_barrier_semaphore()

    def by_offset(step):
        t = lax.rem(me + step + 256, 256)
        return {"node": t // 16, "dev": lax.rem(t, 16)}

    def by_dev(k):
        return {"node": node, "dev": lax.rem(dev + k, 16)}

    def by_node(k):
        return {"node": lax.rem(node + k, 16), "dev": dev}

    partners = [by_offset(o) for o in range(1, 8)] + [by_offset(-o) for o in range(1, 8)]
    partners += [by_dev(k) for k in range(1, 16)] + [by_node(k) for k in range(1, 16)]
    for p in partners:
        pl.semaphore_signal(barrier, inc=1, device_id=p, device_id_type=MESH)
    cv_ref[...] = jnp.zeros_like(cv_ref) + count

    def remote(src, dst, send, recv, to):
        return pltpu.make_async_remote_copy(
            src_ref=src, dst_ref=dst, send_sem=send, recv_sem=recv, device_id=to, device_id_type=MESH
        )

    def stage(src, dst, i, to):
        for k in range(1, 16):
            remote(src, dst.at[k], csend.at[i], crecv.at[i], to(k)).start()

    def stage_wait(dst, i):
        c = remote(dst.at[pl.ds(1, 15)], dst.at[pl.ds(1, 15)], csend.at[i], crecv.at[i], by_dev(1))
        c.wait_send()
        c.wait_recv()

    def forward(o):
        n, b = HALO[o - 1], HBASE[o - 1]
        return remote(lpf_ref.at[pl.ds(0, n)], fw_ref.at[pl.ds(b, n)], dsend.at[0, o], drecv.at[0, o], by_offset(-o))

    def backward(o):
        n, b = HALO[o - 1], HBASE[o - 1]
        return remote(lpb_ref.at[pl.ds(SLOTS - n, n)], bw_ref.at[pl.ds(b, n)], dsend.at[1, o], drecv.at[1, o], by_offset(o))

    def low_pass(slot, carry):
        load_x(slot).wait()

        @pl.when(slot < SLOTS - 2)
        def _():
            load_x(slot + 2).start()

        @pl.when(slot == 0)
        def _():
            for c in load_c[:3]:
                c.wait()

        @pl.when(slot == 1)
        def _():
            wide = lax.broadcasted_iota(jnp.int32, (16, 256), 1) & 15
            same = wide == lax.broadcasted_iota(jnp.int32, (16, 256), 0)
            for part in range(2):
                for j in range(64):
                    row = jnp.broadcast_to(wr_ref[part, j : j + 1], (16, 256))
                    wm_ref[part, 16 * j : 16 * j + 16] = jnp.where(same, row, 0.0).astype(BF16)

        @pl.when(slot == SLOTS - 1)
        def _():
            for c in load_c[3:]:
                c.start()

        for g in range(16):
            y = left_dot(tl_ref[...], xv_ref[slot, :, 256 * g : 256 * g + 256])
            ah_ref[16 * g : 16 * g + 16], al_ref[16 * g : 16 * g + 16] = split(y)
        z = right_dot(ah_ref[:256], al_ref[:256], wl_ref[...])
        rows = pl.ds(slot * 16, 16)
        for g in range(8):
            pair = jnp.where(low[:16], z[32 * g : 32 * g + 16], z[32 * g + 16 : 32 * g + 32])
            cols = slice(128 * g, 128 * g + 128)
            zh_ref[rows, cols], zl_ref[rows, cols] = split(pair)

        @pl.when(slot == 3)
        def _():
            pl.semaphore_wait(barrier, len(partners))
            stage(cv_ref, a_ref, 0, by_dev)

        return carry

    lax.fori_loop(0, SLOTS, low_pass, 0)
    z = right_dot(zh_ref[...], zl_ref[...], jnp.concatenate([wm_ref[0], wm_ref[1], wm_ref[0]], 0))
    for s in range(SLOTS):
        for half in range(2):
            lpf_ref[s, 16 * half : 16 * half + 16] = z[16 * s : 16 * s + 16, 128 * half : 128 * half + 128]
    for s in range(SLOTS):
        lpb_ref[s] = lpf_ref[jnp.maximum(count - SLOTS + s, 0)]
    for o in (2, 1, 6, 3, 5, 7, 4):
        forward(o).start()
        backward(o).start()

    def rows_dot(t, x, g):
        hi, lo = split(left_dot(t, x))
        parts = t.shape[0] // 32
        for nn in range(2):
            cols = slice(128 * nn, 128 * nn + 128)
            for p in range(parts):
                at = 16 * ((2 * g + nn) * parts + p)
                for q in range(2):
                    rows = slice(32 * p + 16 * q, 32 * p + 16 * q + 16)
                    ah_ref[at : at + 16, 128 * q : 128 * q + 128] = hi[rows, cols]
                    al_ref[at : at + 16, 128 * q : 128 * q + 128] = lo[rows, cols]

    def columns(n, parts, w, store):
        size = 16 * parts
        se_ref[: n * size] = right_dot(ah_ref[: n * size], al_ref[: n * size], w_ref[w])
        held = {}

        def emit(i, s, e):
            if i % 2 == 0:
                held[0] = (s, e)
                return
            for band, (x0, x1) in enumerate(zip(held[0], (s, e))):
                r0, r1 = pltpu.roll(x0, 64, 1), pltpu.roll(x1, 64, 1)
                for q, v in enumerate((jnp.where(low[:size], x0, r1), jnp.where(low[:size], r0, x1))):
                    for p in range(parts):
                        store(32 * p + 16 * q, band, i // 2, v[16 * p : 16 * p + 16])

        lift_stream(
            lambda i: se_ref[size * i : size * i + size, :128], lambda i: se_ref[size * i : size * i + size, 128:], n, emit
        )

    def full_pass(slot, carry):
        for g in range(16):
            rows_dot(t1_ref[...], xv_ref[slot, :, 256 * g : 256 * g + 256], g)

        def store1(row, band, u, v):
            o_ref[slot, row : row + 16, 2048 * band + 128 * u : 2048 * band + 128 * u + 128] = v

        columns(32, 2, 0, store1)
        for h in range(8):
            rows_dot(t2_ref[...], o_ref[slot, :32, 256 * h : 256 * h + 256], h)

        def store2(row, band, u, v):
            at = (slot, slice(row, row + 16), slice(1024 * band + 128 * u, 1024 * band + 128 * u + 128))
            o_ref[at] = jnp.where(corner, v, o_ref[at])

        columns(16, 1, 1, store2)

        @pl.when(slot == 1)
        def _():
            stage_wait(a_ref, 0)
            row = jnp.where(lane[:8] == dev, cv_ref[...], 0)
            for k in range(1, 16):
                row = jnp.where(lane[:8] == lax.rem(dev - k + 16, 16), a_ref[k], row)
            row_ref[...] = row
            stage(row_ref, b_ref, 1, by_node)

        return carry

    for c in load_c[3:]:
        c.wait()
    lax.fori_loop(0, SLOTS, full_pass, 0)
    stage_wait(b_ref, 1)
    tab_ref[0:1] = row_ref[0:1]
    for k in range(1, 16):
        tab_ref[k : k + 1] = b_ref[k][0:1]
    for o in range(1, 8):
        forward(o).wait()
        backward(o).wait()


def fine_call(density, counts):
    t1, t2 = left_const(lift_matrix(64)), left_const(lift_matrix(32))
    w = np.stack([fine_right(64), fine_right(32)])
    tl, wl, wm = left_const(low_rows()), low_right(), low_mid()
    vmem = pl.BlockSpec(memory_space=pltpu.VMEM)
    hbm = pl.BlockSpec(memory_space=pltpu.HBM)
    dma = pltpu.SemaphoreType.DMA
    return pl.pallas_call(
        fine_kernel,
        in_specs=[pl.BlockSpec(memory_space=pltpu.SMEM)] + [hbm] * 7,
        out_specs=[vmem] * 5,
        out_shape=[
            jax.ShapeDtypeStruct(density.shape, F32),
            jax.ShapeDtypeStruct((SLOTS, 32, 128), F32),
            jax.ShapeDtypeStruct((HTOTAL, 32, 128), F32),
            jax.ShapeDtypeStruct((HTOTAL, 32, 128), F32),
            jax.ShapeDtypeStruct((16, 128), jnp.int32),
        ],
        scratch_shapes=[
            pltpu.VMEM((SLOTS, 32, 128), F32),
            pltpu.VMEM(w.shape, BF16),
            pltpu.VMEM(t1.shape, BF16),
            pltpu.VMEM(t2.shape, BF16),
            pltpu.VMEM(tl.shape, BF16),
            pltpu.VMEM(wl.shape, BF16),
            pltpu.VMEM(wm.shape, F32),
            pltpu.VMEM((2, 1024, 256), BF16),
            pltpu.VMEM((SLOTS, 64, 4096), F32),
            pltpu.VMEM((1024, 256), BF16),
            pltpu.VMEM((1024, 256), BF16),
            pltpu.VMEM((1024, 256), F32),
            pltpu.VMEM((16 * SLOTS, 1024), BF16),
            pltpu.VMEM((16 * SLOTS, 1024), BF16),
            pltpu.VMEM((8, 128), jnp.int32),
            pltpu.VMEM((16, 8, 128), jnp.int32),
            pltpu.VMEM((8, 128), jnp.int32),
            pltpu.VMEM((16, 8, 128), jnp.int32),
            dma((SLOTS,)),
            dma((6,)),
            dma((2, 8)),
            dma((2, 8)),
            dma((2,)),
            dma((2,)),
        ],
        compiler_params=pltpu.CompilerParams(collective_id=0, has_side_effects=True, vmem_limit_bytes=30 << 20),
        name="fine",
    )(counts, *[pltpu.with_memory_space_constraint(jnp.asarray(a), pltpu.HBM) for a in (density, w, t1, t2, tl, wl, wm)])


def coarse_kernel(tabs_ref, lpf_ref, fw_ref, bw_ref, tab_ref, t1_ref, w1_ref, t2_ref, w2_ref, fine_ref, o_ref, h_ref, ctx_ref, res_ref, zero_ref, wsem):
    node, dev = lax.axis_index("node"), lax.axis_index("dev")
    me = node * 16 + dev
    count = tabs_ref[0, dev]

    def body(s):
        return pltpu.make_async_copy(fine_ref.at[s, pl.ds(16, 48)], o_ref.at[s, pl.ds(16, 48)], wsem.at[s, 0])

    def side(s):
        rows, cols = pl.ds(0, 16), pl.ds(1024, 3072)
        return pltpu.make_async_copy(fine_ref.at[s, rows, cols], o_ref.at[s, rows, cols], wsem.at[s, 1])

    def corner_out(s):
        return pltpu.make_async_copy(ctx_ref.at[s], o_ref.at[s, pl.ds(0, 16), pl.ds(0, 1024)], wsem.at[s, 2])

    def zeros(s):
        return pltpu.make_async_copy(zero_ref, o_ref.at[s], wsem.at[s, 0])

    for s in range(SLOTS):

        @pl.when(s < count)
        def _(s=s):
            body(s).start()
            side(s).start()

    krow = lax.broadcasted_iota(jnp.int32, (16, 128), 0)
    klane = lax.broadcasted_iota(jnp.int32, (16, 128), 1)
    owner = lax.rem(node - krow + 16, 16) * 16 + klane
    start = jnp.sum(jnp.where((klane < 16) & (owner < me), tab_ref[...], 0))
    first = start // 8

    def count_of(t):
        return tabs_ref[lax.rem(node - t // 16 + 16, 16), lax.rem(t, 16)]

    for s in range(SLOTS):
        h_ref[7 + s] = lpf_ref[s]
    after = 7 + count
    before = 7
    for o in range(1, 8):
        n, b = HALO[o - 1], HBASE[o - 1]
        for s in range(n):
            h_ref[jnp.minimum(after + s, 24)] = fw_ref[b + s]
        for s in range(n):
            p = before - n + s
            h_ref[jnp.where(p < 0, 25, p)] = bw_ref[b + s]
        after = after + count_of(lax.rem(me + o, 256))
        before = before - count_of(lax.rem(me - o + 256, 256))

    lane = lax.broadcasted_iota(jnp.int32, (8, 128), 1)
    base = 7 + first * 8 - start
    hs, ls = [], []
    for q in range(2):
        groups = []
        for c1 in range(2):
            for jh in range(2):
                for c2 in range(2):
                    c = 2 * c1 + 4 * c2
                    at = base + 8 * q + c
                    groups.append(jnp.concatenate([h_ref[at, 16 * jh : 16 * jh + 16], h_ref[at + 1, 16 * jh : 16 * jh + 16]], 0))
        y = left_dot(t1_ref[...], jnp.concatenate(groups, 1))
        hi, lo = split(y)
        for g in range(4):
            hs.append(hi[:, 256 * g : 256 * g + 256])
            ls.append(lo[:, 256 * g : 256 * g + 256])
    y = right_dot(jnp.concatenate(hs, 0), jnp.concatenate(ls, 0), w1_ref[...])
    last, firstm = (lane // 16) % 4 == 3, (lane // 16) % 4 == 0
    low = lane < 64
    corners = []
    for q in range(2):
        halves = []
        for r in range(4):
            at = [128 * q + 32 * g + 8 * r for g in range(4)]
            s = [y[a : a + 8, :128] for a in at]
            e = [y[a : a + 8, 128:] for a in at]
            s, e = lift_quarters(s, e, last, firstm)
            for g in range(4):
                res_ref[q, r // 2, 0, g, 8 * (r % 2) : 8 * (r % 2) + 8] = s[g]
                res_ref[q, r // 2, 1, g, 8 * (r % 2) : 8 * (r % 2) + 8] = e[g]
            if r < 2:
                halves.append(
                    jnp.concatenate([jnp.where(low, s[0], pltpu.roll(s[1], 64, 1)), jnp.where(low, s[2], pltpu.roll(s[3], 64, 1))], 1)
                )
        corners.append(jnp.concatenate(halves, 0))
    y = left_dot(t2_ref[...], jnp.concatenate(corners, 1))
    hi, lo = split(y)
    y = right_dot(
        jnp.concatenate([hi[:, :256], hi[:, 256:]], 0), jnp.concatenate([lo[:, :256], lo[:, 256:]], 0), w2_ref[...]
    )
    deep = (lane & 15) < 8
    for q in range(2):
        for r in range(2):
            a = 24 * q + 8 * r
            v0, v1 = y[a : a + 8, :128], y[a : a + 8, 128:256]
            if r == 0:
                v0 = jnp.where(deep, y[24 * q + 16 : 24 * q + 24, 256:], v0)
            rows = slice(8 * r, 8 * r + 8)
            for g, v in enumerate([v0, pltpu.roll(v0, 64, 1), v1, pltpu.roll(v1, 64, 1)]):
                res_ref[q, 0, 0, g, rows] = jnp.where(low, v, res_ref[q, 0, 0, g, rows])
    for s in range(SLOTS):

        @pl.when(s < count)
        def _(s=s):
            block = start + s
            q = block // 8 - first
            c0, c1, c2 = lax.rem(block, 2), lax.rem(block // 2, 2), lax.rem(block // 4, 2)
            for r in range(2):
                rows = slice(8 * r, 8 * r + 8)
                for g in range(4):
                    v = res_ref[q, c0, c1, g, rows]
                    v = jnp.where(c2 == 1, pltpu.roll(v, 64, 1), v)
                    for mh in range(2):
                        cols = slice(256 * g + 128 * mh, 256 * g + 128 * mh + 128)
                        left = pltpu.roll(v, 96, 1) if mh else v
                        right = pltpu.roll(v, 16 if mh else 48, 1)
                        old = fine_ref[s, rows, cols]
                        new = jnp.where(lane < 16, left, jnp.where((lane >= 64) & (lane < 80), right, old))
                        ctx_ref[s, rows, cols] = new
            corner_out(s).start()

    @pl.when(count < SLOTS)
    def _():
        zero_ref[...] = jnp.zeros_like(zero_ref)

    for s in range(1, SLOTS):

        @pl.when(s >= count)
        def _(s=s):
            zeros(s).start()

    for s in range(SLOTS):

        @pl.when(s < count)
        def _(s=s):
            body(s).wait()
            side(s).wait()
            corner_out(s).wait()

        @pl.when(s >= count)
        def _(s=s):
            zeros(s).wait()


def coarse_call(fine, lpf, fw, bw, tab):
    t1, w1, t2, w2 = left_const(lift_matrix(32)), coarse_right(), corner_left(), corner_right()
    vmem = pl.BlockSpec(memory_space=pltpu.VMEM)
    dma = pltpu.SemaphoreType.DMA
    return pl.pallas_call(
        coarse_kernel,
        in_specs=[pl.BlockSpec(memory_space=pltpu.SMEM)] + [vmem] * 9,
        out_specs=pl.BlockSpec(memory_space=pl.ANY),
        out_shape=jax.ShapeDtypeStruct(fine.shape, F32),
        scratch_shapes=[
            pltpu.VMEM((32, 32, 128), F32),
            pltpu.VMEM((SLOTS, 16, 1024), F32),
            pltpu.VMEM((2, 2, 2, 4, 16, 128), F32),
            pltpu.VMEM((64, 4096), F32),
            dma((SLOTS, 3)),
        ],
        compiler_params=pltpu.CompilerParams(vmem_limit_bytes=16 << 20),
        name="coarse",
    )(tab, lpf, fw, bw, tab, jnp.asarray(t1), jnp.asarray(w1), jnp.asarray(t2), jnp.asarray(w2), fine)


def per_device(density, counts):
    fine, lpf, fw, bw, tab = fine_call(density, counts)
    return coarse_call(fine, lpf, fw, bw, tab)


def solution(mesh):
    in_specs = (P(("node", "dev"), None, None), P(("node", "dev")))
    out_specs = P(("node", "dev"), None, None)
    return jax.shard_map(per_device, mesh=mesh, in_specs=in_specs, out_specs=out_specs, check_vma=False)
```

```python
import functools

import jax
import jax.numpy as jnp
import ml_dtypes
import numpy as np
from jax import lax
from jax.experimental import pallas as pl
from jax.experimental.pallas import tpu as pltpu
from jax.sharding import PartitionSpec as P

MESH = pl.DeviceIdType.MESH
F32 = jnp.float32
BF16 = jnp.bfloat16

A_LIFT = -1.586134342059924
B_LIFT = -0.052980118572961
C_LIFT = 0.882911075530934
D_LIFT = 0.443506852043971
K_LIFT = 1.230174104914001
A_SC = A_LIFT * K_LIFT * K_LIFT
B_SC = B_LIFT / (K_LIFT * K_LIFT)
C_SC = C_LIFT * K_LIFT * K_LIFT
D_SC = D_LIFT / (K_LIFT * K_LIFT)

SLOTS = 6
HALO = (6, 6, 5, 4, 3, 2, 1)
HBASE = (0, 6, 12, 17, 21, 24, 26)
HTOTAL = 27


def lift_matrix(n):
    x = np.eye(n)
    s, e = x[0::2].copy(), x[1::2].copy()

    def up(v):
        return np.concatenate([v[1:], v[-1:]], 0)

    def down(v):
        return np.concatenate([v[:1], v[:-1]], 0)

    e = e + A_LIFT * (s + up(s))
    s = s + B_LIFT * (down(e) + e)
    e = e + C_LIFT * (s + up(s))
    s = s + D_LIFT * (down(e) + e)
    return np.concatenate([s / K_LIFT, e * K_LIFT], 0)


def split_const(m):
    hi = m.astype(ml_dtypes.bfloat16)
    lo = (m - hi.astype(np.float64)).astype(ml_dtypes.bfloat16)
    return hi, lo


def left_const(m):
    hi, lo = split_const(m)
    return np.concatenate([hi, lo, hi], 1)


def right_const(m):
    hi, lo = split_const(m)
    return np.concatenate([hi, lo, hi], 0)


def fine_right(n):
    t = lift_matrix(n)
    w = np.zeros((256, 256))
    for q in range(2):
        for par in range(2):
            r = 128 * q + 64 * par
            c = 128 * par + 64 * q
            w[r : r + n, c : c + n] = t.T * (K_LIFT if par else 1.0 / K_LIFT)
    return right_const(w)


def low_rows():
    return lift_matrix(32)[:16] @ lift_matrix(64)[:32]


def low_right():
    return right_const(np.kron(np.eye(4), low_rows().T) @ np.kron(np.ones((1, 2)), np.eye(64)))


def low_mid():
    return np.stack([m.astype(np.float32) for m in split_const(np.kron(low_rows().T, np.ones((1, 16))))])


def coarse_right():
    t = lift_matrix(32)
    w = np.zeros((256, 256))
    for j in range(8):
        for k2 in range(2):
            for kb in range(2):
                r = 128 * k2 + 16 * j
                c = 128 * (j % 2) + 64 * kb + 16 * (j // 2)
                scale = K_LIFT if j % 2 else 1.0 / K_LIFT
                w[r : r + 16, c : c + 16] = t[16 * kb : 16 * kb + 16, 16 * k2 : 16 * k2 + 16].T * scale
    return right_const(w)


def corner_left():
    t16, t8 = lift_matrix(16), lift_matrix(8)
    return left_const(np.concatenate([t16, t8 @ t16[:8]], 0))


def corner_right():
    t16, t8 = lift_matrix(16), lift_matrix(8)
    second = np.kron(t16, t16).T
    low = t8 @ t16[:8]
    both = np.zeros((256, 128))
    for j in range(8):
        for k in range(8):
            both[:, 16 * j + k] = np.kron(low[j], low[k])
    return right_const(np.concatenate([second, both], 1))


def split(x):
    hi = x.astype(BF16)
    lo = (x - hi.astype(F32)).astype(BF16)
    return hi, lo


def left_dot(t, x):
    hi, lo = split(x)
    return jnp.dot(t, jnp.concatenate([hi, hi, lo], 0), preferred_element_type=F32)


def right_dot(hi, lo, w):
    return jnp.dot(jnp.concatenate([hi, hi, lo], 1), w, preferred_element_type=F32)


def lift_lanes(s, e, mask, up, down):
    n = len(s)
    sp = up(s)
    e = [e[g] + A_SC * (s[g] + sp[g]) for g in range(n)]
    em = down(e)
    s = [s[g] + B_SC * (em[g] + e[g]) for g in range(n)]
    sp = up(s)
    e = [e[g] + C_SC * (s[g] + sp[g]) for g in range(n)]
    em = down(e)
    s = [s[g] + D_SC * (em[g] + e[g]) for g in range(n)]
    return s, e


def lift_halves(s, e, low):
    n = len(s)

    def up(v):
        r = [pltpu.roll(x, 64, 1) for x in v]
        return [jnp.where(low, r[g], r[g + 1] if g + 1 < n else v[g]) for g in range(n)]

    def down(v):
        r = [pltpu.roll(x, 64, 1) for x in v]
        return [jnp.where(low, r[g - 1] if g else v[g], r[g]) for g in range(n)]

    return lift_lanes(s, e, low, up, down)


def lift_quarters(s, e, last, first):
    n = len(s)

    def up(v):
        out = []
        for g in range(n):
            near = pltpu.roll(v[g], 112, 1)
            far = pltpu.roll(v[g + 1], 48, 1) if g + 1 < n else v[g]
            out.append(jnp.where(last, far, near))
        return out

    def down(v):
        out = []
        for g in range(n):
            near = pltpu.roll(v[g], 16, 1)
            far = pltpu.roll(v[g - 1], 80, 1) if g else v[g]
            out.append(jnp.where(first, far, near))
        return out

    return lift_lanes(s, e, last, up, down)


def lift_stream(load_s, load_e, n, emit):
    s0, e1, s1, e2 = load_s(0), None, None, None
    for i in range(n):
        s_next = load_s(i + 1) if i + 1 < n else s0
        e1_new = load_e(i) + A_SC * (s0 + s_next)
        s1_new = s0 + B_SC * ((e1 if i else e1_new) + e1_new)
        if i:
            e2_new = e1 + C_SC * (s1 + s1_new)
            emit(i - 1, s1 + D_SC * ((e2 if i > 1 else e2_new) + e2_new), e2_new)
            e2 = e2_new
        s0, e1, s1 = s_next, e1_new, s1_new
    e2_new = e1 + C_SC * (s1 + s1)
    emit(n - 1, s1 + D_SC * (e2 + e2_new), e2_new)


def fine_kernel(
    count_ref, x_ref, wc_ref, t1c_ref, t2c_ref, tlc_ref, wlc_ref, wmc_ref, o_ref, lpf_ref, fw_ref, bw_ref, tab_ref,
    lpb_ref, w_ref, t1_ref, t2_ref, tl_ref, wl_ref, wr_ref, wm_ref, xv_ref, ah_ref, al_ref, se_ref, zh_ref, zl_ref, cv_ref, a_ref, row_ref, b_ref,
    xsem, wsem, dsend, drecv, csend, crecv,
):
    node, dev = lax.axis_index("node"), lax.axis_index("dev")
    me = node * 16 + dev
    count = count_ref[0]
    lane = lax.broadcasted_iota(jnp.int32, (32, 128), 1)
    low = lane < 64
    corner = (lane[:16] & 63) < 32

    def load_x(s):
        return pltpu.make_async_copy(x_ref.at[s], xv_ref.at[s], xsem.at[s])

    constants = [(tlc_ref, tl_ref), (wlc_ref, wl_ref), (wmc_ref, wr_ref), (wc_ref, w_ref), (t1c_ref, t1_ref), (t2c_ref, t2_ref)]
    load_c = [pltpu.make_async_copy(a, b, wsem.at[i]) for i, (a, b) in enumerate(constants)]
    for c in load_c[:3]:
        c.start()
    load_x(0).start()
    load_x(1).start()

    barrier = pltpu.get_barrier_semaphore()

    def by_offset(step):
        t = lax.rem(me + step + 256, 256)
        return {"node": t // 16, "dev": lax.rem(t, 16)}

    def by_dev(k):
        return {"node": node, "dev": lax.rem(dev + k, 16)}

    def by_node(k):
        return {"node": lax.rem(node + k, 16), "dev": dev}

    partners = [by_offset(o) for o in range(1, 8)] + [by_offset(-o) for o in range(1, 8)]
    partners += [by_dev(k) for k in range(1, 16)] + [by_node(k) for k in range(1, 16)]
    for p in partners:
        pl.semaphore_signal(barrier, inc=1, device_id=p, device_id_type=MESH)
    cv_ref[...] = jnp.zeros_like(cv_ref) + count

    def remote(src, dst, send, recv, to):
        return pltpu.make_async_remote_copy(
            src_ref=src, dst_ref=dst, send_sem=send, recv_sem=recv, device_id=to, device_id_type=MESH
        )

    def stage(src, dst, i, to):
        for k in range(1, 16):
            remote(src, dst.at[k], csend.at[i], crecv.at[i], to(k)).start()

    def stage_wait(dst, i):
        c = remote(dst.at[pl.ds(1, 15)], dst.at[pl.ds(1, 15)], csend.at[i], crecv.at[i], by_dev(1))
        c.wait_send()
        c.wait_recv()

    def forward(o):
        n, b = HALO[o - 1], HBASE[o - 1]
        return remote(lpf_ref.at[pl.ds(0, n)], fw_ref.at[pl.ds(b, n)], dsend.at[0, o], drecv.at[0, o], by_offset(-o))

    def backward(o):
        n, b = HALO[o - 1], HBASE[o - 1]
        return remote(lpb_ref.at[pl.ds(SLOTS - n, n)], bw_ref.at[pl.ds(b, n)], dsend.at[1, o], drecv.at[1, o], by_offset(o))

    def low_pass(slot, carry):
        load_x(slot).wait()

        @pl.when(slot < SLOTS - 2)
        def _():
            load_x(slot + 2).start()

        @pl.when(slot == 0)
        def _():
            for c in load_c[:3]:
                c.wait()

        @pl.when(slot == 1)
        def _():
            wide = lax.broadcasted_iota(jnp.int32, (16, 256), 1) & 15
            same = wide == lax.broadcasted_iota(jnp.int32, (16, 256), 0)
            for part in range(2):
                for j in range(64):
                    row = jnp.broadcast_to(wr_ref[part, j : j + 1], (16, 256))
                    wm_ref[part, 16 * j : 16 * j + 16] = jnp.where(same, row, 0.0).astype(BF16)

        @pl.when(slot == SLOTS - 1)
        def _():
            for c in load_c[3:]:
                c.start()

        for g in range(16):
            y = left_dot(tl_ref[...], xv_ref[slot, :, 256 * g : 256 * g + 256])
            ah_ref[16 * g : 16 * g + 16], al_ref[16 * g : 16 * g + 16] = split(y)
        z = right_dot(ah_ref[:256], al_ref[:256], wl_ref[...])
        rows = pl.ds(slot * 16, 16)
        for g in range(8):
            pair = jnp.where(low[:16], z[32 * g : 32 * g + 16], z[32 * g + 16 : 32 * g + 32])
            cols = slice(128 * g, 128 * g + 128)
            zh_ref[rows, cols], zl_ref[rows, cols] = split(pair)

        @pl.when(slot == 3)
        def _():
            pl.semaphore_wait(barrier, len(partners))
            stage(cv_ref, a_ref, 0, by_dev)

        return carry

    lax.fori_loop(0, SLOTS, low_pass, 0)
    z = right_dot(zh_ref[...], zl_ref[...], jnp.concatenate([wm_ref[0], wm_ref[1], wm_ref[0]], 0))
    for s in range(SLOTS):
        for half in range(2):
            lpf_ref[s, 16 * half : 16 * half + 16] = z[16 * s : 16 * s + 16, 128 * half : 128 * half + 128]
    for s in range(SLOTS):
        lpb_ref[s] = lpf_ref[jnp.maximum(count - SLOTS + s, 0)]
    forward(2).start()
    backward(2).start()
    stage_wait(a_ref, 0)
    row = jnp.where(lane[:8] == dev, cv_ref[...], 0)
    for k in range(1, 16):
        row = jnp.where(lane[:8] == lax.rem(dev - k + 16, 16), a_ref[k], row)
    row_ref[...] = row
    stage(row_ref, b_ref, 1, by_node)
    for o in (1, 6, 3, 5, 7, 4):
        forward(o).start()
        backward(o).start()

    def rows_dot(t, x, g):
        hi, lo = split(left_dot(t, x))
        parts = t.shape[0] // 32
        for nn in range(2):
            cols = slice(128 * nn, 128 * nn + 128)
            for p in range(parts):
                at = 16 * ((2 * g + nn) * parts + p)
                for q in range(2):
                    rows = slice(32 * p + 16 * q, 32 * p + 16 * q + 16)
                    ah_ref[at : at + 16, 128 * q : 128 * q + 128] = hi[rows, cols]
                    al_ref[at : at + 16, 128 * q : 128 * q + 128] = lo[rows, cols]

    def columns(n, parts, w, store):
        size = 16 * parts
        se_ref[: n * size] = right_dot(ah_ref[: n * size], al_ref[: n * size], w_ref[w])
        held = {}

        def emit(i, s, e):
            if i % 2 == 0:
                held[0] = (s, e)
                return
            for band, (x0, x1) in enumerate(zip(held[0], (s, e))):
                r0, r1 = pltpu.roll(x0, 64, 1), pltpu.roll(x1, 64, 1)
                for q, v in enumerate((jnp.where(low[:size], x0, r1), jnp.where(low[:size], r0, x1))):
                    for p in range(parts):
                        store(32 * p + 16 * q, band, i // 2, v[16 * p : 16 * p + 16])

        lift_stream(
            lambda i: se_ref[size * i : size * i + size, :128], lambda i: se_ref[size * i : size * i + size, 128:], n, emit
        )

    def full_pass(slot, carry):
        for g in range(16):
            rows_dot(t1_ref[...], xv_ref[slot, :, 256 * g : 256 * g + 256], g)

        def store1(row, band, u, v):
            o_ref[slot, row : row + 16, 2048 * band + 128 * u : 2048 * band + 128 * u + 128] = v

        columns(32, 2, 0, store1)
        for h in range(8):
            rows_dot(t2_ref[...], o_ref[slot, :32, 256 * h : 256 * h + 256], h)

        def store2(row, band, u, v):
            at = (slot, slice(row, row + 16), slice(1024 * band + 128 * u, 1024 * band + 128 * u + 128))
            o_ref[at] = jnp.where(corner, v, o_ref[at])

        columns(16, 1, 1, store2)
        return carry

    for c in load_c[3:]:
        c.wait()
    lax.fori_loop(0, SLOTS, full_pass, 0)
    stage_wait(b_ref, 1)
    tab_ref[0:1] = row_ref[0:1]
    for k in range(1, 16):
        tab_ref[k : k + 1] = b_ref[k][0:1]
    for o in range(1, 8):
        forward(o).wait()
        backward(o).wait()


def fine_call(density, counts):
    t1, t2 = left_const(lift_matrix(64)), left_const(lift_matrix(32))
    w = np.stack([fine_right(64), fine_right(32)])
    tl, wl, wm = left_const(low_rows()), low_right(), low_mid()
    vmem = pl.BlockSpec(memory_space=pltpu.VMEM)
    hbm = pl.BlockSpec(memory_space=pltpu.HBM)
    dma = pltpu.SemaphoreType.DMA
    return pl.pallas_call(
        fine_kernel,
        in_specs=[pl.BlockSpec(memory_space=pltpu.SMEM)] + [hbm] * 7,
        out_specs=[vmem] * 5,
        out_shape=[
            jax.ShapeDtypeStruct(density.shape, F32),
            jax.ShapeDtypeStruct((SLOTS, 32, 128), F32),
            jax.ShapeDtypeStruct((HTOTAL, 32, 128), F32),
            jax.ShapeDtypeStruct((HTOTAL, 32, 128), F32),
            jax.ShapeDtypeStruct((16, 128), jnp.int32),
        ],
        scratch_shapes=[
            pltpu.VMEM((SLOTS, 32, 128), F32),
            pltpu.VMEM(w.shape, BF16),
            pltpu.VMEM(t1.shape, BF16),
            pltpu.VMEM(t2.shape, BF16),
            pltpu.VMEM(tl.shape, BF16),
            pltpu.VMEM(wl.shape, BF16),
            pltpu.VMEM(wm.shape, F32),
            pltpu.VMEM((2, 1024, 256), BF16),
            pltpu.VMEM((SLOTS, 64, 4096), F32),
            pltpu.VMEM((1024, 256), BF16),
            pltpu.VMEM((1024, 256), BF16),
            pltpu.VMEM((1024, 256), F32),
            pltpu.VMEM((16 * SLOTS, 1024), BF16),
            pltpu.VMEM((16 * SLOTS, 1024), BF16),
            pltpu.VMEM((8, 128), jnp.int32),
            pltpu.VMEM((16, 8, 128), jnp.int32),
            pltpu.VMEM((8, 128), jnp.int32),
            pltpu.VMEM((16, 8, 128), jnp.int32),
            dma((SLOTS,)),
            dma((6,)),
            dma((2, 8)),
            dma((2, 8)),
            dma((2,)),
            dma((2,)),
        ],
        compiler_params=pltpu.CompilerParams(collective_id=0, has_side_effects=True, vmem_limit_bytes=30 << 20),
        name="fine",
    )(counts, *[pltpu.with_memory_space_constraint(jnp.asarray(a), pltpu.HBM) for a in (density, w, t1, t2, tl, wl, wm)])


def coarse_kernel(tabs_ref, lpf_ref, fw_ref, bw_ref, tab_ref, t1_ref, w1_ref, t2_ref, w2_ref, fine_ref, o_ref, h_ref, ctx_ref, res_ref, zero_ref, wsem):
    node, dev = lax.axis_index("node"), lax.axis_index("dev")
    me = node * 16 + dev
    count = tabs_ref[0, dev]

    def body(s):
        return pltpu.make_async_copy(fine_ref.at[s, pl.ds(16, 48)], o_ref.at[s, pl.ds(16, 48)], wsem.at[s, 0])

    def side(s):
        rows, cols = pl.ds(0, 16), pl.ds(1024, 3072)
        return pltpu.make_async_copy(fine_ref.at[s, rows, cols], o_ref.at[s, rows, cols], wsem.at[s, 1])

    def corner_out(s):
        return pltpu.make_async_copy(ctx_ref.at[s], o_ref.at[s, pl.ds(0, 16), pl.ds(0, 1024)], wsem.at[s, 2])

    def zeros(s):
        return pltpu.make_async_copy(zero_ref, o_ref.at[s], wsem.at[s, 0])

    for s in range(SLOTS):

        @pl.when(s < count)
        def _(s=s):
            body(s).start()
            side(s).start()

    krow = lax.broadcasted_iota(jnp.int32, (16, 128), 0)
    klane = lax.broadcasted_iota(jnp.int32, (16, 128), 1)
    owner = lax.rem(node - krow + 16, 16) * 16 + klane
    start = jnp.sum(jnp.where((klane < 16) & (owner < me), tab_ref[...], 0))
    first = start // 8

    def count_of(t):
        return tabs_ref[lax.rem(node - t // 16 + 16, 16), lax.rem(t, 16)]

    for s in range(SLOTS):
        h_ref[7 + s] = lpf_ref[s]
    after = 7 + count
    before = 7
    for o in range(1, 8):
        n, b = HALO[o - 1], HBASE[o - 1]
        for s in range(n):
            h_ref[jnp.minimum(after + s, 24)] = fw_ref[b + s]
        for s in range(n):
            p = before - n + s
            h_ref[jnp.where(p < 0, 25, p)] = bw_ref[b + s]
        after = after + count_of(lax.rem(me + o, 256))
        before = before - count_of(lax.rem(me - o + 256, 256))

    lane = lax.broadcasted_iota(jnp.int32, (8, 128), 1)
    base = 7 + first * 8 - start
    hs, ls = [], []
    for q in range(2):
        groups = []
        for c1 in range(2):
            for jh in range(2):
                for c2 in range(2):
                    c = 2 * c1 + 4 * c2
                    at = base + 8 * q + c
                    groups.append(jnp.concatenate([h_ref[at, 16 * jh : 16 * jh + 16], h_ref[at + 1, 16 * jh : 16 * jh + 16]], 0))
        y = left_dot(t1_ref[...], jnp.concatenate(groups, 1))
        hi, lo = split(y)
        for g in range(4):
            hs.append(hi[:, 256 * g : 256 * g + 256])
            ls.append(lo[:, 256 * g : 256 * g + 256])
    y = right_dot(jnp.concatenate(hs, 0), jnp.concatenate(ls, 0), w1_ref[...])
    last, firstm = (lane // 16) % 4 == 3, (lane // 16) % 4 == 0
    low = lane < 64
    corners = []
    for q in range(2):
        halves = []
        for r in range(4):
            at = [128 * q + 32 * g + 8 * r for g in range(4)]
            s = [y[a : a + 8, :128] for a in at]
            e = [y[a : a + 8, 128:] for a in at]
            s, e = lift_quarters(s, e, last, firstm)
            for g in range(4):
                res_ref[q, r // 2, 0, g, 8 * (r % 2) : 8 * (r % 2) + 8] = s[g]
                res_ref[q, r // 2, 1, g, 8 * (r % 2) : 8 * (r % 2) + 8] = e[g]
            if r < 2:
                halves.append(
                    jnp.concatenate([jnp.where(low, s[0], pltpu.roll(s[1], 64, 1)), jnp.where(low, s[2], pltpu.roll(s[3], 64, 1))], 1)
                )
        corners.append(jnp.concatenate(halves, 0))
    y = left_dot(t2_ref[...], jnp.concatenate(corners, 1))
    hi, lo = split(y)
    y = right_dot(
        jnp.concatenate([hi[:, :256], hi[:, 256:]], 0), jnp.concatenate([lo[:, :256], lo[:, 256:]], 0), w2_ref[...]
    )
    deep = (lane & 15) < 8
    for q in range(2):
        for r in range(2):
            a = 24 * q + 8 * r
            v0, v1 = y[a : a + 8, :128], y[a : a + 8, 128:256]
            if r == 0:
                v0 = jnp.where(deep, y[24 * q + 16 : 24 * q + 24, 256:], v0)
            rows = slice(8 * r, 8 * r + 8)
            for g, v in enumerate([v0, pltpu.roll(v0, 64, 1), v1, pltpu.roll(v1, 64, 1)]):
                res_ref[q, 0, 0, g, rows] = jnp.where(low, v, res_ref[q, 0, 0, g, rows])
    for s in range(SLOTS):

        @pl.when(s < count)
        def _(s=s):
            block = start + s
            q = block // 8 - first
            c0, c1, c2 = lax.rem(block, 2), lax.rem(block // 2, 2), lax.rem(block // 4, 2)
            for r in range(2):
                rows = slice(8 * r, 8 * r + 8)
                for g in range(4):
                    v = res_ref[q, c0, c1, g, rows]
                    v = jnp.where(c2 == 1, pltpu.roll(v, 64, 1), v)
                    for mh in range(2):
                        cols = slice(256 * g + 128 * mh, 256 * g + 128 * mh + 128)
                        left = pltpu.roll(v, 96, 1) if mh else v
                        right = pltpu.roll(v, 16 if mh else 48, 1)
                        old = fine_ref[s, rows, cols]
                        new = jnp.where(lane < 16, left, jnp.where((lane >= 64) & (lane < 80), right, old))
                        ctx_ref[s, rows, cols] = new
            corner_out(s).start()

    @pl.when(count < SLOTS)
    def _():
        zero_ref[...] = jnp.zeros_like(zero_ref)

    for s in range(1, SLOTS):

        @pl.when(s >= count)
        def _(s=s):
            zeros(s).start()

    for s in range(SLOTS):

        @pl.when(s < count)
        def _(s=s):
            body(s).wait()
            side(s).wait()
            corner_out(s).wait()

        @pl.when(s >= count)
        def _(s=s):
            zeros(s).wait()


def coarse_call(fine, lpf, fw, bw, tab):
    t1, w1, t2, w2 = left_const(lift_matrix(32)), coarse_right(), corner_left(), corner_right()
    vmem = pl.BlockSpec(memory_space=pltpu.VMEM)
    dma = pltpu.SemaphoreType.DMA
    return pl.pallas_call(
        coarse_kernel,
        in_specs=[pl.BlockSpec(memory_space=pltpu.SMEM)] + [vmem] * 9,
        out_specs=pl.BlockSpec(memory_space=pl.ANY),
        out_shape=jax.ShapeDtypeStruct(fine.shape, F32),
        scratch_shapes=[
            pltpu.VMEM((32, 32, 128), F32),
            pltpu.VMEM((SLOTS, 16, 1024), F32),
            pltpu.VMEM((2, 2, 2, 4, 16, 128), F32),
            pltpu.VMEM((64, 4096), F32),
            dma((SLOTS, 3)),
        ],
        compiler_params=pltpu.CompilerParams(vmem_limit_bytes=16 << 20),
        name="coarse",
    )(tab, lpf, fw, bw, tab, jnp.asarray(t1), jnp.asarray(w1), jnp.asarray(t2), jnp.asarray(w2), fine)


def per_device(density, counts):
    fine, lpf, fw, bw, tab = fine_call(density, counts)
    return coarse_call(fine, lpf, fw, bw, tab)


def solution(mesh):
    in_specs = (P(("node", "dev"), None, None), P(("node", "dev")))
    out_specs = P(("node", "dev"), None, None)
    return jax.shard_map(per_device, mesh=mesh, in_specs=in_specs, out_specs=out_specs, check_vma=False)
```

```python
import functools

import jax
import jax.numpy as jnp
import ml_dtypes
import numpy as np
from jax import lax
from jax.experimental import pallas as pl
from jax.experimental.pallas import tpu as pltpu
from jax.sharding import PartitionSpec as P

MESH = pl.DeviceIdType.MESH
F32 = jnp.float32
BF16 = jnp.bfloat16

A_LIFT = -1.586134342059924
B_LIFT = -0.052980118572961
C_LIFT = 0.882911075530934
D_LIFT = 0.443506852043971
K_LIFT = 1.230174104914001
A_SC = A_LIFT * K_LIFT * K_LIFT
B_SC = B_LIFT / (K_LIFT * K_LIFT)
C_SC = C_LIFT * K_LIFT * K_LIFT
D_SC = D_LIFT / (K_LIFT * K_LIFT)

SLOTS = 6
HALO = (6, 6, 5, 4, 3, 2, 1)
HBASE = (0, 6, 12, 17, 21, 24, 26)
HTOTAL = 27


def lift_matrix(n):
    x = np.eye(n)
    s, e = x[0::2].copy(), x[1::2].copy()

    def up(v):
        return np.concatenate([v[1:], v[-1:]], 0)

    def down(v):
        return np.concatenate([v[:1], v[:-1]], 0)

    e = e + A_LIFT * (s + up(s))
    s = s + B_LIFT * (down(e) + e)
    e = e + C_LIFT * (s + up(s))
    s = s + D_LIFT * (down(e) + e)
    return np.concatenate([s / K_LIFT, e * K_LIFT], 0)


def split_const(m):
    hi = m.astype(ml_dtypes.bfloat16)
    lo = (m - hi.astype(np.float64)).astype(ml_dtypes.bfloat16)
    return hi, lo


def left_const(m):
    hi, lo = split_const(m)
    return np.concatenate([hi, lo, hi], 1)


def right_const(m):
    hi, lo = split_const(m)
    return np.concatenate([hi, lo, hi], 0)


def fine_right(n):
    t = lift_matrix(n)
    w = np.zeros((256, 256))
    for q in range(2):
        for par in range(2):
            r = 128 * q + 64 * par
            c = 128 * par + 64 * q
            w[r : r + n, c : c + n] = t.T * (K_LIFT if par else 1.0 / K_LIFT)
    return right_const(w)


def low_rows():
    return lift_matrix(32)[:16] @ lift_matrix(64)[:32]


def low_right():
    return right_const(np.kron(np.eye(4), low_rows().T) @ np.kron(np.ones((1, 2)), np.eye(64)))


def low_mid():
    return np.stack([m.astype(np.float32) for m in split_const(np.kron(low_rows().T, np.ones((1, 16))))])


def coarse_right():
    t = lift_matrix(32)
    w = np.zeros((256, 256))
    for j in range(8):
        for k2 in range(2):
            for kb in range(2):
                r = 128 * k2 + 16 * j
                c = 128 * (j % 2) + 64 * kb + 16 * (j // 2)
                scale = K_LIFT if j % 2 else 1.0 / K_LIFT
                w[r : r + 16, c : c + 16] = t[16 * kb : 16 * kb + 16, 16 * k2 : 16 * k2 + 16].T * scale
    return right_const(w)


def corner_left():
    t16, t8 = lift_matrix(16), lift_matrix(8)
    return left_const(np.concatenate([t16, t8 @ t16[:8]], 0))


def corner_right():
    t16, t8 = lift_matrix(16), lift_matrix(8)
    second = np.kron(t16, t16).T
    low = t8 @ t16[:8]
    both = np.zeros((256, 128))
    for j in range(8):
        for k in range(8):
            both[:, 16 * j + k] = np.kron(low[j], low[k])
    return right_const(np.concatenate([second, both], 1))


def split(x):
    hi = x.astype(BF16)
    lo = (x - hi.astype(F32)).astype(BF16)
    return hi, lo


def left_dot(t, x):
    hi, lo = split(x)
    return jnp.dot(t, jnp.concatenate([hi, hi, lo], 0), preferred_element_type=F32)


def right_dot(hi, lo, w):
    return jnp.dot(jnp.concatenate([hi, hi, lo], 1), w, preferred_element_type=F32)


def lift_lanes(s, e, mask, up, down):
    n = len(s)
    sp = up(s)
    e = [e[g] + A_SC * (s[g] + sp[g]) for g in range(n)]
    em = down(e)
    s = [s[g] + B_SC * (em[g] + e[g]) for g in range(n)]
    sp = up(s)
    e = [e[g] + C_SC * (s[g] + sp[g]) for g in range(n)]
    em = down(e)
    s = [s[g] + D_SC * (em[g] + e[g]) for g in range(n)]
    return s, e


def lift_halves(s, e, low):
    n = len(s)

    def up(v):
        r = [pltpu.roll(x, 64, 1) for x in v]
        return [jnp.where(low, r[g], r[g + 1] if g + 1 < n else v[g]) for g in range(n)]

    def down(v):
        r = [pltpu.roll(x, 64, 1) for x in v]
        return [jnp.where(low, r[g - 1] if g else v[g], r[g]) for g in range(n)]

    return lift_lanes(s, e, low, up, down)


def lift_quarters(s, e, last, first):
    n = len(s)

    def up(v):
        out = []
        for g in range(n):
            near = pltpu.roll(v[g], 112, 1)
            far = pltpu.roll(v[g + 1], 48, 1) if g + 1 < n else v[g]
            out.append(jnp.where(last, far, near))
        return out

    def down(v):
        out = []
        for g in range(n):
            near = pltpu.roll(v[g], 16, 1)
            far = pltpu.roll(v[g - 1], 80, 1) if g else v[g]
            out.append(jnp.where(first, far, near))
        return out

    return lift_lanes(s, e, last, up, down)


def lift_stream(load_s, load_e, n, emit):
    s0, e1, s1, e2 = load_s(0), None, None, None
    for i in range(n):
        s_next = load_s(i + 1) if i + 1 < n else s0
        e1_new = load_e(i) + A_SC * (s0 + s_next)
        s1_new = s0 + B_SC * ((e1 if i else e1_new) + e1_new)
        if i:
            e2_new = e1 + C_SC * (s1 + s1_new)
            emit(i - 1, s1 + D_SC * ((e2 if i > 1 else e2_new) + e2_new), e2_new)
            e2 = e2_new
        s0, e1, s1 = s_next, e1_new, s1_new
    e2_new = e1 + C_SC * (s1 + s1)
    emit(n - 1, s1 + D_SC * (e2 + e2_new), e2_new)


def fine_kernel(
    count_ref, x_ref, wc_ref, t1c_ref, t2c_ref, tlc_ref, wlc_ref, wmc_ref, o_ref, lpf_ref, fw_ref, bw_ref, tab_ref,
    lpb_ref, w_ref, t1_ref, t2_ref, tl_ref, wl_ref, wr_ref, wm_ref, xv_ref, ah_ref, al_ref, se_ref, zh_ref, zl_ref, cv_ref, a_ref, row_ref, b_ref,
    xsem, wsem, dsend, drecv, csend, crecv,
):
    node, dev = lax.axis_index("node"), lax.axis_index("dev")
    me = node * 16 + dev
    count = count_ref[0]
    lane = lax.broadcasted_iota(jnp.int32, (32, 128), 1)
    low = lane < 64
    corner = (lane[:16] & 63) < 32

    def load_x(s):
        return pltpu.make_async_copy(x_ref.at[s], xv_ref.at[s], xsem.at[s])

    constants = [(tlc_ref, tl_ref), (wlc_ref, wl_ref), (wmc_ref, wr_ref), (wc_ref, w_ref), (t1c_ref, t1_ref), (t2c_ref, t2_ref)]
    load_c = [pltpu.make_async_copy(a, b, wsem.at[i]) for i, (a, b) in enumerate(constants)]
    for c in load_c[:3]:
        c.start()
    load_x(0).start()
    load_x(1).start()

    barrier = pltpu.get_barrier_semaphore()

    def by_offset(step):
        t = lax.rem(me + step + 256, 256)
        return {"node": t // 16, "dev": lax.rem(t, 16)}

    def by_dev(k):
        return {"node": node, "dev": lax.rem(dev + k, 16)}

    def by_node(k):
        return {"node": lax.rem(node + k, 16), "dev": dev}

    partners = [by_offset(o) for o in range(1, 8)] + [by_offset(-o) for o in range(1, 8)]
    partners += [by_dev(k) for k in range(1, 16)] + [by_node(k) for k in range(1, 16)]
    for p in partners:
        pl.semaphore_signal(barrier, inc=1, device_id=p, device_id_type=MESH)
    cv_ref[...] = jnp.zeros_like(cv_ref) + count

    def remote(src, dst, send, recv, to):
        return pltpu.make_async_remote_copy(
            src_ref=src, dst_ref=dst, send_sem=send, recv_sem=recv, device_id=to, device_id_type=MESH
        )

    def stage(src, dst, i, to):
        for k in range(1, 16):
            remote(src, dst.at[k], csend.at[i], crecv.at[i], to(k)).start()

    def stage_wait(dst, i):
        c = remote(dst.at[pl.ds(1, 15)], dst.at[pl.ds(1, 15)], csend.at[i], crecv.at[i], by_dev(1))
        c.wait_send()
        c.wait_recv()

    def forward(o):
        n, b = HALO[o - 1], HBASE[o - 1]
        return remote(lpf_ref.at[pl.ds(0, n)], fw_ref.at[pl.ds(b, n)], dsend.at[0, o], drecv.at[0, o], by_offset(-o))

    def backward(o):
        n, b = HALO[o - 1], HBASE[o - 1]
        return remote(lpb_ref.at[pl.ds(SLOTS - n, n)], bw_ref.at[pl.ds(b, n)], dsend.at[1, o], drecv.at[1, o], by_offset(o))

    def low_pass(slot, carry):
        load_x(slot).wait()

        @pl.when(slot < SLOTS - 2)
        def _():
            load_x(slot + 2).start()

        @pl.when(slot == 0)
        def _():
            for c in load_c[:3]:
                c.wait()

        @pl.when(slot == 1)
        def _():
            wide = lax.broadcasted_iota(jnp.int32, (16, 256), 1) & 15
            same = wide == lax.broadcasted_iota(jnp.int32, (16, 256), 0)
            for part in range(2):
                for j in range(64):
                    row = jnp.broadcast_to(wr_ref[part, j : j + 1], (16, 256))
                    wm_ref[part, 16 * j : 16 * j + 16] = jnp.where(same, row, 0.0).astype(BF16)

        @pl.when(slot == SLOTS - 1)
        def _():
            for c in load_c[3:]:
                c.start()

        for g in range(16):
            y = left_dot(tl_ref[...], xv_ref[slot, :, 256 * g : 256 * g + 256])
            ah_ref[16 * g : 16 * g + 16], al_ref[16 * g : 16 * g + 16] = split(y)
        z = right_dot(ah_ref[:256], al_ref[:256], wl_ref[...])
        rows = pl.ds(slot * 16, 16)
        for g in range(8):
            pair = jnp.where(low[:16], z[32 * g : 32 * g + 16], z[32 * g + 16 : 32 * g + 32])
            cols = slice(128 * g, 128 * g + 128)
            zh_ref[rows, cols], zl_ref[rows, cols] = split(pair)

        @pl.when(slot == 3)
        def _():
            pl.semaphore_wait(barrier, len(partners))
            stage(cv_ref, a_ref, 0, by_dev)

        return carry

    lax.fori_loop(0, SLOTS, low_pass, 0)
    z = right_dot(zh_ref[...], zl_ref[...], jnp.concatenate([wm_ref[0], wm_ref[1], wm_ref[0]], 0))
    for s in range(SLOTS):
        for half in range(2):
            lpf_ref[s, 16 * half : 16 * half + 16] = z[16 * s : 16 * s + 16, 128 * half : 128 * half + 128]
    for s in range(SLOTS):
        lpb_ref[s] = lpf_ref[jnp.maximum(count - SLOTS + s, 0)]
    for o in (2, 1):
        forward(o).start()
        backward(o).start()

    def rows_dot(t, x, g):
        hi, lo = split(left_dot(t, x))
        parts = t.shape[0] // 32
        for nn in range(2):
            cols = slice(128 * nn, 128 * nn + 128)
            for p in range(parts):
                at = 16 * ((2 * g + nn) * parts + p)
                for q in range(2):
                    rows = slice(32 * p + 16 * q, 32 * p + 16 * q + 16)
                    ah_ref[at : at + 16, 128 * q : 128 * q + 128] = hi[rows, cols]
                    al_ref[at : at + 16, 128 * q : 128 * q + 128] = lo[rows, cols]

    def columns(n, parts, w, store):
        size = 16 * parts
        se_ref[: n * size] = right_dot(ah_ref[: n * size], al_ref[: n * size], w_ref[w])
        held = {}

        def emit(i, s, e):
            if i % 2 == 0:
                held[0] = (s, e)
                return
            for band, (x0, x1) in enumerate(zip(held[0], (s, e))):
                r0, r1 = pltpu.roll(x0, 64, 1), pltpu.roll(x1, 64, 1)
                for q, v in enumerate((jnp.where(low[:size], x0, r1), jnp.where(low[:size], r0, x1))):
                    for p in range(parts):
                        store(32 * p + 16 * q, band, i // 2, v[16 * p : 16 * p + 16])

        lift_stream(
            lambda i: se_ref[size * i : size * i + size, :128], lambda i: se_ref[size * i : size * i + size, 128:], n, emit
        )

    def full_pass(slot, carry):
        for g in range(16):
            rows_dot(t1_ref[...], xv_ref[slot, :, 256 * g : 256 * g + 256], g)

        def store1(row, band, u, v):
            o_ref[slot, row : row + 16, 2048 * band + 128 * u : 2048 * band + 128 * u + 128] = v

        columns(32, 2, 0, store1)
        for h in range(8):
            rows_dot(t2_ref[...], o_ref[slot, :32, 256 * h : 256 * h + 256], h)

        def store2(row, band, u, v):
            at = (slot, slice(row, row + 16), slice(1024 * band + 128 * u, 1024 * band + 128 * u + 128))
            o_ref[at] = jnp.where(corner, v, o_ref[at])

        columns(16, 1, 1, store2)

        @pl.when(slot == 0)
        def _():
            stage_wait(a_ref, 0)
            row = jnp.where(lane[:8] == dev, cv_ref[...], 0)
            for k in range(1, 16):
                row = jnp.where(lane[:8] == lax.rem(dev - k + 16, 16), a_ref[k], row)
            row_ref[...] = row
            stage(row_ref, b_ref, 1, by_node)
            for o in (6, 3, 5, 7, 4):
                forward(o).start()
                backward(o).start()

        return carry

    for c in load_c[3:]:
        c.wait()
    lax.fori_loop(0, SLOTS, full_pass, 0)
    stage_wait(b_ref, 1)
    tab_ref[0:1] = row_ref[0:1]
    for k in range(1, 16):
        tab_ref[k : k + 1] = b_ref[k][0:1]
    for o in range(1, 8):
        forward(o).wait()
        backward(o).wait()


def fine_call(density, counts):
    t1, t2 = left_const(lift_matrix(64)), left_const(lift_matrix(32))
    w = np.stack([fine_right(64), fine_right(32)])
    tl, wl, wm = left_const(low_rows()), low_right(), low_mid()
    vmem = pl.BlockSpec(memory_space=pltpu.VMEM)
    hbm = pl.BlockSpec(memory_space=pltpu.HBM)
    dma = pltpu.SemaphoreType.DMA
    return pl.pallas_call(
        fine_kernel,
        in_specs=[pl.BlockSpec(memory_space=pltpu.SMEM)] + [hbm] * 7,
        out_specs=[vmem] * 5,
        out_shape=[
            jax.ShapeDtypeStruct(density.shape, F32),
            jax.ShapeDtypeStruct((SLOTS, 32, 128), F32),
            jax.ShapeDtypeStruct((HTOTAL, 32, 128), F32),
            jax.ShapeDtypeStruct((HTOTAL, 32, 128), F32),
            jax.ShapeDtypeStruct((16, 128), jnp.int32),
        ],
        scratch_shapes=[
            pltpu.VMEM((SLOTS, 32, 128), F32),
            pltpu.VMEM(w.shape, BF16),
            pltpu.VMEM(t1.shape, BF16),
            pltpu.VMEM(t2.shape, BF16),
            pltpu.VMEM(tl.shape, BF16),
            pltpu.VMEM(wl.shape, BF16),
            pltpu.VMEM(wm.shape, F32),
            pltpu.VMEM((2, 1024, 256), BF16),
            pltpu.VMEM((SLOTS, 64, 4096), F32),
            pltpu.VMEM((1024, 256), BF16),
            pltpu.VMEM((1024, 256), BF16),
            pltpu.VMEM((1024, 256), F32),
            pltpu.VMEM((16 * SLOTS, 1024), BF16),
            pltpu.VMEM((16 * SLOTS, 1024), BF16),
            pltpu.VMEM((8, 128), jnp.int32),
            pltpu.VMEM((16, 8, 128), jnp.int32),
            pltpu.VMEM((8, 128), jnp.int32),
            pltpu.VMEM((16, 8, 128), jnp.int32),
            dma((SLOTS,)),
            dma((6,)),
            dma((2, 8)),
            dma((2, 8)),
            dma((2,)),
            dma((2,)),
        ],
        compiler_params=pltpu.CompilerParams(collective_id=0, has_side_effects=True, vmem_limit_bytes=30 << 20),
        name="fine",
    )(counts, *[pltpu.with_memory_space_constraint(jnp.asarray(a), pltpu.HBM) for a in (density, w, t1, t2, tl, wl, wm)])


def coarse_kernel(tabs_ref, lpf_ref, fw_ref, bw_ref, tab_ref, t1_ref, w1_ref, t2_ref, w2_ref, fine_ref, o_ref, h_ref, ctx_ref, res_ref, zero_ref, wsem):
    node, dev = lax.axis_index("node"), lax.axis_index("dev")
    me = node * 16 + dev
    count = tabs_ref[0, dev]

    def body(s):
        return pltpu.make_async_copy(fine_ref.at[s, pl.ds(16, 48)], o_ref.at[s, pl.ds(16, 48)], wsem.at[s, 0])

    def side(s):
        rows, cols = pl.ds(0, 16), pl.ds(1024, 3072)
        return pltpu.make_async_copy(fine_ref.at[s, rows, cols], o_ref.at[s, rows, cols], wsem.at[s, 1])

    def corner_out(s):
        return pltpu.make_async_copy(ctx_ref.at[s], o_ref.at[s, pl.ds(0, 16), pl.ds(0, 1024)], wsem.at[s, 2])

    def zeros(s):
        return pltpu.make_async_copy(zero_ref, o_ref.at[s], wsem.at[s, 0])

    for s in range(SLOTS):

        @pl.when(s < count)
        def _(s=s):
            body(s).start()
            side(s).start()

    krow = lax.broadcasted_iota(jnp.int32, (16, 128), 0)
    klane = lax.broadcasted_iota(jnp.int32, (16, 128), 1)
    owner = lax.rem(node - krow + 16, 16) * 16 + klane
    start = jnp.sum(jnp.where((klane < 16) & (owner < me), tab_ref[...], 0))
    first = start // 8

    def count_of(t):
        return tabs_ref[lax.rem(node - t // 16 + 16, 16), lax.rem(t, 16)]

    for s in range(SLOTS):
        h_ref[7 + s] = lpf_ref[s]
    after = 7 + count
    before = 7
    for o in range(1, 8):
        n, b = HALO[o - 1], HBASE[o - 1]
        for s in range(n):
            h_ref[jnp.minimum(after + s, 24)] = fw_ref[b + s]
        for s in range(n):
            p = before - n + s
            h_ref[jnp.where(p < 0, 25, p)] = bw_ref[b + s]
        after = after + count_of(lax.rem(me + o, 256))
        before = before - count_of(lax.rem(me - o + 256, 256))

    lane = lax.broadcasted_iota(jnp.int32, (8, 128), 1)
    base = 7 + first * 8 - start
    hs, ls = [], []
    for q in range(2):
        groups = []
        for c1 in range(2):
            for jh in range(2):
                for c2 in range(2):
                    c = 2 * c1 + 4 * c2
                    at = base + 8 * q + c
                    groups.append(jnp.concatenate([h_ref[at, 16 * jh : 16 * jh + 16], h_ref[at + 1, 16 * jh : 16 * jh + 16]], 0))
        y = left_dot(t1_ref[...], jnp.concatenate(groups, 1))
        hi, lo = split(y)
        for g in range(4):
            hs.append(hi[:, 256 * g : 256 * g + 256])
            ls.append(lo[:, 256 * g : 256 * g + 256])
    y = right_dot(jnp.concatenate(hs, 0), jnp.concatenate(ls, 0), w1_ref[...])
    last, firstm = (lane // 16) % 4 == 3, (lane // 16) % 4 == 0
    low = lane < 64
    corners = []
    for q in range(2):
        halves = []
        for r in range(4):
            at = [128 * q + 32 * g + 8 * r for g in range(4)]
            s = [y[a : a + 8, :128] for a in at]
            e = [y[a : a + 8, 128:] for a in at]
            s, e = lift_quarters(s, e, last, firstm)
            for g in range(4):
                res_ref[q, r // 2, 0, g, 8 * (r % 2) : 8 * (r % 2) + 8] = s[g]
                res_ref[q, r // 2, 1, g, 8 * (r % 2) : 8 * (r % 2) + 8] = e[g]
            if r < 2:
                halves.append(
                    jnp.concatenate([jnp.where(low, s[0], pltpu.roll(s[1], 64, 1)), jnp.where(low, s[2], pltpu.roll(s[3], 64, 1))], 1)
                )
        corners.append(jnp.concatenate(halves, 0))
    y = left_dot(t2_ref[...], jnp.concatenate(corners, 1))
    hi, lo = split(y)
    y = right_dot(
        jnp.concatenate([hi[:, :256], hi[:, 256:]], 0), jnp.concatenate([lo[:, :256], lo[:, 256:]], 0), w2_ref[...]
    )
    deep = (lane & 15) < 8
    for q in range(2):
        for r in range(2):
            a = 24 * q + 8 * r
            v0, v1 = y[a : a + 8, :128], y[a : a + 8, 128:256]
            if r == 0:
                v0 = jnp.where(deep, y[24 * q + 16 : 24 * q + 24, 256:], v0)
            rows = slice(8 * r, 8 * r + 8)
            for g, v in enumerate([v0, pltpu.roll(v0, 64, 1), v1, pltpu.roll(v1, 64, 1)]):
                res_ref[q, 0, 0, g, rows] = jnp.where(low, v, res_ref[q, 0, 0, g, rows])
    for s in range(SLOTS):

        @pl.when(s < count)
        def _(s=s):
            block = start + s
            q = block // 8 - first
            c0, c1, c2 = lax.rem(block, 2), lax.rem(block // 2, 2), lax.rem(block // 4, 2)
            for r in range(2):
                rows = slice(8 * r, 8 * r + 8)
                for g in range(4):
                    v = res_ref[q, c0, c1, g, rows]
                    v = jnp.where(c2 == 1, pltpu.roll(v, 64, 1), v)
                    for mh in range(2):
                        cols = slice(256 * g + 128 * mh, 256 * g + 128 * mh + 128)
                        left = pltpu.roll(v, 96, 1) if mh else v
                        right = pltpu.roll(v, 16 if mh else 48, 1)
                        old = fine_ref[s, rows, cols]
                        new = jnp.where(lane < 16, left, jnp.where((lane >= 64) & (lane < 80), right, old))
                        ctx_ref[s, rows, cols] = new
            corner_out(s).start()

    @pl.when(count < SLOTS)
    def _():
        zero_ref[...] = jnp.zeros_like(zero_ref)

    for s in range(1, SLOTS):

        @pl.when(s >= count)
        def _(s=s):
            zeros(s).start()

    for s in range(SLOTS):

        @pl.when(s < count)
        def _(s=s):
            body(s).wait()
            side(s).wait()
            corner_out(s).wait()

        @pl.when(s >= count)
        def _(s=s):
            zeros(s).wait()


def coarse_call(fine, lpf, fw, bw, tab):
    t1, w1, t2, w2 = left_const(lift_matrix(32)), coarse_right(), corner_left(), corner_right()
    vmem = pl.BlockSpec(memory_space=pltpu.VMEM)
    dma = pltpu.SemaphoreType.DMA
    return pl.pallas_call(
        coarse_kernel,
        in_specs=[pl.BlockSpec(memory_space=pltpu.SMEM)] + [vmem] * 9,
        out_specs=pl.BlockSpec(memory_space=pl.ANY),
        out_shape=jax.ShapeDtypeStruct(fine.shape, F32),
        scratch_shapes=[
            pltpu.VMEM((32, 32, 128), F32),
            pltpu.VMEM((SLOTS, 16, 1024), F32),
            pltpu.VMEM((2, 2, 2, 4, 16, 128), F32),
            pltpu.VMEM((64, 4096), F32),
            dma((SLOTS, 3)),
        ],
        compiler_params=pltpu.CompilerParams(vmem_limit_bytes=16 << 20),
        name="coarse",
    )(tab, lpf, fw, bw, tab, jnp.asarray(t1), jnp.asarray(w1), jnp.asarray(t2), jnp.asarray(w2), fine)


def per_device(density, counts):
    fine, lpf, fw, bw, tab = fine_call(density, counts)
    return coarse_call(fine, lpf, fw, bw, tab)


def solution(mesh):
    in_specs = (P(("node", "dev"), None, None), P(("node", "dev")))
    out_specs = P(("node", "dev"), None, None)
    return jax.shard_map(per_device, mesh=mesh, in_specs=in_specs, out_specs=out_specs, check_vma=False)
```

```python
import functools

import jax
import jax.numpy as jnp
import ml_dtypes
import numpy as np
from jax import lax
from jax.experimental import pallas as pl
from jax.experimental.pallas import tpu as pltpu
from jax.sharding import PartitionSpec as P

MESH = pl.DeviceIdType.MESH
F32 = jnp.float32
BF16 = jnp.bfloat16

A_LIFT = -1.586134342059924
B_LIFT = -0.052980118572961
C_LIFT = 0.882911075530934
D_LIFT = 0.443506852043971
K_LIFT = 1.230174104914001
A_SC = A_LIFT * K_LIFT * K_LIFT
B_SC = B_LIFT / (K_LIFT * K_LIFT)
C_SC = C_LIFT * K_LIFT * K_LIFT
D_SC = D_LIFT / (K_LIFT * K_LIFT)

SLOTS = 6
HALO = (6, 6, 5, 4, 3, 2, 1)
HBASE = (0, 6, 12, 17, 21, 24, 26)
HTOTAL = 27


def lift_matrix(n):
    x = np.eye(n)
    s, e = x[0::2].copy(), x[1::2].copy()

    def up(v):
        return np.concatenate([v[1:], v[-1:]], 0)

    def down(v):
        return np.concatenate([v[:1], v[:-1]], 0)

    e = e + A_LIFT * (s + up(s))
    s = s + B_LIFT * (down(e) + e)
    e = e + C_LIFT * (s + up(s))
    s = s + D_LIFT * (down(e) + e)
    return np.concatenate([s / K_LIFT, e * K_LIFT], 0)


def split_const(m):
    hi = m.astype(ml_dtypes.bfloat16)
    lo = (m - hi.astype(np.float64)).astype(ml_dtypes.bfloat16)
    return hi, lo


def left_const(m):
    hi, lo = split_const(m)
    return np.concatenate([hi, lo, hi], 1)


def right_const(m):
    hi, lo = split_const(m)
    return np.concatenate([hi, lo, hi], 0)


def fine_right(n):
    t = lift_matrix(n)
    w = np.zeros((256, 256))
    for q in range(2):
        for par in range(2):
            r = 128 * q + 64 * par
            c = 128 * par + 64 * q
            w[r : r + n, c : c + n] = t.T * (K_LIFT if par else 1.0 / K_LIFT)
    return right_const(w)


def low_rows():
    return lift_matrix(32)[:16] @ lift_matrix(64)[:32]


def low_right():
    return right_const(np.kron(np.eye(4), low_rows().T) @ np.kron(np.ones((1, 2)), np.eye(64)))


def low_mid():
    return np.stack([m.astype(np.float32) for m in split_const(np.kron(low_rows().T, np.ones((1, 16))))])


def coarse_right():
    t = lift_matrix(32)
    w = np.zeros((256, 256))
    for j in range(8):
        for k2 in range(2):
            for kb in range(2):
                r = 128 * k2 + 16 * j
                c = 128 * (j % 2) + 64 * kb + 16 * (j // 2)
                scale = K_LIFT if j % 2 else 1.0 / K_LIFT
                w[r : r + 16, c : c + 16] = t[16 * kb : 16 * kb + 16, 16 * k2 : 16 * k2 + 16].T * scale
    return right_const(w)


def corner_left():
    t16, t8 = lift_matrix(16), lift_matrix(8)
    return left_const(np.concatenate([t16, t8 @ t16[:8]], 0))


def corner_right():
    t16, t8 = lift_matrix(16), lift_matrix(8)
    second = np.kron(t16, t16).T
    low = t8 @ t16[:8]
    both = np.zeros((256, 128))
    for j in range(8):
        for k in range(8):
            both[:, 16 * j + k] = np.kron(low[j], low[k])
    return right_const(np.concatenate([second, both], 1))


def split(x):
    hi = x.astype(BF16)
    lo = (x - hi.astype(F32)).astype(BF16)
    return hi, lo


def left_dot(t, x):
    hi, lo = split(x)
    return jnp.dot(t, jnp.concatenate([hi, hi, lo], 0), preferred_element_type=F32)


def right_dot(hi, lo, w):
    return jnp.dot(jnp.concatenate([hi, hi, lo], 1), w, preferred_element_type=F32)


def lift_lanes(s, e, mask, up, down):
    n = len(s)
    sp = up(s)
    e = [e[g] + A_SC * (s[g] + sp[g]) for g in range(n)]
    em = down(e)
    s = [s[g] + B_SC * (em[g] + e[g]) for g in range(n)]
    sp = up(s)
    e = [e[g] + C_SC * (s[g] + sp[g]) for g in range(n)]
    em = down(e)
    s = [s[g] + D_SC * (em[g] + e[g]) for g in range(n)]
    return s, e


def lift_halves(s, e, low):
    n = len(s)

    def up(v):
        r = [pltpu.roll(x, 64, 1) for x in v]
        return [jnp.where(low, r[g], r[g + 1] if g + 1 < n else v[g]) for g in range(n)]

    def down(v):
        r = [pltpu.roll(x, 64, 1) for x in v]
        return [jnp.where(low, r[g - 1] if g else v[g], r[g]) for g in range(n)]

    return lift_lanes(s, e, low, up, down)


def lift_quarters(s, e, last, first):
    n = len(s)

    def up(v):
        out = []
        for g in range(n):
            near = pltpu.roll(v[g], 112, 1)
            far = pltpu.roll(v[g + 1], 48, 1) if g + 1 < n else v[g]
            out.append(jnp.where(last, far, near))
        return out

    def down(v):
        out = []
        for g in range(n):
            near = pltpu.roll(v[g], 16, 1)
            far = pltpu.roll(v[g - 1], 80, 1) if g else v[g]
            out.append(jnp.where(first, far, near))
        return out

    return lift_lanes(s, e, last, up, down)


def lift_stream(load_s, load_e, n, emit):
    s0, e1, s1, e2 = load_s(0), None, None, None
    for i in range(n):
        s_next = load_s(i + 1) if i + 1 < n else s0
        e1_new = load_e(i) + A_SC * (s0 + s_next)
        s1_new = s0 + B_SC * ((e1 if i else e1_new) + e1_new)
        if i:
            e2_new = e1 + C_SC * (s1 + s1_new)
            emit(i - 1, s1 + D_SC * ((e2 if i > 1 else e2_new) + e2_new), e2_new)
            e2 = e2_new
        s0, e1, s1 = s_next, e1_new, s1_new
    e2_new = e1 + C_SC * (s1 + s1)
    emit(n - 1, s1 + D_SC * (e2 + e2_new), e2_new)


def fine_kernel(
    count_ref, x_ref, wc_ref, t1c_ref, t2c_ref, tlc_ref, wlc_ref, wmc_ref, o_ref, lpf_ref, fw_ref, bw_ref, tab_ref,
    lpb_ref, w_ref, t1_ref, t2_ref, tl_ref, wl_ref, wr_ref, wm_ref, xv_ref, ah_ref, al_ref, se_ref, zh_ref, zl_ref, cv_ref, a_ref, row_ref, b_ref,
    xsem, wsem, dsend, drecv, csend, crecv,
):
    node, dev = lax.axis_index("node"), lax.axis_index("dev")
    me = node * 16 + dev
    count = count_ref[0]
    lane = lax.broadcasted_iota(jnp.int32, (32, 128), 1)
    low = lane < 64
    corner = (lane[:16] & 63) < 32

    def load_x(s):
        return pltpu.make_async_copy(x_ref.at[s], xv_ref.at[s], xsem.at[s])

    constants = [(tlc_ref, tl_ref), (wlc_ref, wl_ref), (wmc_ref, wr_ref), (wc_ref, w_ref), (t1c_ref, t1_ref), (t2c_ref, t2_ref)]
    load_c = [pltpu.make_async_copy(a, b, wsem.at[i]) for i, (a, b) in enumerate(constants)]
    for c in load_c[:3]:
        c.start()
    load_x(0).start()
    load_x(1).start()

    barrier = pltpu.get_barrier_semaphore()

    def by_offset(step):
        t = lax.rem(me + step + 256, 256)
        return {"node": t // 16, "dev": lax.rem(t, 16)}

    def by_dev(k):
        return {"node": node, "dev": lax.rem(dev + k, 16)}

    def by_node(k):
        return {"node": lax.rem(node + k, 16), "dev": dev}

    partners = [by_offset(o) for o in range(1, 8)] + [by_offset(-o) for o in range(1, 8)]
    partners += [by_dev(k) for k in range(1, 16)] + [by_node(k) for k in range(1, 16)]
    for p in partners:
        pl.semaphore_signal(barrier, inc=1, device_id=p, device_id_type=MESH)
    cv_ref[...] = jnp.zeros_like(cv_ref) + count

    def remote(src, dst, send, recv, to):
        return pltpu.make_async_remote_copy(
            src_ref=src, dst_ref=dst, send_sem=send, recv_sem=recv, device_id=to, device_id_type=MESH
        )

    def stage(src, dst, i, to):
        for k in range(1, 16):
            remote(src, dst.at[k], csend.at[i], crecv.at[i], to(k)).start()

    def stage_wait(dst, i):
        c = remote(dst.at[pl.ds(1, 15)], dst.at[pl.ds(1, 15)], csend.at[i], crecv.at[i], by_dev(1))
        c.wait_send()
        c.wait_recv()

    def forward(o):
        n, b = HALO[o - 1], HBASE[o - 1]
        return remote(lpf_ref.at[pl.ds(0, n)], fw_ref.at[pl.ds(b, n)], dsend.at[0, o], drecv.at[0, o], by_offset(-o))

    def backward(o):
        n, b = HALO[o - 1], HBASE[o - 1]
        return remote(lpb_ref.at[pl.ds(SLOTS - n, n)], bw_ref.at[pl.ds(b, n)], dsend.at[1, o], drecv.at[1, o], by_offset(o))

    def low_pass(slot, carry):
        load_x(slot).wait()

        @pl.when(slot < SLOTS - 2)
        def _():
            load_x(slot + 2).start()

        @pl.when(slot == 0)
        def _():
            for c in load_c[:3]:
                c.wait()

        @pl.when(slot == 1)
        def _():
            wide = lax.broadcasted_iota(jnp.int32, (16, 256), 1) & 15
            same = wide == lax.broadcasted_iota(jnp.int32, (16, 256), 0)
            for part in range(2):
                for j in range(64):
                    row = jnp.broadcast_to(wr_ref[part, j : j + 1], (16, 256))
                    wm_ref[part, 16 * j : 16 * j + 16] = jnp.where(same, row, 0.0).astype(BF16)

        @pl.when(slot == SLOTS - 1)
        def _():
            for c in load_c[3:]:
                c.start()

        for g in range(16):
            y = left_dot(tl_ref[...], xv_ref[slot, :, 256 * g : 256 * g + 256])
            ah_ref[16 * g : 16 * g + 16], al_ref[16 * g : 16 * g + 16] = split(y)
        z = right_dot(ah_ref[:256], al_ref[:256], wl_ref[...])
        rows = pl.ds(slot * 16, 16)
        for g in range(8):
            pair = jnp.where(low[:16], z[32 * g : 32 * g + 16], z[32 * g + 16 : 32 * g + 32])
            cols = slice(128 * g, 128 * g + 128)
            zh_ref[rows, cols], zl_ref[rows, cols] = split(pair)

        @pl.when(slot == 3)
        def _():
            pl.semaphore_wait(barrier, len(partners))
            stage(cv_ref, a_ref, 0, by_dev)

        return carry

    lax.fori_loop(0, SLOTS, low_pass, 0)
    z = right_dot(zh_ref[...], zl_ref[...], jnp.concatenate([wm_ref[0], wm_ref[1], wm_ref[0]], 0))
    for s in range(SLOTS):
        for half in range(2):
            lpf_ref[s, 16 * half : 16 * half + 16] = z[16 * s : 16 * s + 16, 128 * half : 128 * half + 128]
    for s in range(SLOTS):
        lpb_ref[s] = lpf_ref[jnp.maximum(count - SLOTS + s, 0)]
    for o in (2, 1, 6):
        forward(o).start()
        backward(o).start()

    def rows_dot(t, x, g):
        hi, lo = split(left_dot(t, x))
        parts = t.shape[0] // 32
        for nn in range(2):
            cols = slice(128 * nn, 128 * nn + 128)
            for p in range(parts):
                at = 16 * ((2 * g + nn) * parts + p)
                for q in range(2):
                    rows = slice(32 * p + 16 * q, 32 * p + 16 * q + 16)
                    ah_ref[at : at + 16, 128 * q : 128 * q + 128] = hi[rows, cols]
                    al_ref[at : at + 16, 128 * q : 128 * q + 128] = lo[rows, cols]

    def columns(n, parts, w, store):
        size = 16 * parts
        se_ref[: n * size] = right_dot(ah_ref[: n * size], al_ref[: n * size], w_ref[w])
        held = {}

        def emit(i, s, e):
            if i % 2 == 0:
                held[0] = (s, e)
                return
            for band, (x0, x1) in enumerate(zip(held[0], (s, e))):
                r0, r1 = pltpu.roll(x0, 64, 1), pltpu.roll(x1, 64, 1)
                for q, v in enumerate((jnp.where(low[:size], x0, r1), jnp.where(low[:size], r0, x1))):
                    for p in range(parts):
                        store(32 * p + 16 * q, band, i // 2, v[16 * p : 16 * p + 16])

        lift_stream(
            lambda i: se_ref[size * i : size * i + size, :128], lambda i: se_ref[size * i : size * i + size, 128:], n, emit
        )

    def full_pass(slot, carry):
        for g in range(16):
            rows_dot(t1_ref[...], xv_ref[slot, :, 256 * g : 256 * g + 256], g)

        def store1(row, band, u, v):
            o_ref[slot, row : row + 16, 2048 * band + 128 * u : 2048 * band + 128 * u + 128] = v

        columns(32, 2, 0, store1)
        for h in range(8):
            rows_dot(t2_ref[...], o_ref[slot, :32, 256 * h : 256 * h + 256], h)

        def store2(row, band, u, v):
            at = (slot, slice(row, row + 16), slice(1024 * band + 128 * u, 1024 * band + 128 * u + 128))
            o_ref[at] = jnp.where(corner, v, o_ref[at])

        columns(16, 1, 1, store2)

        @pl.when(slot == 0)
        def _():
            stage_wait(a_ref, 0)
            row = jnp.where(lane[:8] == dev, cv_ref[...], 0)
            for k in range(1, 16):
                row = jnp.where(lane[:8] == lax.rem(dev - k + 16, 16), a_ref[k], row)
            row_ref[...] = row
            stage(row_ref, b_ref, 1, by_node)
            for o in (3, 5, 7, 4):
                forward(o).start()
                backward(o).start()

        return carry

    for c in load_c[3:]:
        c.wait()
    lax.fori_loop(0, SLOTS, full_pass, 0)
    stage_wait(b_ref, 1)
    tab_ref[0:1] = row_ref[0:1]
    for k in range(1, 16):
        tab_ref[k : k + 1] = b_ref[k][0:1]
    for o in range(1, 8):
        forward(o).wait()
        backward(o).wait()


def fine_call(density, counts):
    t1, t2 = left_const(lift_matrix(64)), left_const(lift_matrix(32))
    w = np.stack([fine_right(64), fine_right(32)])
    tl, wl, wm = left_const(low_rows()), low_right(), low_mid()
    vmem = pl.BlockSpec(memory_space=pltpu.VMEM)
    hbm = pl.BlockSpec(memory_space=pltpu.HBM)
    dma = pltpu.SemaphoreType.DMA
    return pl.pallas_call(
        fine_kernel,
        in_specs=[pl.BlockSpec(memory_space=pltpu.SMEM)] + [hbm] * 7,
        out_specs=[vmem] * 5,
        out_shape=[
            jax.ShapeDtypeStruct(density.shape, F32),
            jax.ShapeDtypeStruct((SLOTS, 32, 128), F32),
            jax.ShapeDtypeStruct((HTOTAL, 32, 128), F32),
            jax.ShapeDtypeStruct((HTOTAL, 32, 128), F32),
            jax.ShapeDtypeStruct((16, 128), jnp.int32),
        ],
        scratch_shapes=[
            pltpu.VMEM((SLOTS, 32, 128), F32),
            pltpu.VMEM(w.shape, BF16),
            pltpu.VMEM(t1.shape, BF16),
            pltpu.VMEM(t2.shape, BF16),
            pltpu.VMEM(tl.shape, BF16),
            pltpu.VMEM(wl.shape, BF16),
            pltpu.VMEM(wm.shape, F32),
            pltpu.VMEM((2, 1024, 256), BF16),
            pltpu.VMEM((SLOTS, 64, 4096), F32),
            pltpu.VMEM((1024, 256), BF16),
            pltpu.VMEM((1024, 256), BF16),
            pltpu.VMEM((1024, 256), F32),
            pltpu.VMEM((16 * SLOTS, 1024), BF16),
            pltpu.VMEM((16 * SLOTS, 1024), BF16),
            pltpu.VMEM((8, 128), jnp.int32),
            pltpu.VMEM((16, 8, 128), jnp.int32),
            pltpu.VMEM((8, 128), jnp.int32),
            pltpu.VMEM((16, 8, 128), jnp.int32),
            dma((SLOTS,)),
            dma((6,)),
            dma((2, 8)),
            dma((2, 8)),
            dma((2,)),
            dma((2,)),
        ],
        compiler_params=pltpu.CompilerParams(collective_id=0, has_side_effects=True, vmem_limit_bytes=30 << 20),
        name="fine",
    )(counts, *[pltpu.with_memory_space_constraint(jnp.asarray(a), pltpu.HBM) for a in (density, w, t1, t2, tl, wl, wm)])


def coarse_kernel(tabs_ref, lpf_ref, fw_ref, bw_ref, tab_ref, t1_ref, w1_ref, t2_ref, w2_ref, fine_ref, o_ref, h_ref, ctx_ref, res_ref, zero_ref, wsem):
    node, dev = lax.axis_index("node"), lax.axis_index("dev")
    me = node * 16 + dev
    count = tabs_ref[0, dev]

    def body(s):
        return pltpu.make_async_copy(fine_ref.at[s, pl.ds(16, 48)], o_ref.at[s, pl.ds(16, 48)], wsem.at[s, 0])

    def side(s):
        rows, cols = pl.ds(0, 16), pl.ds(1024, 3072)
        return pltpu.make_async_copy(fine_ref.at[s, rows, cols], o_ref.at[s, rows, cols], wsem.at[s, 1])

    def corner_out(s):
        return pltpu.make_async_copy(ctx_ref.at[s], o_ref.at[s, pl.ds(0, 16), pl.ds(0, 1024)], wsem.at[s, 2])

    def zeros(s):
        return pltpu.make_async_copy(zero_ref, o_ref.at[s], wsem.at[s, 0])

    for s in range(SLOTS):

        @pl.when(s < count)
        def _(s=s):
            body(s).start()
            side(s).start()

    krow = lax.broadcasted_iota(jnp.int32, (16, 128), 0)
    klane = lax.broadcasted_iota(jnp.int32, (16, 128), 1)
    owner = lax.rem(node - krow + 16, 16) * 16 + klane
    start = jnp.sum(jnp.where((klane < 16) & (owner < me), tab_ref[...], 0))
    first = start // 8

    def count_of(t):
        return tabs_ref[lax.rem(node - t // 16 + 16, 16), lax.rem(t, 16)]

    for s in range(SLOTS):
        h_ref[7 + s] = lpf_ref[s]
    after = 7 + count
    before = 7
    for o in range(1, 8):
        n, b = HALO[o - 1], HBASE[o - 1]
        for s in range(n):
            h_ref[jnp.minimum(after + s, 24)] = fw_ref[b + s]
        for s in range(n):
            p = before - n + s
            h_ref[jnp.where(p < 0, 25, p)] = bw_ref[b + s]
        after = after + count_of(lax.rem(me + o, 256))
        before = before - count_of(lax.rem(me - o + 256, 256))

    lane = lax.broadcasted_iota(jnp.int32, (8, 128), 1)
    base = 7 + first * 8 - start
    hs, ls = [], []
    for q in range(2):
        groups = []
        for c1 in range(2):
            for jh in range(2):
                for c2 in range(2):
                    c = 2 * c1 + 4 * c2
                    at = base + 8 * q + c
                    groups.append(jnp.concatenate([h_ref[at, 16 * jh : 16 * jh + 16], h_ref[at + 1, 16 * jh : 16 * jh + 16]], 0))
        y = left_dot(t1_ref[...], jnp.concatenate(groups, 1))
        hi, lo = split(y)
        for g in range(4):
            hs.append(hi[:, 256 * g : 256 * g + 256])
            ls.append(lo[:, 256 * g : 256 * g + 256])
    y = right_dot(jnp.concatenate(hs, 0), jnp.concatenate(ls, 0), w1_ref[...])
    last, firstm = (lane // 16) % 4 == 3, (lane // 16) % 4 == 0
    low = lane < 64
    corners = []
    for q in range(2):
        halves = []
        for r in range(4):
            at = [128 * q + 32 * g + 8 * r for g in range(4)]
            s = [y[a : a + 8, :128] for a in at]
            e = [y[a : a + 8, 128:] for a in at]
            s, e = lift_quarters(s, e, last, firstm)
            for g in range(4):
                res_ref[q, r // 2, 0, g, 8 * (r % 2) : 8 * (r % 2) + 8] = s[g]
                res_ref[q, r // 2, 1, g, 8 * (r % 2) : 8 * (r % 2) + 8] = e[g]
            if r < 2:
                halves.append(
                    jnp.concatenate([jnp.where(low, s[0], pltpu.roll(s[1], 64, 1)), jnp.where(low, s[2], pltpu.roll(s[3], 64, 1))], 1)
                )
        corners.append(jnp.concatenate(halves, 0))
    y = left_dot(t2_ref[...], jnp.concatenate(corners, 1))
    hi, lo = split(y)
    y = right_dot(
        jnp.concatenate([hi[:, :256], hi[:, 256:]], 0), jnp.concatenate([lo[:, :256], lo[:, 256:]], 0), w2_ref[...]
    )
    deep = (lane & 15) < 8
    for q in range(2):
        for r in range(2):
            a = 24 * q + 8 * r
            v0, v1 = y[a : a + 8, :128], y[a : a + 8, 128:256]
            if r == 0:
                v0 = jnp.where(deep, y[24 * q + 16 : 24 * q + 24, 256:], v0)
            rows = slice(8 * r, 8 * r + 8)
            for g, v in enumerate([v0, pltpu.roll(v0, 64, 1), v1, pltpu.roll(v1, 64, 1)]):
                res_ref[q, 0, 0, g, rows] = jnp.where(low, v, res_ref[q, 0, 0, g, rows])
    def place(s):
        block = start + s
        q = block // 8 - first
        c0, c1, c2 = lax.rem(block, 2), lax.rem(block // 2, 2), lax.rem(block // 4, 2)
        for r in range(2):
            rows = slice(8 * r, 8 * r + 8)
            for g in range(4):
                v = res_ref[q, c0, c1, g, rows]
                v = jnp.where(c2 == 1, pltpu.roll(v, 64, 1), v)
                for mh in range(2):
                    cols = slice(256 * g + 128 * mh, 256 * g + 128 * mh + 128)
                    left = pltpu.roll(v, 96, 1) if mh else v
                    right = pltpu.roll(v, 16 if mh else 48, 1)
                    old = fine_ref[s, rows, cols]
                    new = jnp.where(lane < 16, left, jnp.where((lane >= 64) & (lane < 80), right, old))
                    ctx_ref[s, rows, cols] = new

    for s0 in range(0, SLOTS, 3):

        @pl.when(s0 < count)
        def _(s0=s0):
            for s in range(s0, s0 + 3):
                place(s)
            corner_out(s0).start()

        for s in range(s0 + 1, s0 + 3):

            @pl.when(s < count)
            def _(s=s):
                corner_out(s).start()

    @pl.when(count < SLOTS)
    def _():
        zero_ref[...] = jnp.zeros_like(zero_ref)

    for s in range(1, SLOTS):

        @pl.when(s >= count)
        def _(s=s):
            zeros(s).start()

    for s in range(SLOTS):

        @pl.when(s < count)
        def _(s=s):
            body(s).wait()
            side(s).wait()
            corner_out(s).wait()

        @pl.when(s >= count)
        def _(s=s):
            zeros(s).wait()


def coarse_call(fine, lpf, fw, bw, tab):
    t1, w1, t2, w2 = left_const(lift_matrix(32)), coarse_right(), corner_left(), corner_right()
    vmem = pl.BlockSpec(memory_space=pltpu.VMEM)
    dma = pltpu.SemaphoreType.DMA
    return pl.pallas_call(
        coarse_kernel,
        in_specs=[pl.BlockSpec(memory_space=pltpu.SMEM)] + [vmem] * 9,
        out_specs=pl.BlockSpec(memory_space=pl.ANY),
        out_shape=jax.ShapeDtypeStruct(fine.shape, F32),
        scratch_shapes=[
            pltpu.VMEM((32, 32, 128), F32),
            pltpu.VMEM((SLOTS, 16, 1024), F32),
            pltpu.VMEM((2, 2, 2, 4, 16, 128), F32),
            pltpu.VMEM((64, 4096), F32),
            dma((SLOTS, 3)),
        ],
        compiler_params=pltpu.CompilerParams(vmem_limit_bytes=16 << 20),
        name="coarse",
    )(tab, lpf, fw, bw, tab, jnp.asarray(t1), jnp.asarray(w1), jnp.asarray(t2), jnp.asarray(w2), fine)


def per_device(density, counts):
    fine, lpf, fw, bw, tab = fine_call(density, counts)
    return coarse_call(fine, lpf, fw, bw, tab)


def solution(mesh):
    in_specs = (P(("node", "dev"), None, None), P(("node", "dev")))
    out_specs = P(("node", "dev"), None, None)
    return jax.shard_map(per_device, mesh=mesh, in_specs=in_specs, out_specs=out_specs, check_vma=False)
```
